32 devices in a mesh: ctx: 16 (over z, y, core), wt: 2 (over x).
Axes of the slice: x: 2, y: 2, z: 4, core: 2. Of those that a mesh axis runs over, the one named last changes fastest.
Arguments:
- tokens: bfloat16 [16384, 512], P('ctx'), may hold values from -6 to 6
- memory: bfloat16 [20, 512], replicated, may hold values from -3 to 3
- doc_starts: int32 [8], replicated, may hold values from 0 to 16383, as said below
- w_query: bfloat16 [512, 512], P(None, 'wt'), may hold values from -0.25 to 0.25
- b_query: bfloat16 [512], P('wt'), may hold values from -3 to 3
- w_key: bfloat16 [512, 512], P(None, 'wt'), may hold values from -0.25 to 0.25
- w_value: bfloat16 [512, 512], P(None, 'wt'), may hold values from -0.25 to 0.25
- b_value: bfloat16 [512], P('wt'), may hold values from -3 to 3
- w_output: bfloat16 [512, 512], P('wt'), may hold values from -6 to 6
- b_output: bfloat16 [512], replicated, may hold values from -3 to 3
- first_gain: bfloat16 [512], replicated, may hold values from 0.099609375 to 1.8984375
- first_bias: bfloat16 [512], replicated, may hold values from -3 to 3
- w_up: bfloat16 [512, 2048], P(None, 'wt'), may hold values from -0.25 to 0.25
- b_up: bfloat16 [2048], P('wt'), may hold values from -3 to 3
- w_down: bfloat16 [2048, 512], P('wt'), may hold values from -0.125 to 0.125
- b_down: bfloat16 [512], replicated, may hold values from -3 to 3
- second_gain: bfloat16 [512], replicated, may hold values from 0.099609375 to 1.8984375
- second_bias: bfloat16 [512], replicated, may hold values from -3 to 3
- cotangent: bfloat16 [16384, 512], P('ctx'), may hold values from -6 to 6
- mem_cotangent: bfloat16 [20, 512], replicated, may hold values from -6 to 6
Outputs:
- token_out: bfloat16 [16384, 512], P('ctx')
- memory_out: bfloat16 [20, 512], replicated
- token_grad: float32 [16384, 512], P('ctx')
- memory_grad: float32 [20, 512], replicated
- query_grad: float32 [512, 512], P(None, 'wt')
- query_bias_grad: float32 [512], P('wt')
- key_grad: float32 [512, 512], P(None, 'wt')
- value_grad: float32 [512, 512], P(None, 'wt')
- value_bias_grad: float32 [512], P('wt')
- output_grad: float32 [512, 512], P('wt')
- output_bias_grad: float32 [512], replicated
- first_gain_grad: float32 [512], replicated
- first_bias_grad: float32 [512], replicated
- up_grad: float32 [512, 2048], P(None, 'wt')
- up_bias_grad: float32 [2048], P('wt')
- down_grad: float32 [2048, 512], P('wt')
- down_bias_grad: float32 [512], replicated
- second_gain_grad: float32 [512], replicated
- second_bias_grad: float32 [512], replicated
The draws below stay inside these ranges and needn't reach their ends.
Inputs may be any that keep to these rules, and one draw needn't show every extreme that they name: doc_starts[0] is 0 and the entries rise strictly; each document, from its start to the next start (the last one to 16384), holds 1 to 4096 tokens, and one holds exactly 4096.
All inputs are finite; a program needn't handle non-finite values.
Results may differ from the reference program's by a relative error of at most 0.015.
Values may be sent and summed in bfloat16 or wider, within the bound.
A program may use at most 128 MiB of HBM per device.

```python
import jax
import jax.numpy as jnp
from jax import lax

D = 512
HEADS = 8
HEAD = 64
FF = 2048
MEM = 20
TOK_DEV = 1024
LONGEST = 4096
TOKENS = 16384
DOCS = 8


def draw_doc_starts(key, part):
    count = DOCS
    others = count - 1
    weights = jax.random.randint(jax.random.fold_in(key, 11), (others,), 64, 128, dtype=jnp.int32)
    remaining = TOKENS - LONGEST
    lengths = weights * remaining // jnp.sum(weights)
    spare = remaining - jnp.sum(lengths)
    lengths = lengths + (jnp.arange(others, dtype=jnp.int32) < spare).astype(jnp.int32)
    place = jax.random.randint(jax.random.fold_in(key, 12), (), 0, count, dtype=jnp.int32)
    position = jnp.arange(count, dtype=jnp.int32)
    source = jnp.clip(jnp.where(position > place, position - 1, position), 0, others - 1)
    every = jnp.where(position == place, LONGEST, lengths[source])
    return (jnp.cumsum(every) - every).astype(jnp.int32)


def levels(rng, shape, split, smallest, high):
    level, own = 1.0, jax.random.fold_in(rng, 6)
    for axis_at, parts in split:
        steps = jnp.exp(jax.random.uniform(jax.random.fold_in(own, axis_at), (parts,), jnp.float32, smallest / len(split), high / len(split)))
        level = level * jnp.repeat(steps, shape[axis_at] // parts).reshape([-1 if axis == axis_at else 1 for axis in range(len(shape))])
    return level


def bell_draw(rng, dims, width, most, shards=(), held_as=jnp.bfloat16):
    values = jax.random.normal(rng, dims, jnp.float32) * width
    if len(shards) > 0:
        values = levels(rng, dims, shards, -0.22, 0.18) * values
    return jnp.clip(values, min=-most, max=most).astype(held_as)


def setup_inputs(seed: int = 0) -> dict:
    key_of = jax.random.split(jax.random.key(seed), 21)
    return {
        "tokens": bell_draw(key_of[0], (TOKENS, D), 1.0, 6.0, ((0, 16),)),
        "memory": bell_draw(key_of[1], (MEM, D), 0.5, 3.0),
        "doc_starts": draw_doc_starts(jax.random.fold_in(key_of[20], 71), 0),
        "w_query": bell_draw(key_of[3], (D, D), D ** -0.5, 0.25, ((1, 2),)),
        "b_query": bell_draw(key_of[4], (D,), 0.5, 3.0, ((0, 2),)),
        "w_key": bell_draw(key_of[5], (D, D), D ** -0.5, 0.25, ((1, 2),)),
        "w_value": bell_draw(key_of[6], (D, D), D ** -0.5, 0.25, ((1, 2),)),
        "b_value": bell_draw(key_of[7], (D,), 0.5, 3.0, ((0, 2),)),
        "w_output": bell_draw(key_of[8], (D, D), (max(1, D // TOK_DEV)) ** -0.5, 6.0, ((0, 2),)),
        "b_output": bell_draw(key_of[9], (D,), 0.5, 3.0),
        "first_gain": jnp.clip(1.0 + 0.18 * jax.random.normal(key_of[10], (D,), jnp.float32), 0.099609375, 1.8984375).astype(jnp.bfloat16),
        "first_bias": bell_draw(key_of[11], (D,), 0.5, 3.0),
        "w_up": bell_draw(key_of[12], (D, FF), D ** -0.5, 0.25, ((1, 2),)),
        "b_up": bell_draw(key_of[13], (FF,), 0.5, 3.0, ((0, 2),)),
        "w_down": bell_draw(key_of[14], (FF, D), FF ** -0.5, 0.125, ((0, 2),)),
        "b_down": bell_draw(key_of[15], (D,), 0.5, 3.0),
        "second_gain": jnp.clip(1.0 + 0.18 * jax.random.normal(key_of[16], (D,), jnp.float32), 0.099609375, 1.8984375).astype(jnp.bfloat16),
        "second_bias": bell_draw(key_of[17], (D,), 0.5, 3.0),
        "cotangent": bell_draw(key_of[18], (TOKENS, D), 1.0, 6.0, ((0, 16),)),
        "mem_cotangent": bell_draw(key_of[19], (MEM, D), 1.0, 6.0),
    }


@jax.custom_vjp
def low(v):
    return lax.optimization_barrier(v.astype(jnp.bfloat16)).astype(jnp.float32)

@jax.custom_vjp
def low_back(v):
    return v

def low_keep(v):
    return (low(v), None)

def low_pass(kept, grad):
    return (grad,)

def back_keep(v):
    return (v, None)

def back_low(kept, grad):
    return (low(grad),)
low.defvjp(low_keep, low_pass)
low_back.defvjp(back_keep, back_low)
EPSILON = 1e-05
MASKED = -1e+30

def product(left, right):
    return jnp.dot(left, right, precision=lax.Precision.HIGHEST)

def activate(value):
    return jax.nn.gelu(value, approximate=True)

def layer_norm(value, gain, shift):
    centered = value - lax.optimization_barrier(jnp.mean(value, axis=-1, keepdims=True))
    variance = lax.optimization_barrier(jnp.mean(centered * centered, axis=-1, keepdims=True))
    return centered * lax.rsqrt(variance + EPSILON) * gain + shift

def attend(queries, keys, values, allowed):
    scores = jnp.einsum('qhd,khd->hqk', queries, keys, precision=lax.Precision.HIGHEST) * HEAD ** (-0.5)
    scores = low_back(scores)
    scores = jnp.where(allowed[None], scores, MASKED)
    top = lax.optimization_barrier(jnp.max(scores, axis=-1, keepdims=True))
    total = lax.optimization_barrier(jnp.sum(jnp.exp(scores - top), axis=-1, keepdims=True))
    shares = low(jnp.exp(scores - (top + jnp.log(total))))
    return jnp.einsum('hqk,khd->qhd', shares, values, precision=lax.Precision.HIGHEST)

def forward(labels, tokens, memory, w_query, b_query, w_key, w_value, b_value, w_output, b_output, first_gain, first_bias, w_up, b_up, w_down, b_down, second_gain, second_bias):
    rows = jnp.concatenate([tokens, memory], axis=0)
    count = rows.shape[0]
    queries = low(low_back(product(rows, w_query) + b_query)).reshape(count, HEADS, HEAD)
    keys = low(low_back(product(rows, w_key))).reshape(count, HEADS, HEAD)
    values = low(low_back(product(rows, w_value) + b_value)).reshape(count, HEADS, HEAD)
    query_rows = 512 if TOKENS % 512 == 0 else TOKENS
    blocks = TOKENS // query_rows
    memory_allowed = jnp.ones((query_rows, MEM), dtype=bool)

    def token_block(number):
        start = number * query_rows
        query_block = lax.dynamic_slice_in_dim(queries, start, query_rows, 0)
        label_block = lax.dynamic_slice_in_dim(labels, start, query_rows, 0)
        allowed = jnp.concatenate([label_block[:, None] == labels[None, :], memory_allowed], axis=1)
        return attend(query_block, keys, values, allowed)
    token_mixed = lax.map(jax.checkpoint(token_block), jnp.arange(blocks, dtype=jnp.int32))
    token_mixed = token_mixed.reshape(TOKENS, D)
    memory_mixed = attend(queries[TOKENS:], keys[:TOKENS], values[:TOKENS], jnp.ones((MEM, TOKENS), dtype=bool)).reshape(MEM, D)
    mixed = low(low_back(jnp.concatenate([token_mixed, memory_mixed], axis=0)))
    attended = low_back(product(mixed, w_output) + b_output)
    normed = layer_norm(rows + attended, first_gain, first_bias)
    inner = low_back(product(low(normed), w_up) + b_up)
    acted = low(activate(inner))
    fed = low_back(product(acted, w_down) + b_down)
    return layer_norm(normed + fed, second_gain, second_bias)

def reference(tokens, memory, doc_starts, w_query, b_query, w_key, w_value, b_value, w_output, b_output, first_gain, first_bias, w_up, b_up, w_down, b_down, second_gain, second_bias, cotangent, mem_cotangent):
    positions = jnp.arange(TOKENS, dtype=jnp.int32)
    labels = lax.optimization_barrier(jnp.sum((doc_starts[None, :] <= positions[:, None]).astype(jnp.int32), axis=1)) - 1
    floats = [array.astype(jnp.float32) for array in (tokens, memory, w_query, b_query, w_key, w_value, b_value, w_output, b_output, first_gain, first_bias, w_up, b_up, w_down, b_down, second_gain, second_bias)]

    def wrapped(*values):
        return forward(labels, *values)
    final, pullback = jax.vjp(wrapped, *floats)
    upstream = jnp.concatenate([cotangent, mem_cotangent], axis=0).astype(jnp.float32)
    grads = pullback(upstream)
    return (final[:TOKENS].astype(jnp.bfloat16), final[TOKENS:].astype(jnp.bfloat16), grads[0], grads[1], grads[2], grads[3], grads[4], grads[5], grads[6], grads[7], grads[8], grads[9], grads[10], grads[11], grads[12], grads[13], grads[14], grads[15], grads[16])
```

```python
import functools

import jax
import jax.numpy as jnp
from jax import lax
from jax.experimental import pallas as pl
from jax.experimental.pallas import tpu as pltpu
from jax.sharding import PartitionSpec as P

HEAD = 64
EPSILON = 1e-05
MASKED = -1e30
MESH = pl.DeviceIdType.MESH
TQ = 512
TK = 512
MEMK = 32
MEMQ = 128
ONES = 16
VROWS = HEAD + ONES
SROWS = VROWS + 8
F32 = jnp.float32
BF16 = jnp.bfloat16
VMEM_LIMIT = 56 * 1024 * 1024


def vmem():
    return pl.BlockSpec(memory_space=pltpu.VMEM)


def smem():
    return pl.BlockSpec(memory_space=pltpu.SMEM)


def anyspace():
    return pl.BlockSpec(memory_space=pl.ANY)


def dot(a, b):
    return jnp.dot(a, b, preferred_element_type=F32)


def greet(partners):
    barrier = pltpu.get_barrier_semaphore()
    for partner in partners:
        pl.semaphore_signal(barrier, inc=1, device_id=partner, device_id_type=MESH)
    pl.semaphore_wait(barrier, len(partners))


def remote(src, dst, send, recv, device):
    return pltpu.make_async_remote_copy(
        src_ref=src, dst_ref=dst, send_sem=send, recv_sem=recv, device_id=device, device_id_type=MESH
    )


def group_place(group):
    here = lax.axis_index("ctx")
    return here // group * group, lax.rem(here, group), lax.axis_index("wt")


def scatter_heads_kernel(group, block, q_ref, kv_ref, qo_ref, kvo_ref, own, send, recv):
    base, me, side = group_place(group)
    width = 2 * HEAD
    partners = [(base + lax.rem(me + t, group), side) for t in range(1, group)]
    greet(partners)
    copies = []
    for t in range(1, group):
        peer = lax.rem(me + t, group)
        copies.append(
            remote(
                kv_ref.at[pl.ds(0, block), pl.ds(pl.multiple_of(peer * width, width), width)],
                kvo_ref.at[pl.ds(pl.multiple_of(me * block, block), block), :],
                send.at[2 * t - 2],
                recv.at[2 * t - 2],
                partners[t - 1],
            )
        )
        copies.append(
            remote(
                q_ref.at[pl.ds(pl.multiple_of(peer * HEAD, HEAD), HEAD), :],
                qo_ref.at[:, pl.ds(pl.multiple_of(me * block, block), block)],
                send.at[2 * t - 1],
                recv.at[2 * t - 1],
                partners[t - 1],
            )
        )
    for copy in copies:
        copy.start()
    mine = [
        pltpu.make_async_copy(
            kv_ref.at[pl.ds(0, block), pl.ds(pl.multiple_of(me * width, width), width)],
            kvo_ref.at[pl.ds(pl.multiple_of(me * block, block), block), :],
            own.at[0],
        ),
        pltpu.make_async_copy(
            q_ref.at[pl.ds(pl.multiple_of(me * HEAD, HEAD), HEAD), :],
            qo_ref.at[:, pl.ds(pl.multiple_of(me * block, block), block)],
            own.at[1],
        ),
    ]
    for copy in mine:
        copy.start()
    for copy in mine + copies:
        copy.wait()


def scatter_heads(q, kv, group, block):
    return pl.pallas_call(
        functools.partial(scatter_heads_kernel, group, block),
        out_shape=(
            jax.ShapeDtypeStruct((HEAD, group * block), BF16),
            jax.ShapeDtypeStruct((group * block, 2 * HEAD), BF16),
        ),
        in_specs=[anyspace()] * 2,
        out_specs=(anyspace(), anyspace()),
        scratch_shapes=[
            pltpu.SemaphoreType.DMA((2,)),
            pltpu.SemaphoreType.DMA((2 * group - 2,)),
            pltpu.SemaphoreType.DMA((2 * group - 2,)),
        ],
        compiler_params=pltpu.CompilerParams(collective_id=0, has_side_effects=True),
        name="scatter_heads",
    )(q, kv)


def gather_heads_kernel(group, block, q_ref, kv_ref, qo_ref, kvo_ref, own, send, recv):
    base, me, side = group_place(group)
    width = 2 * HEAD
    partners = [(base + lax.rem(me + t, group), side) for t in range(1, group)]
    greet(partners)
    copies = []
    for t in range(1, group):
        peer = lax.rem(me + t, group)
        copies.append(
            remote(
                kv_ref.at[pl.ds(pl.multiple_of(peer * block, block), block), :],
                kvo_ref.at[:, pl.ds(pl.multiple_of(me * width, width), width)],
                send.at[2 * t - 2],
                recv.at[2 * t - 2],
                partners[t - 1],
            )
        )
        copies.append(
            remote(
                q_ref.at[:, pl.ds(pl.multiple_of(peer * block, block), block)],
                qo_ref.at[pl.ds(pl.multiple_of(me * HEAD, HEAD), HEAD), :],
                send.at[2 * t - 1],
                recv.at[2 * t - 1],
                partners[t - 1],
            )
        )
    for copy in copies:
        copy.start()
    mine = [
        pltpu.make_async_copy(
            kv_ref.at[pl.ds(pl.multiple_of(me * block, block), block), :],
            kvo_ref.at[:, pl.ds(pl.multiple_of(me * width, width), width)],
            own.at[0],
        ),
        pltpu.make_async_copy(
            q_ref.at[:, pl.ds(pl.multiple_of(me * block, block), block)],
            qo_ref.at[pl.ds(pl.multiple_of(me * HEAD, HEAD), HEAD), :],
            own.at[1],
        ),
    ]
    for copy in mine:
        copy.start()
    for copy in mine + copies:
        copy.wait()


def gather_heads(q, kv, group, block):
    return pl.pallas_call(
        functools.partial(gather_heads_kernel, group, block),
        out_shape=(
            jax.ShapeDtypeStruct((group * HEAD, block), BF16),
            jax.ShapeDtypeStruct((block, group * 2 * HEAD), BF16),
        ),
        in_specs=[anyspace()] * 2,
        out_specs=(anyspace(), anyspace()),
        scratch_shapes=[
            pltpu.SemaphoreType.DMA((2,)),
            pltpu.SemaphoreType.DMA((2 * group - 2,)),
            pltpu.SemaphoreType.DMA((2 * group - 2,)),
        ],
        compiler_params=pltpu.CompilerParams(collective_id=1, has_side_effects=True),
        name="gather_heads",
    )(q, kv)


def near_partners(group, sides):
    base, me, side = group_place(group)
    found = []
    for u in range(sides):
        for t in range(group):
            if t or u:
                found.append((lax.rem(me + t, group), lax.rem(side + u, sides)))
    return base, me, side, found


def mix_kernel(
    group, sides, groups, half,
    o_ref, mine_ref, mixed_ref, mem_ref, sum_ref,
    parts, memt, own, psend, precv, send, recv, msend, mrecv,
):
    base, me, side, found = near_partners(group, sides)
    number = base // group
    far = [
        (lax.rem(number + t, groups) * group + me, side) for t in range(1, groups)
    ]
    greet([(base + l, u) for l, u in found] + far)
    for t in range(1, groups):
        remote(
            mine_ref, parts.at[t], psend.at[t - 1], precv.at[t - 1], far[t - 1]
        ).start()
    head = side * group + me
    rows = pl.ds(pl.multiple_of(head * HEAD, HEAD), HEAD)
    copies = []
    for k, (l, u) in enumerate(found):
        start = pl.multiple_of((l * sides + u) * half, half)
        copies.append(
            remote(
                o_ref.at[:, pl.ds(start, half)],
                mixed_ref.at[rows, :],
                send.at[k],
                recv.at[k],
                (base + l, u),
            )
        )
    for copy in copies:
        copy.start()
    start = pl.multiple_of((me * sides + side) * half, half)
    mine = pltpu.make_async_copy(o_ref.at[:, pl.ds(start, half)], mixed_ref.at[rows, :], own.at[0])
    mine.start()
    parts[0] = mine_ref[...]
    for t in range(1, groups):
        remote(
            mine_ref, parts.at[t], psend.at[t - 1], precv.at[t - 1], far[t - 1]
        ).wait()
    top = parts[0, VROWS : VROWS + 1, :]
    for t in range(1, groups):
        top = jnp.maximum(top, parts[t, VROWS : VROWS + 1, :])
    total = jnp.zeros((VROWS, MEMQ), F32)
    for t in range(groups):
        total = total + parts[t, 0:VROWS, :] * jnp.exp(parts[t, VROWS : VROWS + 1, :] - top)
    mass = total[HEAD : HEAD + 1, :]
    wide = total[0:HEAD, :] / mass
    sum_ref[0:HEAD, :] = wide
    sum_ref[HEAD : HEAD + 8, :] = jnp.broadcast_to(top + jnp.log(mass), (8, MEMQ))
    memt[...] = wide.astype(BF16)
    more = []
    for k, (l, u) in enumerate(found):
        more.append(remote(memt, mem_ref.at[rows, :], msend.at[k], mrecv.at[k], (base + l, u)))
    for copy in more:
        copy.start()
    last = pltpu.make_async_copy(memt, mem_ref.at[rows, :], own.at[1])
    last.start()
    mine.wait()
    last.wait()
    for copy in copies + more:
        copy.wait()


def mix(o, mine, group, sides, groups, half):
    near = group * sides - 1
    heads = group * sides
    return pl.pallas_call(
        functools.partial(mix_kernel, group, sides, groups, half),
        out_shape=(
            jax.ShapeDtypeStruct((heads * HEAD, half), BF16),
            jax.ShapeDtypeStruct((heads * HEAD, MEMQ), BF16),
            jax.ShapeDtypeStruct((HEAD + 8, MEMQ), F32),
        ),
        in_specs=[anyspace(), vmem()],
        out_specs=(anyspace(), anyspace(), vmem()),
        scratch_shapes=[
            pltpu.VMEM((groups, SROWS, MEMQ), F32),
            pltpu.VMEM((HEAD, MEMQ), BF16),
            pltpu.SemaphoreType.DMA((2,)),
            pltpu.SemaphoreType.DMA((groups - 1,)),
            pltpu.SemaphoreType.DMA((groups - 1,)),
            pltpu.SemaphoreType.DMA((near,)),
            pltpu.SemaphoreType.DMA((near,)),
            pltpu.SemaphoreType.DMA((near,)),
            pltpu.SemaphoreType.DMA((near,)),
        ],
        compiler_params=pltpu.CompilerParams(collective_id=2, has_side_effects=True),
        name="mix",
    )(o, mine)


def unmix_kernel(
    group, sides, half, back_ref, final_ref, do_ref, out_ref, own, send, recv, fsend, frecv
):
    base, me, side, found = near_partners(group, sides)
    greet([(base + l, u) for l, u in found])
    columns = pl.ds(pl.multiple_of((me * sides + side) * half, half), half)
    copies = []
    for k, (l, u) in enumerate(found):
        head = pl.multiple_of((u * group + l) * HEAD, HEAD)
        copies.append(
            remote(
                back_ref.at[pl.ds(head, HEAD), :],
                do_ref.at[:, columns],
                send.at[k],
                recv.at[k],
                (base + l, u),
            )
        )
    rows = pl.ds(pl.multiple_of(side * half, half), half)
    for u in range(1, sides):
        copies.append(
            remote(
                final_ref,
                out_ref.at[rows, :],
                fsend.at[u - 1],
                frecv.at[u - 1],
                (base + me, lax.rem(side + u, sides)),
            )
        )
    for copy in copies:
        copy.start()
    head = pl.multiple_of((side * group + me) * HEAD, HEAD)
    mine = [
        pltpu.make_async_copy(back_ref.at[pl.ds(head, HEAD), :], do_ref.at[:, columns], own.at[0]),
        pltpu.make_async_copy(final_ref, out_ref.at[rows, :], own.at[1]),
    ]
    for copy in mine:
        copy.start()
    for copy in mine + copies:
        copy.wait()


def unmix(back, final, group, sides, half):
    near = group * sides - 1
    width = final.shape[1]
    return pl.pallas_call(
        functools.partial(unmix_kernel, group, sides, half),
        out_shape=(
            jax.ShapeDtypeStruct((HEAD, group * sides * half), BF16),
            jax.ShapeDtypeStruct((sides * half, width), BF16),
        ),
        in_specs=[anyspace()] * 2,
        out_specs=(anyspace(), anyspace()),
        scratch_shapes=[
            pltpu.SemaphoreType.DMA((2,)),
            pltpu.SemaphoreType.DMA((near,)),
            pltpu.SemaphoreType.DMA((near,)),
            pltpu.SemaphoreType.DMA((sides - 1,)),
            pltpu.SemaphoreType.DMA((sides - 1,)),
        ],
        compiler_params=pltpu.CompilerParams(collective_id=3, has_side_effects=True),
        name="unmix",
    )(back, final)


def swap_kernel(sides, part_ref, other_ref, send, recv):
    here, side = lax.axis_index("ctx"), lax.axis_index("wt")
    peer = (here, lax.rem(side + 1, sides))
    greet([peer])
    copy = remote(part_ref, other_ref, send, recv, peer)
    copy.start()
    copy.wait()


def swap(part, sides):
    return pl.pallas_call(
        functools.partial(swap_kernel, sides),
        out_shape=jax.ShapeDtypeStruct(part.shape, part.dtype),
        in_specs=[anyspace()],
        out_specs=anyspace(),
        scratch_shapes=[pltpu.SemaphoreType.DMA, pltpu.SemaphoreType.DMA],
        compiler_params=pltpu.CompilerParams(collective_id=4, has_side_effects=True),
        name="swap",
    )(part)


def doc_bounds(starts_ref, docs, first, last, total):
    low = starts_ref[0]
    low_end = total
    top = starts_ref[0]
    high = total
    for d in range(docs):
        start = starts_ref[d]
        low = jnp.where(start <= first, start, low)
        top = jnp.where(start <= last, start, top)
    for d in range(docs - 1, -1, -1):
        start = starts_ref[d]
        low_end = jnp.where(start > first, start, low_end)
        high = jnp.where(start > last, start, high)
    return low, low_end, top, high


def doc_rows(starts_ref, docs, first, total):
    place = first + lax.broadcasted_iota(jnp.int32, (1, TQ), 1)
    low = jnp.zeros((1, TQ), jnp.int32)
    high = jnp.full((1, TQ), total, jnp.int32)
    for d in range(docs):
        start = starts_ref[d]
        low = jnp.where(place >= start, start, low)
    for d in range(docs - 1, -1, -1):
        start = starts_ref[d]
        high = jnp.where(place < start, start, high)
    return low, high


def allowed_block(key_first, low, high):
    place = key_first + lax.broadcasted_iota(jnp.int32, (TK, TQ), 0)
    return (place >= low) & (place < high)


def tile(ref, number, size):
    return ref[pl.ds(pl.multiple_of(number * size, size), size), :]


def lanes(ref, number, size):
    return ref[:, pl.ds(pl.multiple_of(number * size, size), size)]


def pad_query(q, size):
    return jnp.concatenate([q, jnp.zeros((HEAD, size), BF16)], axis=0)


def fill_values(kv_ref, va, column):
    def step(k, carry):
        turned = tile(kv_ref, k, TK).T
        at = pl.ds(pl.multiple_of(column + k * TK, TK), TK)
        va[0:HEAD, at] = turned[HEAD : 2 * HEAD, :]
        va[HEAD:VROWS, at] = jnp.ones((ONES, TK), BF16)
        return carry

    lax.fori_loop(0, kv_ref.shape[0] // TK, step, 0)


def online(score, value, acc, top):
    old = top[0:1, :]
    new = jnp.maximum(old, jnp.max(score, axis=0, keepdims=True))
    share = jnp.exp(score - new).astype(BF16)
    acc[...] = acc[...] * jnp.exp(old - new) + dot(value, share)
    top[...] = jnp.broadcast_to(new, top.shape)


def forward_tiles(bounds, low, high, kv_ref, kv_first, va, va_column, qz, acc, top):
    doc_first, doc_first_end, doc_last, doc_end = bounds
    count = kv_ref.shape[0]
    begin = jnp.clip(doc_first - kv_first, 0, count) // TK
    end = (jnp.clip(doc_end - kv_first, 0, count) + TK - 1) // TK

    def step(k, carry):
        at = kv_first + k * TK
        score = dot(tile(kv_ref, k, TK), qz)
        value = va[:, pl.ds(pl.multiple_of(va_column + k * TK, TK), TK)]
        whole = (doc_first == doc_last) & (at >= doc_first) & (at + TK <= doc_end)

        @pl.when(whole)
        def _():
            online(score, value, acc, top)

        @pl.when(jnp.logical_not(whole))
        def _():
            online(jnp.where(allowed_block(at, low, high), score, MASKED), value, acc, top)

        return carry

    lax.fori_loop(begin, end, step, 0)


def forward_own_kernel(
    docs, memory_rows, meta_ref, q_ref, kv_ref, mq_ref, mkv_ref,
    state_ref, mstate_ref, va, acc, top, macc, mtop,
):
    total = meta_ref[docs]
    base = meta_ref[docs + 1]
    fill_values(kv_ref, va, 0)
    turned = mkv_ref[...].T
    mem_value = jnp.concatenate(
        [turned[HEAD : 2 * HEAD, :], jnp.ones((ONES, MEMQ), BF16)], axis=0
    )
    mem_key = mkv_ref[...]

    def query_step(qi, carry):
        first = base + qi * TQ
        bounds = doc_bounds(meta_ref, docs, first, first + TQ - 1, total)
        low, high = doc_rows(meta_ref, docs, first, total)
        qz = pad_query(lanes(q_ref, qi, TQ), TQ)
        score = dot(mem_key, qz)
        inside = lax.broadcasted_iota(jnp.int32, (MEMQ, TQ), 0) < memory_rows
        score = jnp.where(inside, score, MASKED)
        new = jnp.max(score, axis=0, keepdims=True)
        share = jnp.exp(score - new).astype(BF16)
        acc[...] = dot(mem_value, share)
        top[...] = jnp.broadcast_to(new, top.shape)
        forward_tiles(bounds, low, high, kv_ref, base, va, 0, qz, acc, top)
        at = pl.ds(pl.multiple_of(qi * TQ, TQ), TQ)
        state_ref[0:VROWS, at] = acc[...]
        state_ref[VROWS:SROWS, at] = top[...]
        return carry

    lax.fori_loop(0, q_ref.shape[1] // TQ, query_step, 0)

    mq = pad_query(mq_ref[...], MEMQ)
    macc[...] = jnp.zeros_like(macc)
    mtop[...] = jnp.full_like(mtop, MASKED)

    def memory_step(k, carry):
        online(
            dot(tile(kv_ref, k, TK), mq),
            va[:, pl.ds(pl.multiple_of(k * TK, TK), TK)],
            macc,
            mtop,
        )
        return carry

    lax.fori_loop(0, kv_ref.shape[0] // TK, memory_step, 0)
    mstate_ref[0:VROWS, :] = macc[...]
    mstate_ref[VROWS:SROWS, :] = mtop[...]


def forward_own(meta, q, kv, mq, mkv, docs, memory_rows):
    count = kv.shape[0]
    return pl.pallas_call(
        functools.partial(forward_own_kernel, docs, memory_rows),
        out_shape=(
            jax.ShapeDtypeStruct((SROWS, count), F32),
            jax.ShapeDtypeStruct((SROWS, MEMQ), F32),
        ),
        in_specs=[smem()] + [vmem()] * 4,
        out_specs=(vmem(), vmem()),
        scratch_shapes=[
            pltpu.VMEM((VROWS, count), BF16),
            pltpu.VMEM((VROWS, TQ), F32),
            pltpu.VMEM((8, TQ), F32),
            pltpu.VMEM((VROWS, MEMQ), F32),
            pltpu.VMEM((8, MEMQ), F32),
        ],
        compiler_params=pltpu.CompilerParams(vmem_limit_bytes=VMEM_LIMIT),
        cost_estimate=pl.CostEstimate(
            flops=8 * count * count * HEAD, bytes_accessed=4 << 20, transcendentals=count * count
        ),
        name="forward_own",
    )(meta, q, kv, mq, mkv)


def forward_halo_kernel(
    docs, meta_ref, q_ref, before_ref, after_ref, state_ref, o_ref, wide_ref, va, acc, top
):
    total = meta_ref[docs]
    base = meta_ref[docs + 1]
    count = before_ref.shape[0]
    fill_values(before_ref, va, 0)
    fill_values(after_ref, va, count)

    def query_step(qi, carry):
        first = base + qi * TQ
        bounds = doc_bounds(meta_ref, docs, first, first + TQ - 1, total)
        low, high = doc_rows(meta_ref, docs, first, total)
        at = pl.ds(pl.multiple_of(qi * TQ, TQ), TQ)
        qz = pad_query(lanes(q_ref, qi, TQ), TQ)
        acc[...] = state_ref[0:VROWS, at]
        top[...] = state_ref[VROWS:SROWS, at]
        forward_tiles(bounds, low, high, before_ref, base - count, va, 0, qz, acc, top)
        forward_tiles(bounds, low, high, after_ref, base + count, va, count, qz, acc, top)
        mass = acc[HEAD : HEAD + 1, :]
        wide = acc[0:HEAD, :] / mass
        o_ref[:, at] = wide.astype(BF16)
        wide_ref[0:HEAD, at] = wide
        wide_ref[HEAD : HEAD + 8, at] = top[...] + jnp.log(jnp.broadcast_to(mass, top.shape))
        return carry

    lax.fori_loop(0, q_ref.shape[1] // TQ, query_step, 0)


def forward_halo(meta, q, before, after, state, docs):
    count = before.shape[0]
    return pl.pallas_call(
        functools.partial(forward_halo_kernel, docs),
        out_shape=(
            jax.ShapeDtypeStruct((HEAD, count), BF16),
            jax.ShapeDtypeStruct((HEAD + 8, count), F32),
        ),
        in_specs=[smem()] + [vmem()] * 4,
        out_specs=(vmem(), vmem()),
        scratch_shapes=[
            pltpu.VMEM((VROWS, 2 * count), BF16),
            pltpu.VMEM((VROWS, TQ), F32),
            pltpu.VMEM((8, TQ), F32),
        ],
        compiler_params=pltpu.CompilerParams(vmem_limit_bytes=VMEM_LIMIT),
        cost_estimate=pl.CostEstimate(
            flops=4 * count * count * HEAD, bytes_accessed=6 << 20, transcendentals=count * count
        ),
        name="forward_halo",
    )(meta, q, before, after, state)


def backward_math(score, slope_source, kv_tile, log_total, delta):
    share = jnp.exp(score - log_total)
    slope = dot(kv_tile, slope_source)
    return share.astype(BF16), (share * (slope - delta)).astype(BF16)


def backward_tiles(
    bounds, low, high, kv_ref, kv_first, kt, kt_column, grad, qz, doz, qr, dor, log_total, delta, acc
):
    doc_first, doc_first_end, doc_last, doc_end = bounds
    count = kv_ref.shape[0]
    begin = jnp.clip(doc_first - kv_first, 0, count) // TK
    end = (jnp.clip(doc_end - kv_first, 0, count) + TK - 1) // TK

    def step(k, carry):
        at = kv_first + k * TK
        pair = tile(kv_ref, k, TK)
        score = dot(pair, qz)
        key = kt[:, pl.ds(pl.multiple_of(kt_column + k * TK, TK), TK)]
        where = pl.ds(pl.multiple_of(kt_column + k * TK, TK), TK)
        whole = (doc_first == doc_last) & (at >= doc_first) & (at + TK <= doc_end)

        def finish(score):
            share, back = backward_math(score, doz, pair, log_total, delta)
            grad[where, :] += dot(back, qr) + dot(share, dor)
            acc[...] += dot(key, back)

        @pl.when(whole)
        def _():
            finish(score)

        @pl.when(jnp.logical_not(whole))
        def _():
            finish(jnp.where(allowed_block(at, low, high), score, MASKED))

        return carry

    lax.fori_loop(begin, end, step, 0)


def fill_keys(kv_ref, kt, column):
    def step(k, carry):
        turned = tile(kv_ref, k, TK).T
        kt[:, pl.ds(pl.multiple_of(column + k * TK, TK), TK)] = turned[0:HEAD, :]
        return carry

    lax.fori_loop(0, kv_ref.shape[0] // TK, step, 0)


def query_sides(q, do, size):
    zero = jnp.zeros((HEAD, size), BF16)
    qz = jnp.concatenate([q, zero], axis=0)
    doz = jnp.concatenate([zero, do], axis=0)
    return qz, doz, qz.T, doz.T


def row_stats(wide, do):
    return wide[HEAD : HEAD + 1, :], jnp.sum(
        wide[0:HEAD, :] * do.astype(F32), axis=0, keepdims=True
    )


def backward_halo_kernel(
    docs, meta_ref, q_ref, do_ref, wide_ref, before_ref, after_ref,
    dq_ref, dbefore_ref, dafter_ref, kt, grad, acc,
):
    total = meta_ref[docs]
    base = meta_ref[docs + 1]
    count = before_ref.shape[0]
    fill_keys(before_ref, kt, 0)
    fill_keys(after_ref, kt, count)
    grad[...] = jnp.zeros_like(grad)

    def query_step(qi, carry):
        first = base + qi * TQ
        bounds = doc_bounds(meta_ref, docs, first, first + TQ - 1, total)
        low, high = doc_rows(meta_ref, docs, first, total)
        at = pl.ds(pl.multiple_of(qi * TQ, TQ), TQ)
        do = do_ref[:, at]
        qz, doz, qr, dor = query_sides(q_ref[:, at], do, TQ)
        log_total, delta = row_stats(wide_ref[:, at], do)
        acc[...] = jnp.zeros_like(acc)
        for ref, begin, column in (
            (before_ref, base - count, 0),
            (after_ref, base + count, count),
        ):
            backward_tiles(
                bounds, low, high, ref, begin, kt, column, grad,
                qz, doz, qr, dor, log_total, delta, acc,
            )
        dq_ref[:, at] = acc[...]
        return carry

    lax.fori_loop(0, q_ref.shape[1] // TQ, query_step, 0)
    dbefore_ref[...] = grad[0:count, :].astype(BF16)
    dafter_ref[...] = grad[count : 2 * count, :].astype(BF16)


def backward_halo(meta, q, do, wide, before, after, docs):
    count = before.shape[0]
    return pl.pallas_call(
        functools.partial(backward_halo_kernel, docs),
        out_shape=(
            jax.ShapeDtypeStruct((HEAD, count), F32),
            jax.ShapeDtypeStruct((count, 2 * HEAD), BF16),
            jax.ShapeDtypeStruct((count, 2 * HEAD), BF16),
        ),
        in_specs=[smem()] + [vmem()] * 5,
        out_specs=(vmem(),) * 3,
        scratch_shapes=[
            pltpu.VMEM((HEAD, 2 * count), BF16),
            pltpu.VMEM((2 * count, 2 * HEAD), F32),
            pltpu.VMEM((HEAD, TQ), F32),
        ],
        compiler_params=pltpu.CompilerParams(vmem_limit_bytes=VMEM_LIMIT),
        cost_estimate=pl.CostEstimate(
            flops=8 * count * count * HEAD, bytes_accessed=8 << 20, transcendentals=count * count
        ),
        name="backward_halo",
    )(meta, q, do, wide, before, after)


def backward_own_kernel(
    docs, memory_rows, meta_ref, q_ref, do_ref, wide_ref, kv_ref, part_ref,
    mq_ref, mdo_ref, mwide_ref, mkv_ref,
    dq_ref, grad, dmq_ref, mgrad, kt, acc, macc,
):
    total = meta_ref[docs]
    base = meta_ref[docs + 1]
    fill_keys(kv_ref, kt, 0)
    grad[...] = jnp.zeros_like(grad)
    mgrad[...] = jnp.zeros_like(mgrad)
    mem_pair = mkv_ref[...]
    mem_key = mem_pair.T[0:HEAD, :]
    scale = HEAD ** (-0.5)

    def query_step(qi, carry):
        first = base + qi * TQ
        bounds = doc_bounds(meta_ref, docs, first, first + TQ - 1, total)
        low, high = doc_rows(meta_ref, docs, first, total)
        at = pl.ds(pl.multiple_of(qi * TQ, TQ), TQ)
        do = do_ref[:, at]
        qz, doz, qr, dor = query_sides(q_ref[:, at], do, TQ)
        log_total, delta = row_stats(wide_ref[:, at], do)
        inside = lax.broadcasted_iota(jnp.int32, (MEMQ, TQ), 0) < memory_rows
        score = jnp.where(inside, dot(mem_pair, qz), MASKED)
        share, back = backward_math(score, doz, mem_pair, log_total, delta)
        mgrad[...] += dot(back, qr) + dot(share, dor)
        acc[...] = part_ref[:, at] + dot(mem_key, back)
        backward_tiles(
            bounds, low, high, kv_ref, base, kt, 0, grad, qz, doz, qr, dor, log_total, delta, acc
        )
        dq_ref[:, at] = (acc[...] * scale).astype(BF16)
        return carry

    lax.fori_loop(0, q_ref.shape[1] // TQ, query_step, 0)

    do = mdo_ref[...]
    qz, doz, qr, dor = query_sides(mq_ref[...], do, MEMQ)
    log_total, delta = row_stats(mwide_ref[...], do)
    macc[...] = jnp.zeros_like(macc)

    def memory_step(k, carry):
        pair = tile(kv_ref, k, TK)
        where = pl.ds(pl.multiple_of(k * TK, TK), TK)
        share, back = backward_math(dot(pair, qz), doz, pair, log_total, delta)
        grad[where, :] += dot(back, qr) + dot(share, dor)
        macc[...] += dot(kt[:, where], back)
        return carry

    lax.fori_loop(0, kv_ref.shape[0] // TK, memory_step, 0)
    dmq_ref[...] = (macc[...] * scale).astype(BF16)


def backward_own(meta, q, do, wide, kv, part, mq, mdo, mwide, mkv, docs, memory_rows):
    count = kv.shape[0]
    return pl.pallas_call(
        functools.partial(backward_own_kernel, docs, memory_rows),
        out_shape=(
            jax.ShapeDtypeStruct((HEAD, count), BF16),
            jax.ShapeDtypeStruct((count, 2 * HEAD), F32),
            jax.ShapeDtypeStruct((HEAD, MEMQ), BF16),
            jax.ShapeDtypeStruct((MEMQ, 2 * HEAD), F32),
        ),
        in_specs=[smem()] + [vmem()] * 9,
        out_specs=(vmem(),) * 4,
        scratch_shapes=[
            pltpu.VMEM((HEAD, count), BF16),
            pltpu.VMEM((HEAD, TQ), F32),
            pltpu.VMEM((HEAD, MEMQ), F32),
        ],
        compiler_params=pltpu.CompilerParams(vmem_limit_bytes=VMEM_LIMIT),
        cost_estimate=pl.CostEstimate(
            flops=16 * count * count * HEAD, bytes_accessed=8 << 20, transcendentals=count * count
        ),
        name="backward_own",
    )(meta, q, do, wide, kv, part, mq, mdo, mwide, mkv)


def activate(value):
    return jax.nn.gelu(value, approximate=True)


def normalize(value):
    centered = value - jnp.mean(value, axis=-1, keepdims=True)
    variance = jnp.mean(centered * centered, axis=-1, keepdims=True)
    return centered * lax.rsqrt(variance + EPSILON)


def local(
    tokens, memory, doc_starts, w_query, b_query, w_key, w_value, b_value, w_output, b_output,
    first_gain, first_bias, w_up, b_up, w_down, b_down, second_gain, second_bias,
    cotangent, mem_cotangent,
):
    block, model = tokens.shape
    memory_rows = memory.shape[0]
    docs = doc_starts.shape[0]
    width = w_query.shape[1]
    group = width // HEAD
    ctx, sides = lax.axis_size("ctx"), lax.axis_size("wt")
    groups = ctx // group
    here, side = lax.axis_index("ctx"), lax.axis_index("wt")
    me = lax.rem(here, group)
    half = block // sides
    span = group * block
    scale = HEAD ** (-0.5)
    total = ctx * block
    meta = jnp.concatenate(
        [
            doc_starts,
            jnp.stack([jnp.int32(total), (here // group * span).astype(jnp.int32)]),
        ]
    )

    mem_pad = jnp.pad(memory, ((0, MEMQ - memory_rows), (0, 0)))
    rows = jnp.concatenate([tokens, mem_pad], axis=0)
    w_pair = jnp.stack(
        [w_key.reshape(model, group, HEAD), w_value.reshape(model, group, HEAD)], axis=2
    ).reshape(model, 2 * width)
    b_pair = jnp.stack(
        [jnp.zeros((group, HEAD), F32), b_value.astype(F32).reshape(group, HEAD)], axis=1
    ).reshape(2 * width)
    pairs = (dot(rows, w_pair) + b_pair).astype(BF16)
    queries = lax.dot_general(w_query, rows, (((0,), (1,)), ((), ())), preferred_element_type=F32)
    queries = (queries + b_query.astype(F32)[:, None]).astype(BF16)
    queries = queries * BF16(scale)
    q, kv = scatter_heads(queries[:, :block], pairs, group, block)
    mq = lax.dynamic_slice(queries, (me * HEAD, block), (HEAD, MEMQ))
    mkv = lax.dynamic_slice(pairs, (block, me * 2 * HEAD), (MEMQ, 2 * HEAD))
    forwards = [(i, i + group) for i in range(ctx - group)]
    backwards = [(i + group, i) for i in range(ctx - group)]
    before = lax.ppermute(kv, "ctx", forwards)
    after = lax.ppermute(kv, "ctx", backwards)
    out_full = lax.all_gather(w_output, "wt", axis=0, tiled=True)
    up_full = lax.all_gather(w_up, "wt", axis=1, tiled=True)
    down_full = lax.all_gather(w_down, "wt", axis=0, tiled=True)
    b_up_full = lax.all_gather(b_up, "wt", axis=0, tiled=True)

    state, mstate = forward_own(meta, q, kv, mq, mkv, docs, memory_rows)
    o, wide = forward_halo(meta, q, before, after, state, docs)
    mixed_t, mem_t, mwide = mix(o, mstate, group, sides, groups, half)
    mixed = jnp.concatenate([mixed_t.T, mem_t[:, :MEMK].T], axis=0)

    mine = lax.dynamic_slice_in_dim(tokens, side * half, half, 0)
    own = jnp.concatenate([mine, mem_pad[:MEMK]], axis=0).astype(F32)
    weight = jnp.concatenate(
        [
            jnp.ones((half, 1), F32),
            jnp.ones((MEMK, 1), F32) * ((here == 0) & (side == 0)).astype(F32),
        ],
        axis=0,
    )
    weight_low = weight.astype(BF16)
    upstream = jnp.concatenate(
        [
            lax.dynamic_slice_in_dim(cotangent, side * half, half, 0),
            jnp.pad(mem_cotangent, ((0, MEMK - memory_rows), (0, 0))),
        ],
        axis=0,
    ).astype(F32)
    hidden_first = own + dot(mixed, out_full) + b_output
    first_hat = normalize(hidden_first)
    normed = first_hat * first_gain + first_bias
    normed_low = normed.astype(BF16)
    inner = dot(normed_low, up_full) + b_up_full
    acted_wide, activate_pull = jax.vjp(activate, inner)
    acted = acted_wide.astype(BF16)
    fed = dot(acted, down_full) + b_down
    hidden_second = normed + fed
    second_hat = normalize(hidden_second)
    final = second_hat * second_gain + second_bias
    second_gain_grad = jnp.sum(weight * second_hat * upstream, axis=0)
    second_bias_grad = jnp.sum(weight * upstream, axis=0)
    unused, second_pull = jax.vjp(normalize, hidden_second)
    (second_back,) = second_pull(upstream * second_gain)
    fed_back = second_back.astype(BF16)
    down_bias_grad = jnp.sum(weight * fed_back.astype(F32), axis=0)
    down_grad = jnp.einsum("rf,rd->fd", acted, fed_back * weight_low, preferred_element_type=F32)
    acted_back = jnp.einsum("rd,fd->rf", fed_back, down_full, preferred_element_type=F32)
    (inner_back_wide,) = activate_pull(acted_back)
    inner_back = inner_back_wide.astype(BF16)
    up_bias_grad = jnp.sum(weight * inner_back.astype(F32), axis=0)
    up_grad = jnp.einsum("rd,rf->df", normed_low, inner_back * weight_low, preferred_element_type=F32)
    normed_back = second_back + jnp.einsum(
        "rf,df->rd", inner_back, up_full, preferred_element_type=F32
    )
    first_gain_grad = jnp.sum(weight * first_hat * normed_back, axis=0)
    first_bias_grad = jnp.sum(weight * normed_back, axis=0)
    unused, first_pull = jax.vjp(normalize, hidden_first)
    (first_back,) = first_pull(normed_back * first_gain)
    attended_back = first_back.astype(BF16)
    output_bias_grad = jnp.sum(weight * attended_back.astype(F32), axis=0)
    output_grad = jnp.einsum(
        "rc,rd->cd", mixed, attended_back * weight_low, preferred_element_type=F32
    )
    mixed_back = jnp.einsum(
        "cd,rd->cr", out_full, attended_back, preferred_element_type=F32
    ).astype(BF16)
    do, token_out = unmix(mixed_back[:, :half], final[:half].astype(BF16), group, sides, half)
    memory_out = final[half : half + memory_rows].astype(BF16)
    head = side * group + me
    mdo = lax.dynamic_slice(mixed_back, (head * HEAD, half), (HEAD, MEMK))
    mdo = jnp.pad(mdo, ((0, 0), (0, MEMQ - MEMK)))

    up_part = lax.psum_scatter(up_grad.astype(BF16), "wt", scatter_dimension=1, tiled=True)
    down_part = lax.psum_scatter(down_grad.astype(BF16), "wt", scatter_dimension=0, tiled=True)
    out_part = lax.psum_scatter(output_grad.astype(BF16), "wt", scatter_dimension=0, tiled=True)
    up_sum, down_sum, out_sum = lax.psum((up_part, down_part, out_part), "ctx")

    part, dbefore, dafter = backward_halo(meta, q, do, wide, before, after, docs)
    from_after = lax.ppermute(dbefore, "ctx", backwards)
    from_before = lax.ppermute(dafter, "ctx", forwards)
    dq, dkv, dmq, dmkv = backward_own(
        meta, q, do, wide, kv, part, mq, mdo, mwide, mkv, docs, memory_rows
    )
    dkv = (dkv + from_after.astype(F32) + from_before.astype(F32)).astype(BF16)
    dq_rows, dkv_rows = gather_heads(dq, dkv, group, block)
    place = (jnp.arange(group) == me).astype(BF16)
    dmq_rows = (place[:, None, None] * dmq[None]).reshape(width, MEMQ)
    dmkv_rows = (place[None, :, None] * dmkv.astype(BF16)[:, None, :]).reshape(MEMQ, 2 * width)
    dq_all = jnp.concatenate([dq_rows, dmq_rows], axis=1)
    dkv_all = jnp.concatenate([dkv_rows, dmkv_rows], axis=0)
    query_grad = lax.dot_general(rows, dq_all, (((0,), (1,)), ((), ())), preferred_element_type=F32)
    pair_grad = lax.dot_general(rows, dkv_all, (((0,), (0,)), ((), ())), preferred_element_type=F32)
    pair_grad = pair_grad.reshape(model, group, 2, HEAD)
    key_grad = pair_grad[:, :, 0].reshape(model, width)
    value_grad = pair_grad[:, :, 1].reshape(model, width)
    query_bias_grad = jnp.sum(dq_all.astype(F32), axis=1)
    value_bias_grad = jnp.sum(
        dkv_all.astype(F32).reshape(-1, group, 2, HEAD)[:, :, 1], axis=0
    ).reshape(width)
    partial = lax.dot_general(dq_all, w_query, (((0,), (1,)), ((), ())), preferred_element_type=F32)
    partial = partial + lax.dot_general(
        dkv_all, w_pair, (((1,), (1,)), ((), ())), preferred_element_type=F32
    )
    keep = (jnp.arange(block) // half == side).astype(F32)[:, None]
    partial_rows = partial[:block] + keep * jnp.tile(first_back[:half], (sides, 1))
    token_grad = partial_rows + swap(partial_rows.astype(BF16), sides).astype(F32)
    memory_grad = first_back[half : half + memory_rows] + lax.psum(
        partial[block : block + memory_rows], ("ctx", "wt")
    )
    query_grad, key_grad, value_grad = (
        value.astype(F32)
        for value in lax.psum(
            (query_grad.astype(BF16), key_grad.astype(BF16), value_grad.astype(BF16)), "ctx"
        )
    )
    query_bias_grad, value_bias_grad = lax.psum((query_bias_grad, value_bias_grad), "ctx")
    smalls = lax.psum(
        (
            output_bias_grad, first_gain_grad, first_bias_grad, up_bias_grad, down_bias_grad,
            second_gain_grad, second_bias_grad,
        ),
        ("ctx", "wt"),
    )
    mine_up = lax.dynamic_slice_in_dim(smalls[3], side * b_up.shape[0], b_up.shape[0], 0)
    return (
        token_out, memory_out, token_grad, memory_grad,
        query_grad, query_bias_grad, key_grad, value_grad, value_bias_grad,
        out_sum.astype(F32), smalls[0], smalls[1], smalls[2],
        up_sum.astype(F32), mine_up, down_sum.astype(F32), smalls[4], smalls[5], smalls[6],
    )


def solution(mesh):
    placed = (
        P("ctx", None), P(), P(), P(None, "wt"), P("wt"), P(None, "wt"), P(None, "wt"), P("wt"),
        P("wt", None), P(), P(), P(), P(None, "wt"), P("wt"), P("wt", None), P(), P(), P(),
        P("ctx", None), P(),
    )
    return jax.shard_map(
        local,
        mesh=mesh,
        in_specs=placed,
        out_specs=(
            P("ctx", None), P(), P("ctx", None), P(), P(None, "wt"), P("wt"), P(None, "wt"),
            P(None, "wt"), P("wt"), P("wt", None), P(), P(), P(), P(None, "wt"), P("wt"),
            P("wt", None), P(), P(), P(),
        ),
        check_vma=False,
    )
```

```python
import functools

import jax
import jax.numpy as jnp
from jax import lax
from jax.experimental import pallas as pl
from jax.experimental.pallas import tpu as pltpu
from jax.sharding import PartitionSpec as P

HEAD = 64
EPSILON = 1e-05
MASKED = -1e30
MESH = pl.DeviceIdType.MESH
TQ = 512
TK = 512
MEMK = 32
MEMQ = 128
ONES = 16
VROWS = HEAD + ONES
SROWS = VROWS + 8
PACK = 256
BIAS = 128
CHUNKS = 4
GROUP = 4
F32 = jnp.float32
BF16 = jnp.bfloat16
VMEM_LIMIT = 56 * 1024 * 1024


def vmem():
    return pl.BlockSpec(memory_space=pltpu.VMEM)


def smem():
    return pl.BlockSpec(memory_space=pltpu.SMEM)


def anyspace():
    return pl.BlockSpec(memory_space=pl.ANY)


def dot(a, b):
    return jnp.dot(a, b, preferred_element_type=F32)


def dot_nt(a, b):
    return lax.dot_general(a, b, (((1,), (1,)), ((), ())), preferred_element_type=F32)


def greet(partners):
    barrier = pltpu.get_barrier_semaphore()
    for partner in partners:
        pl.semaphore_signal(barrier, inc=1, device_id=partner, device_id_type=MESH)
    pl.semaphore_wait(barrier, len(partners))


def remote(src, dst, send, recv, device):
    return pltpu.make_async_remote_copy(
        src_ref=src, dst_ref=dst, send_sem=send, recv_sem=recv, device_id=device, device_id_type=MESH
    )


def group_place(group):
    here = lax.axis_index("ctx")
    return here // group * group, lax.rem(here, group), lax.axis_index("wt")


def core_partner(me):
    return me + 1 - 2 * lax.rem(me, 2)


def scatter_kernel(
    group, block, tokens_ref, memory_ref, wq_ref, bq_ref, wk_ref, wv_ref, bv_ref,
    wo_ref, wu_ref, bu_ref,
    qo_ref, kvo_ref, wo_other, wu_other, bu_other, mq_ref, mkv_ref, mem_ref, wp_ref, wqt_ref,
    qs, kvs, bpair, bcol, own, send, recv, wsend, wrecv, fsend, frecv,
):
    base, me, side = group_place(group)
    width = 2 * HEAD
    partners = [(base + lax.rem(me + t, group), side) for t in range(1, group)]
    across = (base + me, lax.rem(side + 1, lax.axis_size("wt")))
    beside = (base + core_partner(me), side)
    greet(partners + [across])
    core = lax.rem(me, 2)
    rows_o, rows_u = wo_ref.shape[0] // 2, wu_ref.shape[0] // 2

    def part(ref, rows, which):
        return ref.at[pl.ds(pl.multiple_of(which * rows, rows), rows), :]

    firsts = [
        remote(part(wo_ref, rows_o, core), part(wo_other, rows_o, core), wsend.at[0], wrecv.at[0], across),
        remote(part(wu_ref, rows_u, core), part(wu_other, rows_u, core), wsend.at[1], wrecv.at[1], across),
        remote(bu_ref, bu_other, wsend.at[2], wrecv.at[2], across),
    ]
    for copy in firsts:
        copy.start()

    bq = bq_ref[...].astype(F32)
    bv = bv_ref[...].astype(F32)
    none = jnp.zeros((1, HEAD), F32)
    for h in range(group):
        at = slice(h * HEAD, (h + 1) * HEAD)
        wp_ref[:, h * width : (h + 1) * width] = jnp.concatenate([wk_ref[:, at], wv_ref[:, at]], axis=1)
        bpair[:, h * width : (h + 1) * width] = jnp.concatenate([none, bv[:, at]], axis=1)
    wqt_ref[...] = wq_ref[...].T
    bcol[...] = jnp.broadcast_to(bq, (BIAS, bq.shape[1])).T
    mem_ref[...] = jnp.zeros_like(mem_ref)
    mem_ref[0 : memory_ref.shape[0], :] = memory_ref[...]
    scale = HEAD ** (-0.5)

    def project(rows_value, head):
        lanes_at = pl.ds(pl.multiple_of(head * width, width), width)
        rows_at = pl.ds(pl.multiple_of(head * HEAD, HEAD), HEAD)
        pair = (dot(rows_value, wp_ref[:, lanes_at]) + bpair[:, lanes_at]).astype(BF16)
        query = (dot_nt(wqt_ref[rows_at, :], rows_value) + bcol[rows_at, 0:1]).astype(BF16)
        return pair, query * jnp.asarray(scale, BF16)

    copies = []
    mine_rows = pl.ds(pl.multiple_of(me * block, block), block)
    for k, t in enumerate((2, 1, 3) if group == 4 else range(1, group)):
        peer = lax.rem(me + t, group)
        pair, query = project(tokens_ref[...], peer)
        kvs[t] = pair
        qs[t] = query
        device = (base + peer, side)
        copies.append(remote(kvs.at[t], kvo_ref.at[mine_rows, :], send.at[2 * k], recv.at[2 * t - 2], device))
        copies.append(remote(qs.at[t], qo_ref.at[:, mine_rows], send.at[2 * k + 1], recv.at[2 * t - 1], device))
        copies[-2].start()
        copies[-1].start()
    pair, query = project(tokens_ref[...], me)
    kvs[0] = pair
    qs[0] = query
    mine = [
        pltpu.make_async_copy(kvs.at[0], kvo_ref.at[mine_rows, :], own.at[0]),
        pltpu.make_async_copy(qs.at[0], qo_ref.at[:, mine_rows], own.at[1]),
    ]
    for copy in mine:
        copy.start()
    pair, query = project(mem_ref[...], me)
    mkv_ref[...] = pair
    mq_ref[...] = query
    for copy in firsts:
        copy.wait()
    forwards = [
        remote(part(wo_other, rows_o, core), part(wo_other, rows_o, core), fsend.at[0], frecv.at[0], beside),
        remote(part(wu_other, rows_u, core), part(wu_other, rows_u, core), fsend.at[1], frecv.at[1], beside),
    ]
    for copy in forwards:
        copy.start()
    for copy in mine + copies + forwards:
        copy.wait()


def scatter_heads(tokens, memory, wq, bq, wk, wv, bv, wo, wu, bu, group):
    block, model = tokens.shape
    width = wq.shape[1]
    like = lambda a: jax.ShapeDtypeStruct(a.shape, a.dtype)
    return pl.pallas_call(
        functools.partial(scatter_kernel, group, block),
        out_shape=(
            jax.ShapeDtypeStruct((HEAD, group * block), BF16),
            jax.ShapeDtypeStruct((group * block, 2 * HEAD), BF16),
            like(wo), like(wu), like(bu),
            jax.ShapeDtypeStruct((HEAD, MEMQ), BF16),
            jax.ShapeDtypeStruct((MEMQ, 2 * HEAD), BF16),
            jax.ShapeDtypeStruct((MEMQ, model), BF16),
            jax.ShapeDtypeStruct((model, 2 * width), BF16),
            jax.ShapeDtypeStruct((width, model), BF16),
        ),
        in_specs=[vmem()] * 7 + [anyspace()] * 3,
        out_specs=(anyspace(),) * 5 + (vmem(),) * 5,
        scratch_shapes=[
            pltpu.VMEM((group, HEAD, block), BF16),
            pltpu.VMEM((group, block, 2 * HEAD), BF16),
            pltpu.VMEM((1, 2 * width), F32),
            pltpu.VMEM((width, BIAS), F32),
            pltpu.SemaphoreType.DMA((2,)),
            pltpu.SemaphoreType.DMA((2 * group - 2,)),
            pltpu.SemaphoreType.DMA((2 * group - 2,)),
            pltpu.SemaphoreType.DMA((3,)),
            pltpu.SemaphoreType.DMA((3,)),
            pltpu.SemaphoreType.DMA((2,)),
            pltpu.SemaphoreType.DMA((2,)),
        ],
        compiler_params=pltpu.CompilerParams(
            collective_id=0, has_side_effects=True, vmem_limit_bytes=VMEM_LIMIT
        ),
        name="scatter_heads",
    )(tokens, memory, wq, bq, wk, wv, bv, wo, wu, bu)


def tail_kernel(
    group, groups, sides, block, dq_ref, dkv_ref, pack_ref, first_ref, wqt_ref, wp_ref, grad_ref,
    part_ref, other_ref, packs_ref, mems_ref, grads_ref,
    parts, sums, qrows, kvrows, low, own, send, recv, rsend, rrecv, gsend, grecv,
    xsend, xrecv, psend, precv, msend, mrecv, csend, crecv,
):
    base, me, side = group_place(group)
    number = base // group
    width = 2 * HEAD
    across = lax.rem(side + 1, sides)
    partners = [(base + lax.rem(me + t, group), side) for t in range(1, group)]
    far = [(lax.rem(number + t, groups) * group + me, side) for t in range(1, groups)]
    beyond = [(base + lax.rem(me + t, group), across) for t in range(group)]
    greet(partners + far + beyond)
    core = lax.rem(me, 2)
    beside = remote(
        grad_ref, grads_ref.at[core], csend, crecv, (base + core_partner(me), side)
    )
    rows = PACK // groups
    reduces = []
    for t in range(1, groups):
        peer = lax.rem(number + t, groups)
        at = pl.ds(pl.multiple_of(peer * rows, rows), rows)
        reduces.append(
            remote(pack_ref.at[at, :], parts.at[t - 1], rsend.at[t - 1], rrecv.at[t - 1], far[t - 1])
        )
    for copy in reduces:
        copy.start()
    chunk = block // CHUNKS
    head_rows = pl.ds(pl.multiple_of(me * HEAD, HEAD), HEAD)
    head_lanes = pl.ds(pl.multiple_of(me * width, width), width)
    moves = []
    for r in range(CHUNKS):
        step = []
        for t in range(1, group):
            peer = lax.rem(me + t, group)
            at = pl.ds(pl.multiple_of(peer * block + r * chunk, chunk), chunk)
            here = pl.ds(r * chunk, chunk)
            slot = (r * (group - 1) + t - 1) * 2
            step.append(
                remote(dkv_ref.at[at, :], kvrows.at[here, head_lanes], send.at[slot], recv.at[slot], partners[t - 1])
            )
            step.append(
                remote(dq_ref.at[:, at], qrows.at[head_rows, here], send.at[slot + 1], recv.at[slot + 1], partners[t - 1])
            )
        moves.append(step)
    for step in moves[:2]:
        for copy in step:
            copy.start()
    beside.start()
    at = pl.ds(pl.multiple_of(me * block, block), block)
    mine = [
        pltpu.make_async_copy(dkv_ref.at[at, :], kvrows.at[:, head_lanes], own.at[0]),
        pltpu.make_async_copy(dq_ref.at[:, at], qrows.at[head_rows, :], own.at[1]),
        pltpu.make_async_copy(grad_ref, grads_ref.at[core], own.at[2]),
    ]
    for copy in mine:
        copy.start()
    here = pl.ds(pl.multiple_of(number * rows, rows), rows)
    total = pack_ref[here, :].astype(F32)
    for t in range(1, groups):
        reduces[t - 1].wait()
        total = total + parts[t - 1].astype(F32)
    sums[here, :] = total.astype(BF16)
    spread = []
    for t in range(1, groups):
        spread.append(
            remote(sums.at[here, :], sums.at[here, :], gsend.at[t - 1], grecv.at[t - 1], far[t - 1])
        )
    for copy in spread:
        copy.start()
    mine[0].wait()
    mine[1].wait()
    swaps = []
    half = block // sides
    for r in range(CHUNKS):
        for copy in moves[r]:
            copy.wait()
        at = pl.ds(r * chunk, chunk)
        value = dot(qrows[:, at].T, wqt_ref[...]) + dot_nt(kvrows[at, :], wp_ref[...])
        inside = (r * chunk) // half
        extra = first_ref[pl.ds(r * chunk - inside * half, chunk), :]
        value = value + extra * (side == inside).astype(F32)
        part_ref[at, :] = value
        low[at, :] = value.astype(BF16)
        swaps.append(remote(low.at[at, :], other_ref.at[at, :], xsend.at[r], xrecv.at[r], beyond[0]))
        swaps[-1].start()
        if r + 2 < CHUNKS:
            for copy in moves[r + 2]:
                copy.start()
    for copy in spread:
        copy.wait()
    memory = pl.ds(3 * HEAD, MEMK)
    extras = []
    for t in range(1, group):
        extras.append(
            remote(sums, packs_ref.at[me], psend.at[t - 1], precv.at[t - 1], partners[t - 1])
        )
    for t in range(group):
        extras.append(
            remote(sums.at[memory, :], mems_ref.at[me], msend.at[t], mrecv.at[t], beyond[t])
        )
    for copy in extras:
        copy.start()
    last = pltpu.make_async_copy(sums, packs_ref.at[me], own.at[3])
    last.start()
    last.wait()
    mine[2].wait()
    beside.wait()
    for copy in swaps + extras:
        copy.wait()


def tail(dq, dkv, pack, first, wqt, wp, grad, group, groups, sides, block):
    model = first.shape[1]
    width = wqt.shape[0]
    moves = CHUNKS * (group - 1) * 2
    return pl.pallas_call(
        functools.partial(tail_kernel, group, groups, sides, block),
        out_shape=(
            jax.ShapeDtypeStruct((block, model), F32),
            jax.ShapeDtypeStruct((block, model), BF16),
            jax.ShapeDtypeStruct((group,) + pack.shape, BF16),
            jax.ShapeDtypeStruct((group, MEMK, model), BF16),
            jax.ShapeDtypeStruct((2,) + grad.shape, BF16),
        ),
        in_specs=[anyspace()] * 2 + [vmem()] * 4 + [anyspace()],
        out_specs=(vmem(),) + (anyspace(),) * 4,
        scratch_shapes=[
            pltpu.VMEM((groups - 1, PACK // groups, model), BF16),
            pltpu.VMEM((PACK, model), BF16),
            pltpu.VMEM((width, block), BF16),
            pltpu.VMEM((block, 2 * width), BF16),
            pltpu.VMEM((block, model), BF16),
            pltpu.SemaphoreType.DMA((4,)),
            pltpu.SemaphoreType.DMA((moves,)),
            pltpu.SemaphoreType.DMA((moves,)),
            pltpu.SemaphoreType.DMA((groups - 1,)),
            pltpu.SemaphoreType.DMA((groups - 1,)),
            pltpu.SemaphoreType.DMA((groups - 1,)),
            pltpu.SemaphoreType.DMA((groups - 1,)),
            pltpu.SemaphoreType.DMA((CHUNKS,)),
            pltpu.SemaphoreType.DMA((CHUNKS,)),
            pltpu.SemaphoreType.DMA((group - 1,)),
            pltpu.SemaphoreType.DMA((group - 1,)),
            pltpu.SemaphoreType.DMA((group,)),
            pltpu.SemaphoreType.DMA((group,)),
            pltpu.SemaphoreType.DMA,
            pltpu.SemaphoreType.DMA,
        ],
        compiler_params=pltpu.CompilerParams(
            collective_id=1, has_side_effects=True, vmem_limit_bytes=VMEM_LIMIT
        ),
        name="tail",
    )(dq, dkv, pack, first, wqt, wp, grad)


def near_partners(group, sides):
    base, me, side = group_place(group)
    found = []
    for u in range(sides):
        for t in range(group):
            if t or u:
                found.append((lax.rem(me + t, group), lax.rem(side + u, sides), u))
    return base, me, side, found


def mix_kernel(
    group, sides, groups, half,
    o_ref, mine_ref, mixed_ref, mem_ref, sum_ref,
    parts, memt, own, psend, precv, send, recv, msend, mrecv,
):
    base, me, side, found = near_partners(group, sides)
    number = base // group
    far = [
        (lax.rem(number + t, groups) * group + me, side) for t in range(1, groups)
    ]
    greet([(base + l, u) for l, u, apart in found] + far)
    for t in range(1, groups):
        remote(
            mine_ref, parts.at[t], psend.at[t - 1], precv.at[t - 1], far[t - 1]
        ).start()
    def rows(apart):
        slot = (sides - apart) % sides * group
        return pl.ds(pl.multiple_of((slot + me) * HEAD, HEAD), HEAD)

    copies = []
    for k, (l, u, apart) in enumerate(found):
        start = pl.multiple_of((l * sides + u) * half, half)
        copies.append(
            remote(
                o_ref.at[:, pl.ds(start, half)],
                mixed_ref.at[rows(apart), :],
                send.at[k],
                recv.at[k],
                (base + l, u),
            )
        )
    for copy in copies:
        copy.start()
    start = pl.multiple_of((me * sides + side) * half, half)
    mine = pltpu.make_async_copy(
        o_ref.at[:, pl.ds(start, half)], mixed_ref.at[rows(0), :], own.at[0]
    )
    mine.start()
    parts[0] = mine_ref[...]
    for t in range(1, groups):
        remote(
            mine_ref, parts.at[t], psend.at[t - 1], precv.at[t - 1], far[t - 1]
        ).wait()
    top = parts[0, VROWS : VROWS + 1, :]
    for t in range(1, groups):
        top = jnp.maximum(top, parts[t, VROWS : VROWS + 1, :])
    total = jnp.zeros((VROWS, MEMQ), F32)
    for t in range(groups):
        total = total + parts[t, 0:VROWS, :] * jnp.exp(parts[t, VROWS : VROWS + 1, :] - top)
    mass = total[HEAD : HEAD + 1, :]
    wide = total[0:HEAD, :] / mass
    sum_ref[0:HEAD, :] = wide
    sum_ref[HEAD : HEAD + 8, :] = jnp.broadcast_to(top + jnp.log(mass), (8, MEMQ))
    memt[...] = wide.astype(BF16)
    more = []
    for k, (l, u, apart) in enumerate(found):
        more.append(
            remote(memt, mem_ref.at[rows(apart), :], msend.at[k], mrecv.at[k], (base + l, u))
        )
    for copy in more:
        copy.start()
    last = pltpu.make_async_copy(memt, mem_ref.at[rows(0), :], own.at[1])
    last.start()
    mine.wait()
    last.wait()
    for copy in copies + more:
        copy.wait()


def mix(o, mine, group, sides, groups, half):
    near = group * sides - 1
    heads = group * sides
    return pl.pallas_call(
        functools.partial(mix_kernel, group, sides, groups, half),
        out_shape=(
            jax.ShapeDtypeStruct((heads * HEAD, half), BF16),
            jax.ShapeDtypeStruct((heads * HEAD, MEMQ), BF16),
            jax.ShapeDtypeStruct((HEAD + 8, MEMQ), F32),
        ),
        in_specs=[anyspace(), vmem()],
        out_specs=(anyspace(), anyspace(), vmem()),
        scratch_shapes=[
            pltpu.VMEM((groups, SROWS, MEMQ), F32),
            pltpu.VMEM((HEAD, MEMQ), BF16),
            pltpu.SemaphoreType.DMA((2,)),
            pltpu.SemaphoreType.DMA((groups - 1,)),
            pltpu.SemaphoreType.DMA((groups - 1,)),
            pltpu.SemaphoreType.DMA((near,)),
            pltpu.SemaphoreType.DMA((near,)),
            pltpu.SemaphoreType.DMA((near,)),
            pltpu.SemaphoreType.DMA((near,)),
        ],
        compiler_params=pltpu.CompilerParams(collective_id=2, has_side_effects=True),
        name="mix",
    )(o, mine)


def unmix_kernel(
    group, sides, half, back_ref, gown_ref, gpeer_ref,
    do_ref, hown_ref, hpeer_ref, buffers, own, send, recv, csend, crecv,
):
    base, me, side, found = near_partners(group, sides)
    greet([(base + l, u) for l, u, apart in found])
    columns = pl.ds(pl.multiple_of((me * sides + side) * half, half), half)
    core = lax.rem(me, 2)
    size = hown_ref.shape[0]
    theirs = pl.ds(pl.multiple_of((1 - core) * size, size), size)
    ours = pl.ds(pl.multiple_of(core * size, size), size)
    beside = (base + core_partner(me), side)
    copies = []
    for k, (l, u, apart) in enumerate(found):
        head = pl.multiple_of((apart * group + l) * HEAD, HEAD)
        copies.append(
            remote(
                back_ref.at[pl.ds(head, HEAD), pl.ds(0, half)],
                do_ref.at[:, columns],
                send.at[k],
                recv.at[k],
                (base + l, u),
            )
        )
    sums = []
    for k, (grad, total) in enumerate(((gpeer_ref, hpeer_ref), (gown_ref, hown_ref))):
        sums.append(
            (remote(grad.at[theirs, :], buffers.at[k], csend.at[k], crecv.at[k], beside), grad, total)
        )
    for copy in copies + [entry[0] for entry in sums]:
        copy.start()
    head = pl.multiple_of(me * HEAD, HEAD)
    mine = [
        pltpu.make_async_copy(
            back_ref.at[pl.ds(head, HEAD), pl.ds(0, half)], do_ref.at[:, columns], own.at[0]
        ),
    ]
    for copy in mine:
        copy.start()
    for k, (copy, grad, total) in enumerate(sums):
        copy.wait()
        total[...] = (grad[ours, :].astype(F32) + buffers[k].astype(F32)).astype(BF16)
    for copy in mine + copies:
        copy.wait()


def unmix(back, gown, gpeer, group, sides, half):
    near = group * sides - 1
    width = gown.shape[1]
    size = gown.shape[0] // 2
    return pl.pallas_call(
        functools.partial(unmix_kernel, group, sides, half),
        out_shape=(
            jax.ShapeDtypeStruct((HEAD, group * sides * half), BF16),
            jax.ShapeDtypeStruct((size, width), BF16),
            jax.ShapeDtypeStruct((size, width), BF16),
        ),
        in_specs=[anyspace()] + [vmem()] * 2,
        out_specs=(anyspace(), vmem(), vmem()),
        scratch_shapes=[
            pltpu.VMEM((2, size, width), BF16),
            pltpu.SemaphoreType.DMA((1,)),
            pltpu.SemaphoreType.DMA((near,)),
            pltpu.SemaphoreType.DMA((near,)),
            pltpu.SemaphoreType.DMA((2,)),
            pltpu.SemaphoreType.DMA((2,)),
        ],
        compiler_params=pltpu.CompilerParams(
            collective_id=3, has_side_effects=True, vmem_limit_bytes=VMEM_LIMIT
        ),
        name="unmix",
    )(back, gown, gpeer)


def span_place(span):
    block = span // GROUP
    return lax.axis_size("ctx") * block, lax.axis_index("ctx") // GROUP * span


def doc_bounds(starts_ref, docs, first, last, total):
    low = starts_ref[0]
    low_end = total
    top = starts_ref[0]
    high = total
    for d in range(docs):
        start = starts_ref[d]
        low = jnp.where(start <= first, start, low)
        top = jnp.where(start <= last, start, top)
    for d in range(docs - 1, -1, -1):
        start = starts_ref[d]
        low_end = jnp.where(start > first, start, low_end)
        high = jnp.where(start > last, start, high)
    return low, low_end, top, high


def doc_rows(starts_ref, docs, first, total):
    place = first + lax.broadcasted_iota(jnp.int32, (1, TQ), 1)
    low = jnp.zeros((1, TQ), jnp.int32)
    high = jnp.full((1, TQ), total, jnp.int32)
    for d in range(docs):
        start = starts_ref[d]
        low = jnp.where(place >= start, start, low)
    for d in range(docs - 1, -1, -1):
        start = starts_ref[d]
        high = jnp.where(place < start, start, high)
    return low, high


def allowed_block(key_first, low, high):
    place = lax.broadcasted_iota(jnp.int32, (TK, TQ), 0) - (low - key_first)
    return place.astype(jnp.uint32) < (high - low).astype(jnp.uint32)


def tile(ref, number, size):
    return ref[pl.ds(pl.multiple_of(number * size, size), size), :]


def lanes(ref, number, size):
    return ref[:, pl.ds(pl.multiple_of(number * size, size), size)]


def pad_query(q, size):
    return jnp.concatenate([q, jnp.zeros((HEAD, size), BF16)], axis=0)


def fill_values(kv_ref, va, column, begin, end):
    def step(k, carry):
        turned = tile(kv_ref, k, TK).T
        at = pl.ds(pl.multiple_of(column + k * TK, TK), TK)
        va[0:HEAD, at] = turned[HEAD : 2 * HEAD, :]
        va[HEAD:VROWS, at] = jnp.ones((ONES, TK), BF16)
        return carry

    lax.fori_loop(begin, end, step, 0)


def key_range(bounds, kv_first, count):
    begin = jnp.clip(bounds[0] - kv_first, 0, count) // TK
    end = (jnp.clip(bounds[3] - kv_first, 0, count) + TK - 1) // TK
    return begin, end


def pair_loop(bounds, begin, end, kv_first, low, high, score, use):
    doc_first, doc_first_end, doc_last, doc_end = bounds
    single = doc_first == doc_last

    @pl.when(begin < end)
    def _():
        score(0, begin)

        def step(i, carry):
            k = begin + 2 * i
            at = kv_first + k * TK
            both = k + 1 < end
            whole = single & both & (at >= doc_first) & (at + 2 * TK <= doc_end)

            @pl.when(whole)
            def _():
                score(1, k + 1)
                use(0, k, None)
                score(0, k + 2)
                use(1, k + 1, None)

            @pl.when(jnp.logical_not(whole) & both)
            def _():
                score(1, k + 1)
                use(0, k, allowed_block(at, low, high))
                score(0, k + 2)
                use(1, k + 1, allowed_block(at + TK, low, high))

            @pl.when(jnp.logical_not(both))
            def _():
                use(0, k, allowed_block(at, low, high))

            return carry

        lax.fori_loop(0, (end - begin + 1) // 2, step, 0)


def online(score, value, acc, top):
    old = top[0:1, :]
    new = jnp.maximum(old, jnp.max(score, axis=0, keepdims=True))
    share = jnp.exp(score - new).astype(BF16)
    acc[...] = acc[...] * jnp.exp(old - new) + dot(value, share)
    top[...] = jnp.broadcast_to(new, top.shape)


def forward_tiles(bounds, low, high, kv_ref, kv_first, va, va_column, qz, acc, top, held):
    begin, end = key_range(bounds, kv_first, kv_ref.shape[0])

    def score(slot, k):
        held[slot][...] = dot(tile(kv_ref, jnp.minimum(k, end - 1), TK), qz)

    def use(slot, k, allowed):
        at = pl.ds(pl.multiple_of(va_column + k * TK, TK), TK)
        score = held[slot][...]
        if allowed is not None:
            score = jnp.where(allowed, score, MASKED)
        online(score, va[:, at], acc, top)

    pair_loop(bounds, begin, end, kv_first, low, high, score, use)


def forward_own_kernel(
    docs, span, memory_rows, meta_ref, q_ref, kv_ref, mq_ref, mkv_ref,
    state_ref, mstate_ref, va, acc, top, held0, held1,
):
    total, base = span_place(span)
    fill_values(kv_ref, va, 0, 0, span // TK)
    turned = mkv_ref[...].T
    mem_value = jnp.concatenate(
        [turned[HEAD : 2 * HEAD, 0:MEMK], jnp.ones((ONES, MEMK), BF16)], axis=0
    )
    score = dot(mkv_ref[0:MEMK, 0:HEAD], q_ref[...])
    inside = lax.broadcasted_iota(jnp.int32, score.shape, 0) < memory_rows
    score = jnp.where(inside, score, MASKED)
    new = jnp.max(score, axis=0, keepdims=True)
    state_ref[0:VROWS, :] = dot(mem_value, jnp.exp(score - new).astype(BF16))
    state_ref[VROWS:SROWS, :] = jnp.broadcast_to(new, (8, span))

    def query_step(qi, carry):
        first = base + qi * TQ
        bounds = doc_bounds(meta_ref, docs, first, first + TQ - 1, total)
        low, high = doc_rows(meta_ref, docs, first, total)
        at = pl.ds(pl.multiple_of(qi * TQ, TQ), TQ)
        qz = pad_query(q_ref[:, at], TQ)
        acc[...] = state_ref[0:VROWS, at]
        top[...] = state_ref[VROWS:SROWS, at]
        forward_tiles(bounds, low, high, kv_ref, base, va, 0, qz, acc, top, (held0, held1))
        state_ref[0:VROWS, at] = acc[...]
        state_ref[VROWS:SROWS, at] = top[...]
        return carry

    lax.fori_loop(0, span // TQ, query_step, 0)

    score = dot(kv_ref[...], pad_query(mq_ref[...], MEMQ))
    new = jnp.max(score, axis=0, keepdims=True)
    mstate_ref[0:VROWS, :] = dot(va[...], jnp.exp(score - new).astype(BF16))
    mstate_ref[VROWS:SROWS, :] = jnp.broadcast_to(new, (8, MEMQ))


def forward_own(meta, q, kv, mq, mkv, docs, memory_rows):
    count = kv.shape[0]
    return pl.pallas_call(
        functools.partial(forward_own_kernel, docs, count, memory_rows),
        out_shape=(
            jax.ShapeDtypeStruct((SROWS, count), F32),
            jax.ShapeDtypeStruct((SROWS, MEMQ), F32),
        ),
        in_specs=[smem()] + [vmem()] * 4,
        out_specs=(vmem(), vmem()),
        scratch_shapes=[
            pltpu.VMEM((VROWS, count), BF16),
            pltpu.VMEM((VROWS, TQ), F32),
            pltpu.VMEM((8, TQ), F32),
            pltpu.VMEM((TK, TQ), F32),
            pltpu.VMEM((TK, TQ), F32),
        ],
        compiler_params=pltpu.CompilerParams(vmem_limit_bytes=VMEM_LIMIT),
        cost_estimate=pl.CostEstimate(
            flops=8 * count * count * HEAD, bytes_accessed=4 << 20, transcendentals=count * count
        ),
        name="forward_own",
    )(meta, q, kv, mq, mkv)


def halo_ranges(meta_ref, docs, base, span, total):
    first = doc_bounds(meta_ref, docs, base, base + span - 1, total)
    before = jnp.clip(first[0] - (base - span), 0, span) // TK
    after = (jnp.clip(first[3] - (base + span), 0, span) + TK - 1) // TK
    return before, after


def forward_halo_kernel(
    docs, span, meta_ref, q_ref, before_ref, after_ref, state_ref, o_ref, wide_ref,
    va, acc, top, held0, held1,
):
    total, base = span_place(span)
    count = before_ref.shape[0]
    from_before, to_after = halo_ranges(meta_ref, docs, base, span, total)
    fill_values(before_ref, va, 0, from_before, span // TK)
    fill_values(after_ref, va, count, 0, to_after)
    held = (held0, held1)

    def query_step(qi, carry):
        first = base + qi * TQ
        bounds = doc_bounds(meta_ref, docs, first, first + TQ - 1, total)
        low, high = doc_rows(meta_ref, docs, first, total)
        at = pl.ds(pl.multiple_of(qi * TQ, TQ), TQ)
        qz = pad_query(q_ref[:, at], TQ)
        acc[...] = state_ref[0:VROWS, at]
        top[...] = state_ref[VROWS:SROWS, at]
        forward_tiles(bounds, low, high, before_ref, base - count, va, 0, qz, acc, top, held)
        forward_tiles(bounds, low, high, after_ref, base + count, va, count, qz, acc, top, held)
        mass = acc[HEAD : HEAD + 1, :]
        wide = acc[0:HEAD, :] / mass
        o_ref[:, at] = wide.astype(BF16)
        wide_ref[0:HEAD, at] = wide
        wide_ref[HEAD : HEAD + 8, at] = top[...] + jnp.log(jnp.broadcast_to(mass, top.shape))
        return carry

    lax.fori_loop(0, span // TQ, query_step, 0)


def forward_halo(meta, q, before, after, state, docs):
    count = before.shape[0]
    return pl.pallas_call(
        functools.partial(forward_halo_kernel, docs, count),
        out_shape=(
            jax.ShapeDtypeStruct((HEAD, count), BF16),
            jax.ShapeDtypeStruct((HEAD + 8, count), F32),
        ),
        in_specs=[smem()] + [vmem()] * 4,
        out_specs=(vmem(), vmem()),
        scratch_shapes=[
            pltpu.VMEM((VROWS, 2 * count), BF16),
            pltpu.VMEM((VROWS, TQ), F32),
            pltpu.VMEM((8, TQ), F32),
            pltpu.VMEM((TK, TQ), F32),
            pltpu.VMEM((TK, TQ), F32),
        ],
        compiler_params=pltpu.CompilerParams(vmem_limit_bytes=VMEM_LIMIT),
        cost_estimate=pl.CostEstimate(
            flops=4 * count * count * HEAD, bytes_accessed=6 << 20, transcendentals=count * count
        ),
        name="forward_halo",
    )(meta, q, before, after, state)


def backward_tiles(
    bounds, low, high, kv_ref, kv_first, kt, kt_column, grad, sides, stats, acc, held
):
    qz, doz, qr, dor = sides
    log_total, delta = stats
    begin, end = key_range(bounds, kv_first, kv_ref.shape[0])

    def score(slot, k):
        pair = tile(kv_ref, jnp.minimum(k, end - 1), TK)
        held[slot][...] = dot(pair, qz)
        held[slot + 2][...] = dot(pair, doz)

    def use(slot, k, allowed):
        at = pl.ds(pl.multiple_of(kt_column + k * TK, TK), TK)
        share = jnp.exp(held[slot][...] - log_total)
        if allowed is not None:
            share = jnp.where(allowed, share, 0.0)
        back = (share * (held[slot + 2][...] - delta)).astype(BF16)
        grad[at, :] += dot(back, qr) + dot(share.astype(BF16), dor)
        acc[...] += dot(kt[:, at], back)

    pair_loop(bounds, begin, end, kv_first, low, high, score, use)


def fill_keys(kv_ref, kt, column, begin, end):
    def step(k, carry):
        turned = tile(kv_ref, k, TK).T
        kt[:, pl.ds(pl.multiple_of(column + k * TK, TK), TK)] = turned[0:HEAD, :]
        return carry

    lax.fori_loop(begin, end, step, 0)


def query_sides(q, do, size):
    zero = jnp.zeros((HEAD, size), BF16)
    qz = jnp.concatenate([q, zero], axis=0)
    doz = jnp.concatenate([zero, do], axis=0)
    return qz, doz, qz.T, doz.T


def row_stats(wide, do):
    return wide[HEAD : HEAD + 1, :], jnp.sum(
        wide[0:HEAD, :] * do.astype(F32), axis=0, keepdims=True
    )


def backward_halo_kernel(
    docs, span, meta_ref, q_ref, do_ref, wide_ref, before_ref, after_ref,
    dq_ref, dbefore_ref, dafter_ref, kt, grad, acc, *held,
):
    total, base = span_place(span)
    count = before_ref.shape[0]
    from_before, to_after = halo_ranges(meta_ref, docs, base, span, total)
    fill_keys(before_ref, kt, 0, from_before, span // TK)
    fill_keys(after_ref, kt, count, 0, to_after)

    def clear(k, carry):
        grad[pl.ds(pl.multiple_of(k * TK, TK), TK), :] = jnp.zeros((TK, 2 * HEAD), F32)
        return carry

    lax.fori_loop(from_before, span // TK + to_after, clear, 0)

    def query_step(qi, carry):
        first = base + qi * TQ
        bounds = doc_bounds(meta_ref, docs, first, first + TQ - 1, total)
        low, high = doc_rows(meta_ref, docs, first, total)
        at = pl.ds(pl.multiple_of(qi * TQ, TQ), TQ)
        acc[...] = jnp.zeros_like(acc)

        @pl.when((bounds[0] < base) | (bounds[3] > base + count))
        def _():
            do = do_ref[:, at]
            sides = query_sides(q_ref[:, at], do, TQ)
            stats = row_stats(wide_ref[:, at], do)
            for ref, begin, column in (
                (before_ref, base - count, 0),
                (after_ref, base + count, count),
            ):
                backward_tiles(
                    bounds, low, high, ref, begin, kt, column, grad, sides, stats, acc, held
                )

        dq_ref[:, at] = acc[...]
        return carry

    lax.fori_loop(0, span // TQ, query_step, 0)
    dbefore_ref[...] = jnp.zeros_like(dbefore_ref)
    dafter_ref[...] = jnp.zeros_like(dafter_ref)

    def keep_before(k, carry):
        at = pl.ds(pl.multiple_of(k * TK, TK), TK)
        dbefore_ref[at, :] = grad[at, :].astype(BF16)
        return carry

    def keep_after(k, carry):
        at = pl.ds(pl.multiple_of(k * TK, TK), TK)
        dafter_ref[at, :] = grad[pl.ds(pl.multiple_of(count + k * TK, TK), TK), :].astype(BF16)
        return carry

    lax.fori_loop(from_before, span // TK, keep_before, 0)
    lax.fori_loop(0, to_after, keep_after, 0)


def backward_halo(meta, q, do, wide, before, after, docs):
    count = before.shape[0]
    return pl.pallas_call(
        functools.partial(backward_halo_kernel, docs, count),
        out_shape=(
            jax.ShapeDtypeStruct((HEAD, count), F32),
            jax.ShapeDtypeStruct((count, 2 * HEAD), BF16),
            jax.ShapeDtypeStruct((count, 2 * HEAD), BF16),
        ),
        in_specs=[smem()] + [vmem()] * 5,
        out_specs=(vmem(),) * 3,
        scratch_shapes=[
            pltpu.VMEM((HEAD, 2 * count), BF16),
            pltpu.VMEM((2 * count, 2 * HEAD), F32),
            pltpu.VMEM((HEAD, TQ), F32),
        ]
        + [pltpu.VMEM((TK, TQ), F32)] * 4,
        compiler_params=pltpu.CompilerParams(vmem_limit_bytes=VMEM_LIMIT),
        cost_estimate=pl.CostEstimate(
            flops=8 * count * count * HEAD, bytes_accessed=8 << 20, transcendentals=count * count
        ),
        name="backward_halo",
    )(meta, q, do, wide, before, after)


def backward_own_kernel(
    docs, span, memory_rows, meta_ref, q_ref, do_ref, wide_ref, kv_ref, part_ref,
    mq_ref, mdo_ref, mwide_ref, mkv_ref,
    dq_ref, grad, dmq_ref, mgrad, kt, acc, delta_ref, wide_dq, *held,
):
    total, base = span_place(span)
    fill_keys(kv_ref, kt, 0, 0, span // TK)
    scale = HEAD ** (-0.5)

    delta_ref[...] = jnp.broadcast_to(
        jnp.sum(wide_ref[0:HEAD, :] * do_ref[...].astype(F32), axis=0, keepdims=True), (8, span)
    )
    score = dot(mkv_ref[0:MEMK, 0:HEAD], q_ref[...])
    inside = lax.broadcasted_iota(jnp.int32, score.shape, 0) < memory_rows
    share = jnp.exp(jnp.where(inside, score, MASKED) - wide_ref[HEAD : HEAD + 1, :])
    slope = dot(mkv_ref[0:MEMK, HEAD : 2 * HEAD], do_ref[...])
    back = (share * (slope - delta_ref[0:1, :])).astype(BF16)
    mgrad[...] = jnp.zeros_like(mgrad)
    mgrad[0:MEMK, :] = jnp.concatenate(
        [dot_nt(back, q_ref[...]), dot_nt(share.astype(BF16), do_ref[...])], axis=1
    )
    mem_key = mkv_ref[...].T[0:HEAD, 0:MEMK]
    wide_dq[...] = part_ref[...] + dot(mem_key, back)

    me = lax.rem(lax.axis_index("ctx"), GROUP)
    mdo = mdo_ref[pl.ds(pl.multiple_of(me * HEAD, HEAD), HEAD), mdo_ref.shape[1] - MEMQ :]
    qz, doz, qr, dor = query_sides(mq_ref[...], mdo, MEMQ)
    log_total, delta = row_stats(mwide_ref[...], mdo)
    share = jnp.exp(dot(kv_ref[...], qz) - log_total)
    back = (share * (dot(kv_ref[...], doz) - delta)).astype(BF16)
    grad[...] = dot(back, qr) + dot(share.astype(BF16), dor)
    dmq_ref[...] = (dot(kt[...], back) * scale).astype(BF16)

    def query_step(qi, carry):
        first = base + qi * TQ
        bounds = doc_bounds(meta_ref, docs, first, first + TQ - 1, total)
        low, high = doc_rows(meta_ref, docs, first, total)
        at = pl.ds(pl.multiple_of(qi * TQ, TQ), TQ)
        sides = query_sides(q_ref[:, at], do_ref[:, at], TQ)
        stats = wide_ref[HEAD : HEAD + 1, at], delta_ref[0:1, at]
        acc[...] = wide_dq[:, at]
        backward_tiles(bounds, low, high, kv_ref, base, kt, 0, grad, sides, stats, acc, held)
        dq_ref[:, at] = (acc[...] * scale).astype(BF16)
        return carry

    lax.fori_loop(0, span // TQ, query_step, 0)


def backward_own(meta, q, do, wide, kv, part, mq, mdo, mwide, mkv, docs, memory_rows):
    count = kv.shape[0]
    return pl.pallas_call(
        functools.partial(backward_own_kernel, docs, count, memory_rows),
        out_shape=(
            jax.ShapeDtypeStruct((HEAD, count), BF16),
            jax.ShapeDtypeStruct((count, 2 * HEAD), F32),
            jax.ShapeDtypeStruct((HEAD, MEMQ), BF16),
            jax.ShapeDtypeStruct((MEMQ, 2 * HEAD), F32),
        ),
        in_specs=[smem()] + [vmem()] * 9,
        out_specs=(vmem(),) * 4,
        scratch_shapes=[
            pltpu.VMEM((HEAD, count), BF16),
            pltpu.VMEM((HEAD, TQ), F32),
            pltpu.VMEM((8, count), F32),
            pltpu.VMEM((HEAD, count), F32),
        ]
        + [pltpu.VMEM((TK, TQ), F32)] * 4,
        compiler_params=pltpu.CompilerParams(vmem_limit_bytes=VMEM_LIMIT),
        cost_estimate=pl.CostEstimate(
            flops=16 * count * count * HEAD, bytes_accessed=8 << 20, transcendentals=count * count
        ),
        name="backward_own",
    )(meta, q, do, wide, kv, part, mq, mdo, mwide, mkv)


def mean(value):
    return jnp.mean(value, axis=-1, keepdims=True)


def norm_parts(value):
    centered = value - mean(value)
    scale = lax.rsqrt(mean(centered * centered) + EPSILON)
    return centered * scale, scale


def norm_back(back, hat, scale):
    return scale * (back - mean(back) - hat * mean(back * hat))


def feed_kernel(
    half, tokens_ref, mem_ref, cot_ref, mcot_ref, mixed_ref, memt_ref,
    wo_a, wo_b, wu_a, wu_b, wd_a, wd_b, bo_ref, fg_ref, fb_ref, bd_ref, sg_ref, sb_ref, bu_a, bu_b,
    final_ref, mfinal_ref, back_ref, first_ref, gown_ref, gpeer_ref,
    acted_ref, slope_ref, hidden_ref, low_ref, lowt_ref, fed_ref, mup_ref,
):
    side = lax.axis_index("wt")
    leader = ((lax.axis_index("ctx") == 0) & (side == 0)).astype(jnp.int32)
    mup_ref[...] = jnp.zeros_like(mup_ref)
    mup_ref[0 : mcot_ref.shape[0], :] = mcot_ref[...]
    model = tokens_ref.shape[1]
    rows = half + MEMQ
    mine = pl.ds(pl.multiple_of(side * half, half), half)
    hidden = wu_a.shape[1]
    chunk = 512
    place = lax.broadcasted_iota(jnp.int32, (rows, 1), 0)
    weight = jnp.where((place < half) | (leader == 1), 1.0, 0.0).astype(F32)
    b_output, first_gain, first_bias, b_down, second_gain, second_bias = (
        ref[...].astype(F32) for ref in (bo_ref, fg_ref, fb_ref, bd_ref, sg_ref, sb_ref)
    )
    mixed_t = jnp.concatenate([mixed_ref[...], memt_ref[...]], axis=1)
    mixed = mixed_t.T
    heads = wo_a.shape[0]
    attended = dot(mixed[:, 0:heads], wo_a[...]) + dot(mixed[:, heads : 2 * heads], wo_b[...])
    own = jnp.concatenate([tokens_ref[mine, :], mem_ref[...]], axis=0).astype(F32)
    first_hat, first_scale = norm_parts(own + attended + b_output)
    normed = first_hat * first_gain + first_bias
    low = normed.astype(BF16)
    low_ref[...] = low
    lowt_ref[...] = (low.astype(F32) * weight).astype(BF16).T
    hidden_ref[...] = normed + b_down
    root = 0.7978845608028654
    for part, (wu, wd, bu) in enumerate(((wu_a, wd_a, bu_a), (wu_b, wd_b, bu_b))):

        def up_step(k, carry, part=part, wu=wu, wd=wd, bu=bu):
            at = pl.ds(pl.multiple_of(k * chunk, chunk), chunk)
            to = pl.ds(pl.multiple_of(part * hidden + k * chunk, chunk), chunk)
            inner = dot(low_ref[...], wu[:, at]) + bu[0:1, at].astype(F32)
            square = inner * inner
            bent = jnp.tanh(root * inner * (1.0 + 0.044715 * square))
            grown = 0.5 * (1.0 + bent)
            acted = (inner * grown).astype(BF16)
            acted_ref[:, to] = acted
            slope_ref[:, to] = grown + 0.5 * inner * (1.0 - bent * bent) * root * (
                1.0 + 0.134145 * square
            )
            hidden_ref[...] += dot(acted, wd[at, :])
            return carry

        lax.fori_loop(0, hidden // chunk, up_step, 0)
    second_hat, second_scale = norm_parts(hidden_ref[...])
    final = second_hat * second_gain + second_bias
    final_ref[...] = final[0:half].astype(BF16)
    mfinal_ref[...] = final[half:rows].astype(BF16)
    upstream = jnp.concatenate([cot_ref[mine, :], mup_ref[...]], axis=0).astype(F32)
    weighted = upstream * weight
    second_gain_grad = jnp.sum(second_hat * weighted, axis=0, keepdims=True)
    second_bias_grad = jnp.sum(weighted, axis=0, keepdims=True)
    second_back = norm_back(upstream * second_gain, second_hat, second_scale)
    fed = second_back.astype(BF16)
    fed_wide = fed.astype(F32) * weight
    down_bias_grad = jnp.sum(fed_wide, axis=0, keepdims=True)
    fed_ref[...] = fed
    fed_low = fed_wide.astype(BF16)
    hidden_ref[...] = second_back
    zero = jnp.zeros((24, model), F32)
    for part, (wu, wd, grad_ref) in enumerate(((wu_a, wd_a, gown_ref), (wu_b, wd_b, gpeer_ref))):
        for k in range(hidden // chunk):
            at = slice(k * chunk, (k + 1) * chunk)
            to = slice(part * hidden + k * chunk, part * hidden + (k + 1) * chunk)
            back = (dot_nt(fed_ref[...], wd[at, :]) * slope_ref[:, to]).astype(BF16)
            grad_ref[at, :] = dot(lowt_ref[...], back).astype(BF16)
            grad_ref[hidden + k * chunk : hidden + (k + 1) * chunk, :] = dot(
                acted_ref[:, to].T, fed_low
            ).astype(BF16)
            hidden_ref[...] += dot_nt(back, wu[:, at])
            row = 2 * hidden + heads + k
            grad_ref[row : row + 1, :] = jnp.sum(
                back.astype(F32) * weight, axis=0, keepdims=True
            ).astype(BF16)
    normed_back = hidden_ref[...]
    weighted_back = normed_back * weight
    first_gain_grad = jnp.sum(first_hat * weighted_back, axis=0, keepdims=True)
    first_bias_grad = jnp.sum(weighted_back, axis=0, keepdims=True)
    first_back = norm_back(normed_back * first_gain, first_hat, first_scale)
    first_ref[...] = first_back
    attended_back = first_back.astype(BF16)
    attended_wide = attended_back.astype(F32) * weight
    output_bias_grad = jnp.sum(attended_wide, axis=0, keepdims=True)
    attended_low = attended_wide.astype(BF16)
    back_ref[0:heads, :] = dot_nt(wo_a[...], attended_back).astype(BF16)
    back_ref[heads : 2 * heads, :] = dot_nt(wo_b[...], attended_back).astype(BF16)
    out_grad = dot(mixed_t, attended_low).astype(BF16)
    begin = 2 * hidden + heads + hidden // chunk
    small = jnp.concatenate(
        [
            output_bias_grad, first_gain_grad, first_bias_grad, down_bias_grad,
            second_gain_grad, second_bias_grad, zero,
        ],
        axis=0,
    ).astype(BF16)
    for part, grad_ref in enumerate((gown_ref, gpeer_ref)):
        grad_ref[2 * hidden : 2 * hidden + heads, :] = out_grad[part * heads : (part + 1) * heads, :]
        grad_ref[begin : begin + 30, :] = small


def feed(tokens, mem, cot, mcot, mixed, memt, weights, vectors, bu_a, bu_b, half):
    model = tokens.shape[1]
    rows = half + MEMQ
    heads, hidden = weights[0].shape[0], weights[2].shape[1]
    grads = 2 * hidden + heads + 32
    return pl.pallas_call(
        functools.partial(feed_kernel, half),
        out_shape=(
            jax.ShapeDtypeStruct((half, model), BF16),
            jax.ShapeDtypeStruct((MEMQ, model), BF16),
            jax.ShapeDtypeStruct((2 * heads, rows), BF16),
            jax.ShapeDtypeStruct((rows, model), F32),
            jax.ShapeDtypeStruct((grads, model), BF16),
            jax.ShapeDtypeStruct((grads, model), BF16),
        ),
        in_specs=[vmem()] * 20,
        out_specs=(vmem(),) * 6,
        scratch_shapes=[
            pltpu.VMEM((rows, 2 * hidden), BF16),
            pltpu.VMEM((rows, 2 * hidden), F32),
            pltpu.VMEM((rows, model), F32),
            pltpu.VMEM((rows, model), BF16),
            pltpu.VMEM((model, rows), BF16),
            pltpu.VMEM((rows, model), BF16),
            pltpu.VMEM((MEMQ, model), BF16),
        ],
        compiler_params=pltpu.CompilerParams(vmem_limit_bytes=VMEM_LIMIT),
        cost_estimate=pl.CostEstimate(
            flops=12 * rows * model * 2 * hidden, bytes_accessed=16 << 20, transcendentals=rows * hidden
        ),
        name="feed",
    )(tokens, mem, cot, mcot, mixed, memt, *weights, *vectors, bu_a, bu_b)


def grads_kernel(
    dq_ref, dkv_ref, one_ref, two_ref, tokens_ref, dmq_ref, dmkv_ref, mem_ref, wqt_ref, wp_ref,
    low_ref, pack_ref, acc, bias,
):
    acc[...] = jnp.zeros_like(acc)
    bias[...] = jnp.zeros_like(bias)
    step_rows = 512

    def step(k, carry):
        at = pl.ds(pl.multiple_of(k * step_rows, step_rows), step_rows)
        low = (dkv_ref[at, :] + one_ref[at, :].astype(F32) + two_ref[at, :].astype(F32)).astype(BF16)
        low_ref[at, :] = low
        left = jnp.concatenate([dq_ref[:, at], low.T], axis=0)
        acc[...] += dot(left, tokens_ref[at, :])
        bias[...] += jnp.sum(left.astype(F32), axis=1, keepdims=True)
        return carry

    lax.fori_loop(0, dkv_ref.shape[0] // step_rows, step, 0)
    dmkv = dmkv_ref[...].astype(BF16)
    left = jnp.concatenate([dmq_ref[...], dmkv.T], axis=0)
    model = mem_ref.shape[1]
    me = lax.rem(lax.axis_index("ctx"), GROUP)
    pack_ref[0 : 3 * HEAD, :] = (acc[...] + dot(left, mem_ref[...])).astype(BF16)
    wq = wqt_ref[pl.ds(pl.multiple_of(me * HEAD, HEAD), HEAD), :]
    wp = wp_ref[:, pl.ds(pl.multiple_of(me * 2 * HEAD, 2 * HEAD), 2 * HEAD)]
    memory = dot(dmq_ref[...].T, wq) + dot_nt(dmkv, wp)
    pack_ref[3 * HEAD : 3 * HEAD + MEMK, :] = memory[0:MEMK, :].astype(BF16)
    columns = bias[...] + jnp.sum(left.astype(F32), axis=1, keepdims=True)
    rest = PACK - 3 * HEAD - MEMK
    turned = columns.T[0:rest, :]
    pack_ref[3 * HEAD + MEMK : PACK, :] = jnp.concatenate(
        [turned, jnp.zeros((rest, model - 3 * HEAD), F32)], axis=1
    ).astype(BF16)


def weight_grads(dq, dkv, one, two, tokens, dmq, dmkv, mem, wq, wp):
    count = dkv.shape[0]
    model = tokens.shape[1]
    return pl.pallas_call(
        grads_kernel,
        out_shape=(
            jax.ShapeDtypeStruct((count, 2 * HEAD), BF16),
            jax.ShapeDtypeStruct((PACK, model), BF16),
        ),
        in_specs=[vmem()] * 10,
        out_specs=(vmem(),) * 2,
        scratch_shapes=[
            pltpu.VMEM((3 * HEAD, model), F32),
            pltpu.VMEM((3 * HEAD, BIAS), F32),
        ],
        compiler_params=pltpu.CompilerParams(vmem_limit_bytes=VMEM_LIMIT),
        cost_estimate=pl.CostEstimate(
            flops=6 * HEAD * count * model, bytes_accessed=9 << 20, transcendentals=0
        ),
        name="weight_grads",
    )(dq, dkv, one, two, tokens, dmq, dmkv, mem, wq, wp)


def result_kernel(
    group, memory_rows, part_ref, other_ref, packs_ref, mems_ref, first_ref, sum_ref, final_ref, far_ref,
    out_token_ref, token_ref, memory_ref, query_ref, qbias_ref, key_ref, value_ref, vbias_ref,
    out_ref, up_ref, down_ref, upb_ref, small_ref,
):
    model = part_ref.shape[1]
    hidden, width = down_ref.shape[0], out_ref.shape[0]
    token_ref[...] = part_ref[...] + other_ref[...].astype(F32)
    side = lax.axis_index("wt")
    half = final_ref.shape[0]
    out_token_ref[pl.ds(pl.multiple_of(side * half, half), half), :] = final_ref[...]
    out_token_ref[pl.ds(pl.multiple_of((1 - side) * half, half), half), :] = far_ref[...]
    rows = slice(3 * HEAD, 3 * HEAD + MEMK)
    total = first_ref[first_ref.shape[0] - MEMQ : first_ref.shape[0] - MEMQ + MEMK, :]
    for h in range(group):
        total = total + packs_ref[h, rows, :].astype(F32) + mems_ref[h].astype(F32)
    memory_ref[...] = total[0:memory_rows, :]
    for at, ref in ((0, query_ref), (HEAD, key_ref), (2 * HEAD, value_ref)):
        for h in range(0, group, 2):
            both = jnp.concatenate(
                [packs_ref[h, at : at + HEAD, :], packs_ref[h + 1, at : at + HEAD, :]], axis=0
            )
            ref[:, h * HEAD : (h + 2) * HEAD] = both.T.astype(F32)
    row = 3 * HEAD + MEMK
    for at, ref in ((0, qbias_ref), (2 * HEAD, vbias_ref)):
        ref[...] = jnp.concatenate(
            [packs_ref[h, row : row + 1, at : at + HEAD].astype(F32) for h in range(group)], axis=1
        )
    for k in range(hidden // model):
        up_ref[:, k * model : (k + 1) * model] = sum_ref[k * model : (k + 1) * model, :].astype(F32)
    down_ref[...] = sum_ref[hidden : 2 * hidden, :].astype(F32)
    begin = 2 * hidden + width
    out_ref[...] = sum_ref[2 * hidden : begin, :].astype(F32)
    chunks = hidden // model
    upb_ref[...] = jnp.concatenate(
        [sum_ref[begin + k : begin + k + 1, :].astype(F32) for k in range(chunks)], axis=1
    )
    small_ref[...] = sum_ref[begin : begin + 16, :].astype(F32)


def results(part, other, packs, mems, first, total, final, far, group, memory_rows, hidden):
    block, model = part.shape
    width = group * HEAD
    shape = lambda *dims: jax.ShapeDtypeStruct(dims, F32)
    return pl.pallas_call(
        functools.partial(result_kernel, group, memory_rows),
        out_shape=(
            jax.ShapeDtypeStruct((block, model), BF16),
            shape(block, model), shape(memory_rows, model),
            shape(model, width), shape(1, width), shape(model, width), shape(model, width),
            shape(1, width), shape(width, model), shape(model, hidden), shape(hidden, model),
            shape(1, hidden), shape(16, model),
        ),
        in_specs=[vmem()] * 8,
        out_specs=(vmem(),) * 13,
        compiler_params=pltpu.CompilerParams(vmem_limit_bytes=VMEM_LIMIT),
        name="results",
    )(part, other, packs, mems, first, total, final, far)


def local(
    tokens, memory, doc_starts, w_query, b_query, w_key, w_value, b_value, w_output, b_output,
    first_gain, first_bias, w_up, b_up, w_down, b_down, second_gain, second_bias,
    cotangent, mem_cotangent,
):
    block, model = tokens.shape
    memory_rows = memory.shape[0]
    docs = doc_starts.shape[0]
    width = w_query.shape[1]
    hidden = w_up.shape[1]
    group = width // HEAD
    ctx, sides = lax.axis_size("ctx"), lax.axis_size("wt")
    groups = ctx // group
    half = block // sides
    row = lambda a: a.reshape(1, a.shape[0])

    q, kv, out_b, up_b, bias_b, mq, mkv, mem_pad, w_pair, wq_t = scatter_heads(
        tokens, memory, w_query, row(b_query), w_key, w_value, row(b_value),
        w_output, w_up, b_up.reshape(8, hidden // 8), group,
    )
    forwards = [(i, i + group) for i in range(ctx - group)]
    backwards = [(i + group, i) for i in range(ctx - group)]
    swapped = [(i, (i + 1) % sides) for i in range(sides)]
    before = lax.ppermute(kv, "ctx", forwards)
    after = lax.ppermute(kv, "ctx", backwards)
    down_b = lax.ppermute(w_down, "wt", swapped)
    teams = [[g * group + l for l in range(group)] for g in range(groups)]
    late_tokens, kv = lax.optimization_barrier((tokens, kv))
    group_tokens = lax.all_gather(late_tokens, "ctx", axis_index_groups=teams, tiled=True)

    state, mstate = forward_own(doc_starts, q, kv, mq, mkv, docs, memory_rows)
    o, wide = forward_halo(doc_starts, q, before, after, state, docs)
    mixed_t, mem_t, mwide = mix(o, mstate, group, sides, groups, half)
    final, mfinal, back, first_back, gown, gpeer = feed(
        tokens, mem_pad, cotangent, mem_cotangent, mixed_t, mem_t,
        (w_output, out_b, w_up, up_b, w_down, down_b),
        [row(a) for a in (b_output, first_gain, first_bias, b_down, second_gain, second_bias)],
        row(b_up), bias_b.reshape(1, hidden), half,
    )
    do, gown, gpeer = unmix(back, gown, gpeer, group, sides, half)
    from_peer = lax.ppermute(gpeer, "wt", swapped)

    part, dbefore, dafter = backward_halo(doc_starts, q, do, wide, before, after, docs)
    from_peer, dbefore, dafter = lax.optimization_barrier((from_peer, dbefore, dafter))
    far = lax.ppermute(lax.optimization_barrier((final, dbefore))[0], "wt", swapped)
    from_after = lax.ppermute(dbefore, "ctx", backwards)
    from_before = lax.ppermute(dafter, "ctx", forwards)
    gsum = (gown.astype(F32) + from_peer.astype(F32)).astype(BF16)
    cores = [[i for i in range(ctx) if i % 2 == c] for c in range(2)]
    gsum = lax.psum(gsum, "ctx", axis_index_groups=cores)
    dq, dkv, dmq, dmkv = backward_own(
        doc_starts, q, do, wide, kv, part, mq, back, mwide, mkv, docs, memory_rows
    )
    dkv, pack = weight_grads(
        dq, dkv, from_after, from_before, group_tokens, dmq, dmkv, mem_pad, wq_t, w_pair
    )
    part, other, packs, mems, total = tail(
        dq, dkv, pack, first_back, wq_t, w_pair, gsum, group, groups, sides, block
    )
    total = total.reshape(2 * gsum.shape[0], model)
    (
        token_out, token_grad, memory_grad, query_grad, query_bias, key_grad, value_grad, value_bias,
        out_grad, up_grad, down_grad, up_bias, small,
    ) = results(
        part, other, packs, mems, first_back, total, final, far, group, memory_rows, hidden
    )
    chunks = hidden // model
    return (
        token_out, mfinal[:memory_rows], token_grad, memory_grad,
        query_grad, query_bias.reshape(width), key_grad, value_grad, value_bias.reshape(width),
        out_grad, small[chunks], small[chunks + 1], small[chunks + 2],
        up_grad, up_bias.reshape(hidden), down_grad,
        small[chunks + 3], small[chunks + 4], small[chunks + 5],
    )


def solution(mesh):
    placed = (
        P("ctx", None), P(), P(), P(None, "wt"), P("wt"), P(None, "wt"), P(None, "wt"), P("wt"),
        P("wt", None), P(), P(), P(), P(None, "wt"), P("wt"), P("wt", None), P(), P(), P(),
        P("ctx", None), P(),
    )
    return jax.shard_map(
        local,
        mesh=mesh,
        in_specs=placed,
        out_specs=(
            P("ctx", None), P(), P("ctx", None), P(), P(None, "wt"), P("wt"), P(None, "wt"),
            P(None, "wt"), P("wt"), P("wt", None), P(), P(), P(), P(None, "wt"), P("wt"),
            P("wt", None), P(), P(), P(),
        ),
        check_vma=False,
    )
```

```python
import functools

import jax
import jax.numpy as jnp
from jax import lax
from jax.experimental import pallas as pl
from jax.experimental.pallas import tpu as pltpu
from jax.sharding import PartitionSpec as P

HEAD = 64
EPSILON = 1e-05
MASKED = -1e30
MESH = pl.DeviceIdType.MESH
TQ = 512
TK = 512
MEMK = 32
MEMQ = 128
ONES = 16
VROWS = HEAD + ONES
SROWS = VROWS + 8
PACK = 256
BIAS = 128
CHUNKS = 4
AHEAD = 2
GROUP = 4
F32 = jnp.float32
BF16 = jnp.bfloat16
VMEM_LIMIT = 56 * 1024 * 1024


def vmem():
    return pl.BlockSpec(memory_space=pltpu.VMEM)


def smem():
    return pl.BlockSpec(memory_space=pltpu.SMEM)


def anyspace():
    return pl.BlockSpec(memory_space=pl.ANY)


def dot(a, b):
    return jnp.dot(a, b, preferred_element_type=F32)


def dot_nt(a, b):
    return lax.dot_general(a, b, (((1,), (1,)), ((), ())), preferred_element_type=F32)


def greet(partners):
    barrier = pltpu.get_barrier_semaphore()
    for partner in partners:
        pl.semaphore_signal(barrier, inc=1, device_id=partner, device_id_type=MESH)
    pl.semaphore_wait(barrier, len(partners))


def remote(src, dst, send, recv, device):
    return pltpu.make_async_remote_copy(
        src_ref=src, dst_ref=dst, send_sem=send, recv_sem=recv, device_id=device, device_id_type=MESH
    )


def group_place(group):
    here = lax.axis_index("ctx")
    return here // group * group, lax.rem(here, group), lax.axis_index("wt")


def core_partner(me):
    return me + 1 - 2 * lax.rem(me, 2)


def scatter_kernel(
    group, block, tokens_ref, memory_ref, wq_ref, bq_ref, wk_ref, wv_ref, bv_ref,
    wo_ref, wu_ref, bu_ref,
    qo_ref, kvo_ref, wo_other, wu_other, bu_other, mq_ref, mkv_ref, mem_ref, wp_ref, wqt_ref,
    qs, kvs, bpair, bcol, own, send, recv, wsend, wrecv, fsend, frecv,
):
    base, me, side = group_place(group)
    width = 2 * HEAD
    partners = [(base + lax.rem(me + t, group), side) for t in range(1, group)]
    across = (base + me, lax.rem(side + 1, lax.axis_size("wt")))
    beside = (base + core_partner(me), side)
    greet(partners + [across])
    core = lax.rem(me, 2)
    rows_o, rows_u = wo_ref.shape[0] // 2, wu_ref.shape[0] // 2

    def part(ref, rows, which):
        return ref.at[pl.ds(pl.multiple_of(which * rows, rows), rows), :]

    firsts = [
        remote(part(wo_ref, rows_o, core), part(wo_other, rows_o, core), wsend.at[0], wrecv.at[0], across),
        remote(part(wu_ref, rows_u, core), part(wu_other, rows_u, core), wsend.at[1], wrecv.at[1], across),
        remote(bu_ref, bu_other, wsend.at[2], wrecv.at[2], across),
    ]
    for copy in firsts:
        copy.start()

    bq = bq_ref[...].astype(F32)
    bv = bv_ref[...].astype(F32)
    none = jnp.zeros((1, HEAD), F32)
    for h in range(group):
        at = slice(h * HEAD, (h + 1) * HEAD)
        wp_ref[:, h * width : (h + 1) * width] = jnp.concatenate([wk_ref[:, at], wv_ref[:, at]], axis=1)
        bpair[:, h * width : (h + 1) * width] = jnp.concatenate([none, bv[:, at]], axis=1)
    wqt_ref[...] = wq_ref[...].T
    bcol[...] = jnp.broadcast_to(bq, (BIAS, bq.shape[1])).T
    mem_ref[...] = jnp.zeros_like(mem_ref)
    mem_ref[0 : memory_ref.shape[0], :] = memory_ref[...]
    scale = HEAD ** (-0.5)

    def project(rows_value, head):
        lanes_at = pl.ds(pl.multiple_of(head * width, width), width)
        rows_at = pl.ds(pl.multiple_of(head * HEAD, HEAD), HEAD)
        pair = (dot(rows_value, wp_ref[:, lanes_at]) + bpair[:, lanes_at]).astype(BF16)
        query = (dot_nt(wqt_ref[rows_at, :], rows_value) + bcol[rows_at, 0:1]).astype(BF16)
        return pair, query * jnp.asarray(scale, BF16)

    copies = []
    mine_rows = pl.ds(pl.multiple_of(me * block, block), block)
    for k, t in enumerate((2, 1, 3) if group == 4 else range(1, group)):
        peer = lax.rem(me + t, group)
        pair, query = project(tokens_ref[...], peer)
        kvs[t] = pair
        qs[t] = query
        device = (base + peer, side)
        copies.append(remote(kvs.at[t], kvo_ref.at[mine_rows, :], send.at[2 * k], recv.at[2 * t - 2], device))
        copies.append(remote(qs.at[t], qo_ref.at[:, mine_rows], send.at[2 * k + 1], recv.at[2 * t - 1], device))
        copies[-2].start()
        copies[-1].start()
    pair, query = project(tokens_ref[...], me)
    kvs[0] = pair
    qs[0] = query
    mine = [
        pltpu.make_async_copy(kvs.at[0], kvo_ref.at[mine_rows, :], own.at[0]),
        pltpu.make_async_copy(qs.at[0], qo_ref.at[:, mine_rows], own.at[1]),
    ]
    for copy in mine:
        copy.start()
    pair, query = project(mem_ref[...], me)
    mkv_ref[...] = pair
    mq_ref[...] = query
    for copy in firsts:
        copy.wait()
    forwards = [
        remote(part(wo_other, rows_o, core), part(wo_other, rows_o, core), fsend.at[0], frecv.at[0], beside),
        remote(part(wu_other, rows_u, core), part(wu_other, rows_u, core), fsend.at[1], frecv.at[1], beside),
    ]
    for copy in forwards:
        copy.start()
    for copy in mine + copies + forwards:
        copy.wait()


def scatter_heads(tokens, memory, wq, bq, wk, wv, bv, wo, wu, bu, group):
    block, model = tokens.shape
    width = wq.shape[1]
    like = lambda a: jax.ShapeDtypeStruct(a.shape, a.dtype)
    return pl.pallas_call(
        functools.partial(scatter_kernel, group, block),
        out_shape=(
            jax.ShapeDtypeStruct((HEAD, group * block), BF16),
            jax.ShapeDtypeStruct((group * block, 2 * HEAD), BF16),
            like(wo), like(wu), like(bu),
            jax.ShapeDtypeStruct((HEAD, MEMQ), BF16),
            jax.ShapeDtypeStruct((MEMQ, 2 * HEAD), BF16),
            jax.ShapeDtypeStruct((MEMQ, model), BF16),
            jax.ShapeDtypeStruct((model, 2 * width), BF16),
            jax.ShapeDtypeStruct((width, model), BF16),
        ),
        in_specs=[vmem()] * 7 + [anyspace()] * 3,
        out_specs=(anyspace(),) * 5 + (vmem(),) * 5,
        scratch_shapes=[
            pltpu.VMEM((group, HEAD, block), BF16),
            pltpu.VMEM((group, block, 2 * HEAD), BF16),
            pltpu.VMEM((1, 2 * width), F32),
            pltpu.VMEM((width, BIAS), F32),
            pltpu.SemaphoreType.DMA((2,)),
            pltpu.SemaphoreType.DMA((2 * group - 2,)),
            pltpu.SemaphoreType.DMA((2 * group - 2,)),
            pltpu.SemaphoreType.DMA((3,)),
            pltpu.SemaphoreType.DMA((3,)),
            pltpu.SemaphoreType.DMA((2,)),
            pltpu.SemaphoreType.DMA((2,)),
        ],
        compiler_params=pltpu.CompilerParams(
            collective_id=0, has_side_effects=True, vmem_limit_bytes=VMEM_LIMIT
        ),
        name="scatter_heads",
    )(tokens, memory, wq, bq, wk, wv, bv, wo, wu, bu)


def tail_kernel(
    group, groups, sides, block, dq_ref, dkv_ref, pack_ref, first_ref, wqt_ref, wp_ref,
    part_ref, other_ref, packs_ref,
    parts, sums, mems, qrows, kvrows, low, own, send, recv, rsend, rrecv, gsend, grecv,
    xsend, xrecv, psend, precv, msend, mrecv,
):
    base, me, side = group_place(group)
    number = base // group
    width = 2 * HEAD
    across = (base + me, lax.rem(side + 1, sides))
    partners = [(base + lax.rem(me + t, group), side) for t in range(1, group)]
    far = [(lax.rem(number + t, groups) * group + me, side) for t in range(1, groups)]
    greet(partners + far + [across])
    rows = PACK // groups
    reduces = []
    for t in range(1, groups):
        peer = lax.rem(number + t, groups)
        at = pl.ds(pl.multiple_of(peer * rows, rows), rows)
        reduces.append(
            remote(pack_ref.at[at, :], parts.at[t - 1], rsend.at[t - 1], rrecv.at[t - 1], far[t - 1])
        )
    for copy in reduces:
        copy.start()
    chunk = block // CHUNKS
    head_rows = pl.ds(pl.multiple_of(me * HEAD, HEAD), HEAD)
    head_lanes = pl.ds(pl.multiple_of(me * width, width), width)
    moves = []
    for r in range(CHUNKS):
        step = []
        for t in range(1, group):
            peer = lax.rem(me + t, group)
            at = pl.ds(pl.multiple_of(peer * block + r * chunk, chunk), chunk)
            here = pl.ds(r * chunk, chunk)
            slot = (r * (group - 1) + t - 1) * 2
            step.append(
                remote(dkv_ref.at[at, :], kvrows.at[here, head_lanes], send.at[slot], recv.at[slot], partners[t - 1])
            )
            step.append(
                remote(dq_ref.at[:, at], qrows.at[head_rows, here], send.at[slot + 1], recv.at[slot + 1], partners[t - 1])
            )
        moves.append(step)
    for step in moves[:AHEAD]:
        for copy in step:
            copy.start()
    at = pl.ds(pl.multiple_of(me * block, block), block)
    mine = [
        pltpu.make_async_copy(dkv_ref.at[at, :], kvrows.at[:, head_lanes], own.at[0]),
        pltpu.make_async_copy(dq_ref.at[:, at], qrows.at[head_rows, :], own.at[1]),
    ]
    for copy in mine:
        copy.start()
    mine[0].wait()
    mine[1].wait()
    swaps, spread = [], []
    half = block // sides
    memory = pl.ds(3 * HEAD, MEMK)
    here = pl.ds(pl.multiple_of(number * rows, rows), rows)

    def reduced():
        total = pack_ref[here, :].astype(F32)
        for t in range(1, groups):
            reduces[t - 1].wait()
            total = total + parts[t - 1].astype(F32)
        sums[here, :] = total.astype(BF16)
        for t in range(1, groups):
            spread.append(
                remote(sums.at[here, :], sums.at[here, :], gsend.at[t - 1], grecv.at[t - 1], far[t - 1])
            )
            spread[-1].start()

    exchange = remote(sums.at[memory, :], mems, msend, mrecv, across)
    beside = (base + core_partner(me), side)
    opposite = lax.rem(me + 2, group)
    first = [
        remote(sums, packs_ref.at[me], psend.at[0], precv.at[0], (base + opposite, side)),
        remote(sums, packs_ref.at[me], psend.at[1], precv.at[1], beside),
    ]
    last = pltpu.make_async_copy(sums, packs_ref.at[me], own.at[2])
    second = remote(packs_ref.at[opposite], packs_ref.at[opposite], psend.at[2], precv.at[2], beside)
    for r in range(CHUNKS):
        for copy in moves[r]:
            copy.wait()
        if r + AHEAD < CHUNKS:
            for copy in moves[r + AHEAD]:
                copy.start()
        at = pl.ds(r * chunk, chunk)
        value = dot(qrows[:, at].T, wqt_ref[...]) + dot_nt(kvrows[at, :], wp_ref[...])
        inside = (r * chunk) // half
        extra = first_ref[pl.ds(r * chunk - inside * half, chunk), :]
        value = value + extra * (side == inside).astype(F32)
        part_ref[at, :] = value
        low[at, :] = value.astype(BF16)
        swaps.append(remote(low.at[at, :], other_ref.at[at, :], xsend.at[r], xrecv.at[r], across))
        swaps[-1].start()
        if r == 0:
            reduced()
        if r == 1:
            for copy in spread:
                copy.wait()
            exchange.start()
        if r == CHUNKS - 1:
            exchange.wait()
            sums[memory, :] = (sums[memory, :].astype(F32) + mems[...].astype(F32)).astype(BF16)
            for copy in first:
                copy.start()
            last.start()
    first[0].wait()
    second.start()
    last.wait()
    first[1].wait()
    second.wait()
    for copy in swaps:
        copy.wait()


def tail(dq, dkv, pack, first, wqt, wp, group, groups, sides, block):
    model = first.shape[1]
    width = wqt.shape[0]
    moves = CHUNKS * (group - 1) * 2
    return pl.pallas_call(
        functools.partial(tail_kernel, group, groups, sides, block),
        out_shape=(
            jax.ShapeDtypeStruct((block, model), F32),
            jax.ShapeDtypeStruct((block, model), BF16),
            jax.ShapeDtypeStruct((group,) + pack.shape, BF16),
        ),
        in_specs=[anyspace()] * 2 + [vmem()] * 4,
        out_specs=(vmem(),) + (anyspace(),) * 2,
        scratch_shapes=[
            pltpu.VMEM((groups - 1, PACK // groups, model), BF16),
            pltpu.VMEM((PACK, model), BF16),
            pltpu.VMEM((MEMK, model), BF16),
            pltpu.VMEM((width, block), BF16),
            pltpu.VMEM((block, 2 * width), BF16),
            pltpu.VMEM((block, model), BF16),
            pltpu.SemaphoreType.DMA((3,)),
            pltpu.SemaphoreType.DMA((moves,)),
            pltpu.SemaphoreType.DMA((moves,)),
            pltpu.SemaphoreType.DMA((groups - 1,)),
            pltpu.SemaphoreType.DMA((groups - 1,)),
            pltpu.SemaphoreType.DMA((groups - 1,)),
            pltpu.SemaphoreType.DMA((groups - 1,)),
            pltpu.SemaphoreType.DMA((CHUNKS,)),
            pltpu.SemaphoreType.DMA((CHUNKS,)),
            pltpu.SemaphoreType.DMA((3,)),
            pltpu.SemaphoreType.DMA((3,)),
            pltpu.SemaphoreType.DMA,
            pltpu.SemaphoreType.DMA,
        ],
        compiler_params=pltpu.CompilerParams(
            collective_id=1, has_side_effects=True, vmem_limit_bytes=VMEM_LIMIT
        ),
        name="tail",
    )(dq, dkv, pack, first, wqt, wp)


def near_partners(group, sides):
    base, me, side = group_place(group)
    found = []
    for u in range(sides):
        for t in range(group):
            if t or u:
                found.append((lax.rem(me + t, group), lax.rem(side + u, sides), u))
    return base, me, side, found


def mix_kernel(
    group, sides, groups, half,
    o_ref, mine_ref, mixed_ref, mem_ref, sum_ref,
    parts, memt, own, psend, precv, send, recv, msend, mrecv,
):
    base, me, side, found = near_partners(group, sides)
    number = base // group
    far = [
        (lax.rem(number + t, groups) * group + me, side) for t in range(1, groups)
    ]
    greet([(base + l, u) for l, u, apart in found] + far)
    for t in range(1, groups):
        remote(
            mine_ref, parts.at[t], psend.at[t - 1], precv.at[t - 1], far[t - 1]
        ).start()
    def rows(apart):
        slot = (sides - apart) % sides * group
        return pl.ds(pl.multiple_of((slot + me) * HEAD, HEAD), HEAD)

    copies = []
    for k, (l, u, apart) in enumerate(found):
        start = pl.multiple_of((l * sides + u) * half, half)
        copies.append(
            remote(
                o_ref.at[:, pl.ds(start, half)],
                mixed_ref.at[rows(apart), :],
                send.at[k],
                recv.at[k],
                (base + l, u),
            )
        )
    for copy in copies:
        copy.start()
    start = pl.multiple_of((me * sides + side) * half, half)
    mine = pltpu.make_async_copy(
        o_ref.at[:, pl.ds(start, half)], mixed_ref.at[rows(0), :], own.at[0]
    )
    mine.start()
    parts[0] = mine_ref[...]
    for t in range(1, groups):
        remote(
            mine_ref, parts.at[t], psend.at[t - 1], precv.at[t - 1], far[t - 1]
        ).wait()
    top = parts[0, VROWS : VROWS + 1, :]
    for t in range(1, groups):
        top = jnp.maximum(top, parts[t, VROWS : VROWS + 1, :])
    total = jnp.zeros((VROWS, MEMQ), F32)
    for t in range(groups):
        total = total + parts[t, 0:VROWS, :] * jnp.exp(parts[t, VROWS : VROWS + 1, :] - top)
    mass = total[HEAD : HEAD + 1, :]
    wide = total[0:HEAD, :] / mass
    sum_ref[0:HEAD, :] = wide
    sum_ref[HEAD : HEAD + 8, :] = jnp.broadcast_to(top + jnp.log(mass), (8, MEMQ))
    memt[...] = wide.astype(BF16)
    more = []
    for k, (l, u, apart) in enumerate(found):
        more.append(
            remote(memt, mem_ref.at[rows(apart), :], msend.at[k], mrecv.at[k], (base + l, u))
        )
    for copy in more:
        copy.start()
    last = pltpu.make_async_copy(memt, mem_ref.at[rows(0), :], own.at[1])
    last.start()
    mine.wait()
    last.wait()
    for copy in copies + more:
        copy.wait()


def mix(o, mine, group, sides, groups, half):
    near = group * sides - 1
    heads = group * sides
    return pl.pallas_call(
        functools.partial(mix_kernel, group, sides, groups, half),
        out_shape=(
            jax.ShapeDtypeStruct((heads * HEAD, half), BF16),
            jax.ShapeDtypeStruct((heads * HEAD, MEMQ), BF16),
            jax.ShapeDtypeStruct((HEAD + 8, MEMQ), F32),
        ),
        in_specs=[anyspace(), vmem()],
        out_specs=(anyspace(), anyspace(), vmem()),
        scratch_shapes=[
            pltpu.VMEM((groups, SROWS, MEMQ), F32),
            pltpu.VMEM((HEAD, MEMQ), BF16),
            pltpu.SemaphoreType.DMA((2,)),
            pltpu.SemaphoreType.DMA((groups - 1,)),
            pltpu.SemaphoreType.DMA((groups - 1,)),
            pltpu.SemaphoreType.DMA((near,)),
            pltpu.SemaphoreType.DMA((near,)),
            pltpu.SemaphoreType.DMA((near,)),
            pltpu.SemaphoreType.DMA((near,)),
        ],
        compiler_params=pltpu.CompilerParams(collective_id=2, has_side_effects=True),
        name="mix",
    )(o, mine)


def unmix_kernel(
    group, sides, half, back_ref, gown_ref, gpeer_ref,
    do_ref, total_ref, buffers, own, send, recv, csend, crecv,
):
    base, me, side, found = near_partners(group, sides)
    greet([(base + l, u) for l, u, apart in found])
    columns = pl.ds(pl.multiple_of((me * sides + side) * half, half), half)
    core = lax.rem(me, 2)
    beside = (base + core_partner(me), side)
    copies = []
    for k, (l, u, apart) in enumerate(found):
        head = pl.multiple_of((apart * group + l) * HEAD, HEAD)
        copies.append(
            remote(
                back_ref.at[pl.ds(head, HEAD), pl.ds(0, half)],
                do_ref.at[:, columns],
                send.at[k],
                recv.at[k],
                (base + l, u),
            )
        )
    sums = []
    for k, grad in enumerate((gown_ref, gpeer_ref)):
        sums.append(remote(grad.at[:, 1 - core], buffers.at[k], csend.at[k], crecv.at[k], beside))
    for copy in copies + sums:
        copy.start()
    head = pl.multiple_of(me * HEAD, HEAD)
    mine = pltpu.make_async_copy(
        back_ref.at[pl.ds(head, HEAD), pl.ds(0, half)], do_ref.at[:, columns], own
    )
    mine.start()
    for k, grad in enumerate((gown_ref, gpeer_ref)):
        sums[k].wait()
        for p in range(total_ref.shape[1]):
            total_ref[k, p] = (grad[p, core].astype(F32) + buffers[k, p].astype(F32)).astype(BF16)
    mine.wait()
    for copy in copies:
        copy.wait()


def unmix(back, gown, gpeer, group, sides, half):
    near = group * sides - 1
    chips, cores, size, width = gown.shape
    return pl.pallas_call(
        functools.partial(unmix_kernel, group, sides, half),
        out_shape=(
            jax.ShapeDtypeStruct((HEAD, group * sides * half), BF16),
            jax.ShapeDtypeStruct((2, chips, size, width), BF16),
        ),
        in_specs=[anyspace()] + [vmem()] * 2,
        out_specs=(anyspace(), vmem()),
        scratch_shapes=[
            pltpu.VMEM((2, chips, size, width), BF16),
            pltpu.SemaphoreType.DMA,
            pltpu.SemaphoreType.DMA((near,)),
            pltpu.SemaphoreType.DMA((near,)),
            pltpu.SemaphoreType.DMA((2,)),
            pltpu.SemaphoreType.DMA((2,)),
        ],
        compiler_params=pltpu.CompilerParams(
            collective_id=3, has_side_effects=True, vmem_limit_bytes=VMEM_LIMIT
        ),
        name="unmix",
    )(back, gown, gpeer)


def span_place(span):
    block = span // GROUP
    return lax.axis_size("ctx") * block, lax.axis_index("ctx") // GROUP * span


def doc_bounds(starts_ref, docs, first, last, total):
    low = starts_ref[0]
    low_end = total
    top = starts_ref[0]
    high = total
    for d in range(docs):
        start = starts_ref[d]
        low = jnp.where(start <= first, start, low)
        top = jnp.where(start <= last, start, top)
    for d in range(docs - 1, -1, -1):
        start = starts_ref[d]
        low_end = jnp.where(start > first, start, low_end)
        high = jnp.where(start > last, start, high)
    return low, low_end, top, high


def doc_rows(starts_ref, docs, first, total):
    place = first + lax.broadcasted_iota(jnp.int32, (1, TQ), 1)
    low = jnp.zeros((1, TQ), jnp.int32)
    high = jnp.full((1, TQ), total, jnp.int32)
    for d in range(docs):
        start = starts_ref[d]
        low = jnp.where(place >= start, start, low)
    for d in range(docs - 1, -1, -1):
        start = starts_ref[d]
        high = jnp.where(place < start, start, high)
    return low, high


def allowed_block(key_first, low, high):
    place = lax.broadcasted_iota(jnp.int32, (TK, TQ), 0) - (low - key_first)
    return place.astype(jnp.uint32) < (high - low).astype(jnp.uint32)


def tile(ref, number, size):
    return ref[pl.ds(pl.multiple_of(number * size, size), size), :]


def lanes(ref, number, size):
    return ref[:, pl.ds(pl.multiple_of(number * size, size), size)]


def pad_query(q, size):
    return jnp.concatenate([q, jnp.zeros((HEAD, size), BF16)], axis=0)


def fill_values(kv_ref, va, column, begin, end):
    def step(k, carry):
        turned = tile(kv_ref, k, TK).T
        at = pl.ds(pl.multiple_of(column + k * TK, TK), TK)
        va[0:HEAD, at] = turned[HEAD : 2 * HEAD, :]
        va[HEAD:VROWS, at] = jnp.ones((ONES, TK), BF16)
        return carry

    lax.fori_loop(begin, end, step, 0)


def key_range(bounds, kv_first, count):
    begin = jnp.clip(bounds[0] - kv_first, 0, count) // TK
    end = (jnp.clip(bounds[3] - kv_first, 0, count) + TK - 1) // TK
    return begin, end


def pair_loop(bounds, begin, end, kv_first, low, high, score, use):
    doc_first, doc_first_end, doc_last, doc_end = bounds
    single = doc_first == doc_last

    @pl.when(begin < end)
    def _():
        score(0, begin)

        def step(i, carry):
            k = begin + 2 * i
            at = kv_first + k * TK
            both = k + 1 < end
            whole = single & both & (at >= doc_first) & (at + 2 * TK <= doc_end)

            @pl.when(whole)
            def _():
                score(1, k + 1)
                use(0, k, None)
                score(0, k + 2)
                use(1, k + 1, None)

            @pl.when(jnp.logical_not(whole) & both)
            def _():
                score(1, k + 1)
                use(0, k, allowed_block(at, low, high))
                score(0, k + 2)
                use(1, k + 1, allowed_block(at + TK, low, high))

            @pl.when(jnp.logical_not(both))
            def _():
                use(0, k, allowed_block(at, low, high))

            return carry

        lax.fori_loop(0, (end - begin + 1) // 2, step, 0)


def online(score, value, acc, top):
    old = top[0:1, :]
    new = jnp.maximum(old, jnp.max(score, axis=0, keepdims=True))
    share = jnp.exp(score - new).astype(BF16)
    acc[...] = acc[...] * jnp.exp(old - new) + dot(value, share)
    top[...] = jnp.broadcast_to(new, top.shape)


def forward_tiles(bounds, low, high, kv_ref, kv_first, va, va_column, qz, acc, top, held):
    begin, end = key_range(bounds, kv_first, kv_ref.shape[0])

    def score(slot, k):
        held[slot][...] = dot(tile(kv_ref, jnp.minimum(k, end - 1), TK), qz)

    def use(slot, k, allowed):
        at = pl.ds(pl.multiple_of(va_column + k * TK, TK), TK)
        score = held[slot][...]
        if allowed is not None:
            score = jnp.where(allowed, score, MASKED)
        online(score, va[:, at], acc, top)

    pair_loop(bounds, begin, end, kv_first, low, high, score, use)


def forward_own_kernel(
    docs, span, memory_rows, meta_ref, q_ref, kv_ref, mq_ref, mkv_ref,
    state_ref, mstate_ref, va, acc, top, held0, held1,
):
    total, base = span_place(span)
    fill_values(kv_ref, va, 0, 0, span // TK)
    turned = mkv_ref[...].T
    mem_value = jnp.concatenate(
        [turned[HEAD : 2 * HEAD, 0:MEMK], jnp.ones((ONES, MEMK), BF16)], axis=0
    )
    score = dot(mkv_ref[0:MEMK, 0:HEAD], q_ref[...])
    inside = lax.broadcasted_iota(jnp.int32, score.shape, 0) < memory_rows
    score = jnp.where(inside, score, MASKED)
    new = jnp.max(score, axis=0, keepdims=True)
    state_ref[0:VROWS, :] = dot(mem_value, jnp.exp(score - new).astype(BF16))
    state_ref[VROWS:SROWS, :] = jnp.broadcast_to(new, (8, span))

    def query_step(qi, carry):
        first = base + qi * TQ
        bounds = doc_bounds(meta_ref, docs, first, first + TQ - 1, total)
        low, high = doc_rows(meta_ref, docs, first, total)
        at = pl.ds(pl.multiple_of(qi * TQ, TQ), TQ)
        qz = pad_query(q_ref[:, at], TQ)
        acc[...] = state_ref[0:VROWS, at]
        top[...] = state_ref[VROWS:SROWS, at]
        forward_tiles(bounds, low, high, kv_ref, base, va, 0, qz, acc, top, (held0, held1))
        state_ref[0:VROWS, at] = acc[...]
        state_ref[VROWS:SROWS, at] = top[...]
        return carry

    lax.fori_loop(0, span // TQ, query_step, 0)

    score = dot(kv_ref[...], pad_query(mq_ref[...], MEMQ))
    new = jnp.max(score, axis=0, keepdims=True)
    mstate_ref[0:VROWS, :] = dot(va[...], jnp.exp(score - new).astype(BF16))
    mstate_ref[VROWS:SROWS, :] = jnp.broadcast_to(new, (8, MEMQ))


def forward_own(meta, q, kv, mq, mkv, docs, memory_rows):
    count = kv.shape[0]
    return pl.pallas_call(
        functools.partial(forward_own_kernel, docs, count, memory_rows),
        out_shape=(
            jax.ShapeDtypeStruct((SROWS, count), F32),
            jax.ShapeDtypeStruct((SROWS, MEMQ), F32),
        ),
        in_specs=[smem()] + [vmem()] * 4,
        out_specs=(vmem(), vmem()),
        scratch_shapes=[
            pltpu.VMEM((VROWS, count), BF16),
            pltpu.VMEM((VROWS, TQ), F32),
            pltpu.VMEM((8, TQ), F32),
            pltpu.VMEM((TK, TQ), F32),
            pltpu.VMEM((TK, TQ), F32),
        ],
        compiler_params=pltpu.CompilerParams(vmem_limit_bytes=VMEM_LIMIT),
        cost_estimate=pl.CostEstimate(
            flops=8 * count * count * HEAD, bytes_accessed=4 << 20, transcendentals=count * count
        ),
        name="forward_own",
    )(meta, q, kv, mq, mkv)


def halo_ranges(meta_ref, docs, base, span, total):
    first = doc_bounds(meta_ref, docs, base, base + span - 1, total)
    before = jnp.clip(first[0] - (base - span), 0, span) // TK
    after = (jnp.clip(first[3] - (base + span), 0, span) + TK - 1) // TK
    return before, after


def forward_halo_kernel(
    docs, span, meta_ref, q_ref, before_ref, after_ref, state_ref, o_ref, wide_ref,
    va, acc, top, held0, held1,
):
    total, base = span_place(span)
    count = before_ref.shape[0]
    from_before, to_after = halo_ranges(meta_ref, docs, base, span, total)
    fill_values(before_ref, va, 0, from_before, span // TK)
    fill_values(after_ref, va, count, 0, to_after)
    held = (held0, held1)

    def query_step(qi, carry):
        first = base + qi * TQ
        bounds = doc_bounds(meta_ref, docs, first, first + TQ - 1, total)
        low, high = doc_rows(meta_ref, docs, first, total)
        at = pl.ds(pl.multiple_of(qi * TQ, TQ), TQ)
        qz = pad_query(q_ref[:, at], TQ)
        acc[...] = state_ref[0:VROWS, at]
        top[...] = state_ref[VROWS:SROWS, at]
        forward_tiles(bounds, low, high, before_ref, base - count, va, 0, qz, acc, top, held)
        forward_tiles(bounds, low, high, after_ref, base + count, va, count, qz, acc, top, held)
        mass = acc[HEAD : HEAD + 1, :]
        wide = acc[0:HEAD, :] / mass
        o_ref[:, at] = wide.astype(BF16)
        wide_ref[0:HEAD, at] = wide
        wide_ref[HEAD : HEAD + 8, at] = top[...] + jnp.log(jnp.broadcast_to(mass, top.shape))
        return carry

    lax.fori_loop(0, span // TQ, query_step, 0)


def forward_halo(meta, q, before, after, state, docs):
    count = before.shape[0]
    return pl.pallas_call(
        functools.partial(forward_halo_kernel, docs, count),
        out_shape=(
            jax.ShapeDtypeStruct((HEAD, count), BF16),
            jax.ShapeDtypeStruct((HEAD + 8, count), F32),
        ),
        in_specs=[smem()] + [vmem()] * 4,
        out_specs=(vmem(), vmem()),
        scratch_shapes=[
            pltpu.VMEM((VROWS, 2 * count), BF16),
            pltpu.VMEM((VROWS, TQ), F32),
            pltpu.VMEM((8, TQ), F32),
            pltpu.VMEM((TK, TQ), F32),
            pltpu.VMEM((TK, TQ), F32),
        ],
        compiler_params=pltpu.CompilerParams(vmem_limit_bytes=VMEM_LIMIT),
        cost_estimate=pl.CostEstimate(
            flops=4 * count * count * HEAD, bytes_accessed=6 << 20, transcendentals=count * count
        ),
        name="forward_halo",
    )(meta, q, before, after, state)


def backward_tiles(
    bounds, low, high, kv_ref, kv_first, kt, kt_column, grad, sides, stats, acc, held
):
    qz, doz, qr, dor = sides
    log_total, delta = stats
    begin, end = key_range(bounds, kv_first, kv_ref.shape[0])

    def score(slot, k):
        pair = tile(kv_ref, jnp.minimum(k, end - 1), TK)
        held[slot][...] = dot(pair, qz)
        held[slot + 2][...] = dot(pair, doz)

    def use(slot, k, allowed):
        at = pl.ds(pl.multiple_of(kt_column + k * TK, TK), TK)
        share = jnp.exp(held[slot][...] - log_total)
        if allowed is not None:
            share = jnp.where(allowed, share, 0.0)
        back = (share * (held[slot + 2][...] - delta)).astype(BF16)
        grad[at, :] += dot(back, qr) + dot(share.astype(BF16), dor)
        acc[...] += dot(kt[:, at], back)

    pair_loop(bounds, begin, end, kv_first, low, high, score, use)


def fill_keys(kv_ref, kt, column, begin, end):
    def step(k, carry):
        turned = tile(kv_ref, k, TK).T
        kt[:, pl.ds(pl.multiple_of(column + k * TK, TK), TK)] = turned[0:HEAD, :]
        return carry

    lax.fori_loop(begin, end, step, 0)


def query_sides(q, do, size):
    zero = jnp.zeros((HEAD, size), BF16)
    qz = jnp.concatenate([q, zero], axis=0)
    doz = jnp.concatenate([zero, do], axis=0)
    return qz, doz, qz.T, doz.T


def row_stats(wide, do):
    return wide[HEAD : HEAD + 1, :], jnp.sum(
        wide[0:HEAD, :] * do.astype(F32), axis=0, keepdims=True
    )


def backward_halo_kernel(
    docs, span, meta_ref, q_ref, do_ref, wide_ref, before_ref, after_ref,
    dq_ref, dbefore_ref, dafter_ref, kt, grad, acc, *held,
):
    total, base = span_place(span)
    count = before_ref.shape[0]
    from_before, to_after = halo_ranges(meta_ref, docs, base, span, total)
    fill_keys(before_ref, kt, 0, from_before, span // TK)
    fill_keys(after_ref, kt, count, 0, to_after)

    def clear(k, carry):
        grad[pl.ds(pl.multiple_of(k * TK, TK), TK), :] = jnp.zeros((TK, 2 * HEAD), F32)
        return carry

    lax.fori_loop(from_before, span // TK + to_after, clear, 0)

    def query_step(qi, carry):
        first = base + qi * TQ
        bounds = doc_bounds(meta_ref, docs, first, first + TQ - 1, total)
        low, high = doc_rows(meta_ref, docs, first, total)
        at = pl.ds(pl.multiple_of(qi * TQ, TQ), TQ)
        acc[...] = jnp.zeros_like(acc)

        @pl.when((bounds[0] < base) | (bounds[3] > base + count))
        def _():
            do = do_ref[:, at]
            sides = query_sides(q_ref[:, at], do, TQ)
            stats = row_stats(wide_ref[:, at], do)
            for ref, begin, column in (
                (before_ref, base - count, 0),
                (after_ref, base + count, count),
            ):
                backward_tiles(
                    bounds, low, high, ref, begin, kt, column, grad, sides, stats, acc, held
                )

        dq_ref[:, at] = acc[...]
        return carry

    lax.fori_loop(0, span // TQ, query_step, 0)
    dbefore_ref[...] = jnp.zeros_like(dbefore_ref)
    dafter_ref[...] = jnp.zeros_like(dafter_ref)

    def keep_before(k, carry):
        at = pl.ds(pl.multiple_of(k * TK, TK), TK)
        dbefore_ref[at, :] = grad[at, :].astype(BF16)
        return carry

    def keep_after(k, carry):
        at = pl.ds(pl.multiple_of(k * TK, TK), TK)
        dafter_ref[at, :] = grad[pl.ds(pl.multiple_of(count + k * TK, TK), TK), :].astype(BF16)
        return carry

    lax.fori_loop(from_before, span // TK, keep_before, 0)
    lax.fori_loop(0, to_after, keep_after, 0)


def backward_halo(meta, q, do, wide, before, after, docs):
    count = before.shape[0]
    return pl.pallas_call(
        functools.partial(backward_halo_kernel, docs, count),
        out_shape=(
            jax.ShapeDtypeStruct((HEAD, count), F32),
            jax.ShapeDtypeStruct((count, 2 * HEAD), BF16),
            jax.ShapeDtypeStruct((count, 2 * HEAD), BF16),
        ),
        in_specs=[smem()] + [vmem()] * 5,
        out_specs=(vmem(),) * 3,
        scratch_shapes=[
            pltpu.VMEM((HEAD, 2 * count), BF16),
            pltpu.VMEM((2 * count, 2 * HEAD), F32),
            pltpu.VMEM((HEAD, TQ), F32),
        ]
        + [pltpu.VMEM((TK, TQ), F32)] * 4,
        compiler_params=pltpu.CompilerParams(vmem_limit_bytes=VMEM_LIMIT),
        cost_estimate=pl.CostEstimate(
            flops=8 * count * count * HEAD, bytes_accessed=8 << 20, transcendentals=count * count
        ),
        name="backward_halo",
    )(meta, q, do, wide, before, after)


def backward_queries(
    docs, span, first_tile, last_tile, meta_ref, q_ref, do_ref, wide_ref, kv_ref,
    dq_ref, grad, kt, acc, delta_ref, wide_dq, held,
):
    total, base = span_place(span)
    scale = HEAD ** (-0.5)

    def query_step(qi, carry):
        first = base + qi * TQ
        bounds = doc_bounds(meta_ref, docs, first, first + TQ - 1, total)
        low, high = doc_rows(meta_ref, docs, first, total)
        at = pl.ds(pl.multiple_of(qi * TQ, TQ), TQ)
        sides = query_sides(q_ref[:, at], do_ref[:, at], TQ)
        stats = wide_ref[HEAD : HEAD + 1, at], delta_ref[0:1, at]
        acc[...] = wide_dq[:, at]
        backward_tiles(bounds, low, high, kv_ref, base, kt, 0, grad, sides, stats, acc, held)
        dq_ref[:, at] = (acc[...] * scale).astype(BF16)
        return carry

    lax.fori_loop(first_tile, last_tile, query_step, 0)


def backward_first_kernel(
    docs, span, memory_rows, meta_ref, q_ref, do_ref, wide_ref, kv_ref, part_ref,
    mq_ref, mdo_ref, mwide_ref, mkv_ref,
    dq_ref, grad, dmq_ref, mgrad, kt, delta_ref, wide_dq, acc, *held,
):
    fill_keys(kv_ref, kt, 0, 0, span // TK)
    scale = HEAD ** (-0.5)

    delta_ref[...] = jnp.broadcast_to(
        jnp.sum(wide_ref[0:HEAD, :] * do_ref[...].astype(F32), axis=0, keepdims=True), (8, span)
    )
    score = dot(mkv_ref[0:MEMK, 0:HEAD], q_ref[...])
    inside = lax.broadcasted_iota(jnp.int32, score.shape, 0) < memory_rows
    share = jnp.exp(jnp.where(inside, score, MASKED) - wide_ref[HEAD : HEAD + 1, :])
    slope = dot(mkv_ref[0:MEMK, HEAD : 2 * HEAD], do_ref[...])
    back = (share * (slope - delta_ref[0:1, :])).astype(BF16)
    mgrad[...] = jnp.zeros_like(mgrad)
    mgrad[0:MEMK, :] = jnp.concatenate(
        [dot_nt(back, q_ref[...]), dot_nt(share.astype(BF16), do_ref[...])], axis=1
    )
    mem_key = mkv_ref[...].T[0:HEAD, 0:MEMK]
    wide_dq[...] = part_ref[...] + dot(mem_key, back)

    me = lax.rem(lax.axis_index("ctx"), GROUP)
    mdo = mdo_ref[pl.ds(pl.multiple_of(me * HEAD, HEAD), HEAD), mdo_ref.shape[1] - MEMQ :]
    qz, doz, qr, dor = query_sides(mq_ref[...], mdo, MEMQ)
    log_total, delta = row_stats(mwide_ref[...], mdo)
    share = jnp.exp(dot(kv_ref[...], qz) - log_total)
    back = (share * (dot(kv_ref[...], doz) - delta)).astype(BF16)
    grad[...] = dot(back, qr) + dot(share.astype(BF16), dor)
    dmq_ref[...] = (dot(kt[...], back) * scale).astype(BF16)
    dq_ref[:, span // 2 :] = jnp.zeros((HEAD, span // 2), BF16)
    backward_queries(
        docs, span, 0, span // TQ // 2, meta_ref, q_ref, do_ref, wide_ref, kv_ref,
        dq_ref, grad, kt, acc, delta_ref, wide_dq, held,
    )


def backward_second_kernel(
    docs, span, meta_ref, q_ref, do_ref, wide_ref, kv_ref, kt, delta_ref, wide_dq, dq_in, grad_in,
    dq_ref, grad, acc, *held,
):
    dq_ref[...] = dq_in[...]
    grad[...] = grad_in[...]
    backward_queries(
        docs, span, span // TQ // 2, span // TQ, meta_ref, q_ref, do_ref, wide_ref, kv_ref,
        dq_ref, grad, kt, acc, delta_ref, wide_dq, held,
    )


def backward_first(meta, q, do, wide, kv, part, mq, mdo, mwide, mkv, docs, memory_rows):
    count = kv.shape[0]
    return pl.pallas_call(
        functools.partial(backward_first_kernel, docs, count, memory_rows),
        out_shape=(
            jax.ShapeDtypeStruct((HEAD, count), BF16),
            jax.ShapeDtypeStruct((count, 2 * HEAD), F32),
            jax.ShapeDtypeStruct((HEAD, MEMQ), BF16),
            jax.ShapeDtypeStruct((MEMQ, 2 * HEAD), F32),
            jax.ShapeDtypeStruct((HEAD, count), BF16),
            jax.ShapeDtypeStruct((8, count), F32),
            jax.ShapeDtypeStruct((HEAD, count), F32),
        ),
        in_specs=[smem()] + [vmem()] * 9,
        out_specs=(vmem(),) * 7,
        scratch_shapes=[pltpu.VMEM((HEAD, TQ), F32)] + [pltpu.VMEM((TK, TQ), F32)] * 4,
        compiler_params=pltpu.CompilerParams(vmem_limit_bytes=VMEM_LIMIT),
        cost_estimate=pl.CostEstimate(
            flops=8 * count * count * HEAD, bytes_accessed=8 << 20, transcendentals=count * count
        ),
        name="backward_first",
    )(meta, q, do, wide, kv, part, mq, mdo, mwide, mkv)


def backward_second(meta, q, do, wide, kv, kt, delta, wide_dq, dq, grad, docs):
    count = kv.shape[0]
    return pl.pallas_call(
        functools.partial(backward_second_kernel, docs, count),
        out_shape=(
            jax.ShapeDtypeStruct((HEAD, count), BF16),
            jax.ShapeDtypeStruct((count, 2 * HEAD), F32),
        ),
        in_specs=[smem()] + [vmem()] * 9,
        out_specs=(vmem(),) * 2,
        scratch_shapes=[pltpu.VMEM((HEAD, TQ), F32)] + [pltpu.VMEM((TK, TQ), F32)] * 4,
        compiler_params=pltpu.CompilerParams(vmem_limit_bytes=VMEM_LIMIT),
        cost_estimate=pl.CostEstimate(
            flops=8 * count * count * HEAD, bytes_accessed=8 << 20, transcendentals=count * count
        ),
        name="backward_second",
    )(meta, q, do, wide, kv, kt, delta, wide_dq, dq, grad)


def mean(value):
    return jnp.mean(value, axis=-1, keepdims=True)


def norm_parts(value):
    centered = value - mean(value)
    scale = lax.rsqrt(mean(centered * centered) + EPSILON)
    return centered * scale, scale


def norm_back(back, hat, scale):
    return scale * (back - mean(back) - hat * mean(back * hat))


def feed_kernel(
    half, tokens_ref, mem_ref, cot_ref, mcot_ref, mixed_ref, memt_ref,
    wo_a, wo_b, wu_a, wu_b, wd_a, wd_b, bo_ref, fg_ref, fb_ref, bd_ref, sg_ref, sb_ref, bu_a, bu_b,
    final_ref, mfinal_ref, back_ref, first_ref, gown_ref, gpeer_ref,
    acted_ref, slope_ref, hidden_ref, low_ref, lowt_ref, fed_ref, mup_ref,
    inner_0, inner_1, back_0, back_1,
):
    inner_refs, back_refs = (inner_0, inner_1), (back_0, back_1)
    side = lax.axis_index("wt")
    leader = ((lax.axis_index("ctx") == 0) & (side == 0)).astype(jnp.int32)
    mup_ref[...] = jnp.zeros_like(mup_ref)
    mup_ref[0 : mcot_ref.shape[0], :] = mcot_ref[...]
    model = tokens_ref.shape[1]
    rows = half + MEMQ
    mine = pl.ds(pl.multiple_of(side * half, half), half)
    hidden = wu_a.shape[1]
    chunk = 512
    place = lax.broadcasted_iota(jnp.int32, (rows, 1), 0)
    weight = jnp.where((place < half) | (leader == 1), 1.0, 0.0).astype(F32)
    b_output, first_gain, first_bias, b_down, second_gain, second_bias = (
        ref[...].astype(F32).reshape(1, model)
        for ref in (bo_ref, fg_ref, fb_ref, bd_ref, sg_ref, sb_ref)
    )
    mixed_t = jnp.concatenate([mixed_ref[...], memt_ref[...]], axis=1)
    mixed = mixed_t.T
    heads = wo_a.shape[0]
    attended = dot(mixed[:, 0:heads], wo_a[...]) + dot(mixed[:, heads : 2 * heads], wo_b[...])
    own = jnp.concatenate([tokens_ref[mine, :], mem_ref[...]], axis=0).astype(F32)
    first_hat, first_scale = norm_parts(own + attended + b_output)
    normed = first_hat * first_gain + first_bias
    low = normed.astype(BF16)
    low_ref[...] = low
    lowt_ref[...] = (low.astype(F32) * weight).astype(BF16).T
    hidden_ref[...] = normed + b_down
    root = 0.7978845608028654
    count = hidden // chunk
    parts = [
        (slice(k * chunk, (k + 1) * chunk), slice((part * count + k) * chunk, (part * count + k + 1) * chunk), part)
        for part in range(2)
        for k in range(count)
    ]
    ups, downs, up_biases, grads = (wu_a, wu_b), (wd_a, wd_b), (bu_a, bu_b), (gown_ref, gpeer_ref)

    def widen(k):
        at, to, part = parts[k]
        inner_refs[k % 2][...] = dot(low_ref[...], ups[part][:, at])

    widen(0)
    for k, (at, to, part) in enumerate(parts):
        if k + 1 < len(parts):
            widen(k + 1)
        inner = inner_refs[k % 2][...] + up_biases[part][0:1, at].astype(F32)
        square = inner * inner
        bent = jnp.tanh(inner * (root + (root * 0.044715) * square))
        grown = 0.5 + 0.5 * bent
        acted = (inner * grown).astype(BF16)
        acted_ref[:, to] = acted
        slope_ref[:, to] = grown + inner * (1.0 - bent * bent) * (
            0.5 * root + (0.5 * root * 0.134145) * square
        )
        hidden_ref[...] += dot(acted_ref[:, to], downs[part][at, :])
    second_hat, second_scale = norm_parts(hidden_ref[...])
    final = second_hat * second_gain + second_bias
    final_ref[...] = final[0:half].astype(BF16)
    mfinal_ref[...] = final[half:rows].astype(BF16)
    upstream = jnp.concatenate([cot_ref[mine, :], mup_ref[...]], axis=0).astype(F32)
    weighted = upstream * weight
    second_gain_grad = jnp.sum(second_hat * weighted, axis=0, keepdims=True)
    second_bias_grad = jnp.sum(weighted, axis=0, keepdims=True)
    second_back = norm_back(upstream * second_gain, second_hat, second_scale)
    fed = second_back.astype(BF16)
    fed_wide = fed.astype(F32) * weight
    down_bias_grad = jnp.sum(fed_wide, axis=0, keepdims=True)
    fed_ref[...] = fed
    fed_low = fed_wide.astype(BF16)
    hidden_ref[...] = second_back
    begin = 2 * hidden + wo_a.shape[0] + hidden // chunk
    zero = jnp.zeros((gown_ref.shape[0] - begin - 6, model), F32)

    def narrow(k):
        at, to, part = parts[k]
        inner_refs[k % 2][...] = dot_nt(fed_ref[...], downs[part][at, :])

    narrow(0)
    for k, (at, to, part) in enumerate(parts):
        if k + 1 < len(parts):
            narrow(k + 1)
        back = (inner_refs[k % 2][...] * slope_ref[:, to]).astype(BF16)
        back_refs[k % 2][...] = back
        row = 2 * hidden + heads + k % count
        grads[part][row : row + 1, :] = jnp.sum(
            back.astype(F32) * weight, axis=0, keepdims=True
        ).astype(BF16)
        grads[part][hidden + at.start : hidden + at.stop, :] = dot(
            acted_ref[:, to].T, fed_low
        ).astype(BF16)
        grads[part][at, :] = dot(lowt_ref[...], back_refs[k % 2][...]).astype(BF16)
        hidden_ref[...] += dot_nt(back_refs[k % 2][...], ups[part][:, at])
    normed_back = hidden_ref[...]
    weighted_back = normed_back * weight
    first_gain_grad = jnp.sum(first_hat * weighted_back, axis=0, keepdims=True)
    first_bias_grad = jnp.sum(weighted_back, axis=0, keepdims=True)
    first_back = norm_back(normed_back * first_gain, first_hat, first_scale)
    first_ref[...] = first_back
    attended_back = first_back.astype(BF16)
    attended_wide = attended_back.astype(F32) * weight
    output_bias_grad = jnp.sum(attended_wide, axis=0, keepdims=True)
    attended_low = attended_wide.astype(BF16)
    back_ref[0:heads, :] = dot_nt(wo_a[...], attended_back).astype(BF16)
    back_ref[heads : 2 * heads, :] = dot_nt(wo_b[...], attended_back).astype(BF16)
    out_grad = dot(mixed_t, attended_low).astype(BF16)
    small = jnp.concatenate(
        [
            output_bias_grad, first_gain_grad, first_bias_grad, down_bias_grad,
            second_gain_grad, second_bias_grad, zero,
        ],
        axis=0,
    ).astype(BF16)
    for part, grad_ref in enumerate((gown_ref, gpeer_ref)):
        grad_ref[2 * hidden : 2 * hidden + heads, :] = out_grad[part * heads : (part + 1) * heads, :]
        grad_ref[begin:, :] = small


def feed(tokens, mem, cot, mcot, mixed, memt, weights, vectors, bu_a, bu_b, half, grad_rows):
    model = tokens.shape[1]
    rows = half + MEMQ
    heads, hidden = weights[0].shape[0], weights[2].shape[1]
    grads = grad_rows
    return pl.pallas_call(
        functools.partial(feed_kernel, half),
        out_shape=(
            jax.ShapeDtypeStruct((half, model), BF16),
            jax.ShapeDtypeStruct((MEMQ, model), BF16),
            jax.ShapeDtypeStruct((2 * heads, rows), BF16),
            jax.ShapeDtypeStruct((rows, model), F32),
            jax.ShapeDtypeStruct((grads, model), BF16),
            jax.ShapeDtypeStruct((grads, model), BF16),
        ),
        in_specs=[vmem()] * 20,
        out_specs=(vmem(),) * 6,
        scratch_shapes=[
            pltpu.VMEM((rows, 2 * hidden), BF16),
            pltpu.VMEM((rows, 2 * hidden), F32),
            pltpu.VMEM((rows, model), F32),
            pltpu.VMEM((rows, model), BF16),
            pltpu.VMEM((model, rows), BF16),
            pltpu.VMEM((rows, model), BF16),
            pltpu.VMEM((MEMQ, model), BF16),
            pltpu.VMEM((rows, model), F32),
            pltpu.VMEM((rows, model), F32),
            pltpu.VMEM((rows, model), BF16),
            pltpu.VMEM((rows, model), BF16),
        ],
        compiler_params=pltpu.CompilerParams(vmem_limit_bytes=VMEM_LIMIT),
        cost_estimate=pl.CostEstimate(
            flops=12 * rows * model * 2 * hidden, bytes_accessed=16 << 20, transcendentals=rows * hidden
        ),
        name="feed",
    )(tokens, mem, cot, mcot, mixed, memt, *weights, *vectors, bu_a, bu_b)


def grads_kernel(
    dq_ref, dkv_ref, one_ref, two_ref, tokens_ref, dmq_ref, dmkv_ref, mem_ref, wqt_ref, wp_ref,
    low_ref, pack_ref, acc, bias,
):
    acc[...] = jnp.zeros_like(acc)
    bias[...] = jnp.zeros_like(bias)
    step_rows = 512

    def step(k, carry):
        at = pl.ds(pl.multiple_of(k * step_rows, step_rows), step_rows)
        low = (dkv_ref[at, :] + one_ref[at, :].astype(F32) + two_ref[at, :].astype(F32)).astype(BF16)
        low_ref[at, :] = low
        left = jnp.concatenate([dq_ref[:, at], low.T], axis=0)
        acc[...] += dot(left, tokens_ref[at, :])
        bias[...] += jnp.sum(left.astype(F32), axis=1, keepdims=True)
        return carry

    lax.fori_loop(0, dkv_ref.shape[0] // step_rows, step, 0)
    dmkv = dmkv_ref[...].astype(BF16)
    left = jnp.concatenate([dmq_ref[...], dmkv.T], axis=0)
    model = mem_ref.shape[1]
    me = lax.rem(lax.axis_index("ctx"), GROUP)
    pack_ref[0 : 3 * HEAD, :] = (acc[...] + dot(left, mem_ref[...])).astype(BF16)
    wq = wqt_ref[pl.ds(pl.multiple_of(me * HEAD, HEAD), HEAD), :]
    wp = wp_ref[:, pl.ds(pl.multiple_of(me * 2 * HEAD, 2 * HEAD), 2 * HEAD)]
    memory = dot(dmq_ref[...].T, wq) + dot_nt(dmkv, wp)
    pack_ref[3 * HEAD : 3 * HEAD + MEMK, :] = memory[0:MEMK, :].astype(BF16)
    columns = bias[...] + jnp.sum(left.astype(F32), axis=1, keepdims=True)
    rest = PACK - 3 * HEAD - MEMK
    turned = columns.T[0:rest, :]
    pack_ref[3 * HEAD + MEMK : PACK, :] = jnp.concatenate(
        [turned, jnp.zeros((rest, model - 3 * HEAD), F32)], axis=1
    ).astype(BF16)


def weight_grads(dq, dkv, one, two, tokens, dmq, dmkv, mem, wq, wp):
    count = dkv.shape[0]
    model = tokens.shape[1]
    return pl.pallas_call(
        grads_kernel,
        out_shape=(
            jax.ShapeDtypeStruct((count, 2 * HEAD), BF16),
            jax.ShapeDtypeStruct((PACK, model), BF16),
        ),
        in_specs=[vmem()] * 10,
        out_specs=(vmem(),) * 2,
        scratch_shapes=[
            pltpu.VMEM((3 * HEAD, model), F32),
            pltpu.VMEM((3 * HEAD, BIAS), F32),
        ],
        compiler_params=pltpu.CompilerParams(vmem_limit_bytes=VMEM_LIMIT),
        cost_estimate=pl.CostEstimate(
            flops=6 * HEAD * count * model, bytes_accessed=9 << 20, transcendentals=0
        ),
        name="weight_grads",
    )(dq, dkv, one, two, tokens, dmq, dmkv, mem, wq, wp)


def result_kernel(
    group, memory_rows, part_ref, other_ref, packs_ref, first_ref, sum_ref, final_ref, far_ref,
    out_token_ref, token_ref, memory_ref, query_ref, qbias_ref, key_ref, value_ref, vbias_ref,
    out_ref, up_ref, down_ref, upb_ref, small_ref,
):
    model = part_ref.shape[1]
    hidden, width = down_ref.shape[0], out_ref.shape[0]
    token_ref[...] = part_ref[...] + other_ref[...].astype(F32)
    side = lax.axis_index("wt")
    half = final_ref.shape[0]
    out_token_ref[pl.ds(pl.multiple_of(side * half, half), half), :] = final_ref[...]
    out_token_ref[pl.ds(pl.multiple_of((1 - side) * half, half), half), :] = far_ref[...]
    rows = slice(3 * HEAD, 3 * HEAD + MEMK)
    total = first_ref[first_ref.shape[0] - MEMQ : first_ref.shape[0] - MEMQ + MEMK, :]
    for h in range(group):
        total = total + packs_ref[h, rows, :].astype(F32)
    memory_ref[...] = total[0:memory_rows, :]
    for at, ref in ((0, query_ref), (HEAD, key_ref), (2 * HEAD, value_ref)):
        for h in range(0, group, 2):
            both = jnp.concatenate(
                [packs_ref[h, at : at + HEAD, :], packs_ref[h + 1, at : at + HEAD, :]], axis=0
            )
            ref[:, h * HEAD : (h + 2) * HEAD] = both.T.astype(F32)
    row = 3 * HEAD + MEMK
    for at, ref in ((0, qbias_ref), (2 * HEAD, vbias_ref)):
        ref[...] = jnp.concatenate(
            [packs_ref[h, row : row + 1, at : at + HEAD].astype(F32) for h in range(group)], axis=1
        )
    for k in range(hidden // model):
        up_ref[:, k * model : (k + 1) * model] = sum_ref[k * model : (k + 1) * model, :].astype(F32)
    down_ref[...] = sum_ref[hidden : 2 * hidden, :].astype(F32)
    begin = 2 * hidden + width
    out_ref[...] = sum_ref[2 * hidden : begin, :].astype(F32)
    chunks = hidden // model
    upb_ref[...] = jnp.concatenate(
        [sum_ref[begin + k : begin + k + 1, :].astype(F32) for k in range(chunks)], axis=1
    )
    small_ref[...] = sum_ref[begin : begin + 16, :].astype(F32)


def results(part, other, packs, first, total, final, far, group, memory_rows, hidden):
    block, model = part.shape
    width = group * HEAD
    shape = lambda *dims: jax.ShapeDtypeStruct(dims, F32)
    return pl.pallas_call(
        functools.partial(result_kernel, group, memory_rows),
        out_shape=(
            jax.ShapeDtypeStruct((block, model), BF16),
            shape(block, model), shape(memory_rows, model),
            shape(model, width), shape(1, width), shape(model, width), shape(model, width),
            shape(1, width), shape(width, model), shape(model, hidden), shape(hidden, model),
            shape(1, hidden), shape(16, model),
        ),
        in_specs=[vmem()] * 7,
        out_specs=(vmem(),) * 13,
        compiler_params=pltpu.CompilerParams(vmem_limit_bytes=VMEM_LIMIT),
        name="results",
    )(part, other, packs, first, total, final, far)


def local(
    tokens, memory, doc_starts, w_query, b_query, w_key, w_value, b_value, w_output, b_output,
    first_gain, first_bias, w_up, b_up, w_down, b_down, second_gain, second_bias,
    cotangent, mem_cotangent,
):
    block, model = tokens.shape
    memory_rows = memory.shape[0]
    docs = doc_starts.shape[0]
    width = w_query.shape[1]
    hidden = w_up.shape[1]
    group = width // HEAD
    ctx, sides = lax.axis_size("ctx"), lax.axis_size("wt")
    groups = ctx // group
    half = block // sides
    step = 16 * ctx
    grad_rows = (2 * hidden + width + hidden // model + 6 + step - 1) // step * step
    row = lambda a: a.reshape(1, a.shape[0])

    q, kv, out_b, up_b, bias_b, mq, mkv, mem_pad, w_pair, wq_t = scatter_heads(
        tokens, memory, w_query, row(b_query), w_key, w_value, row(b_value),
        w_output, w_up, b_up.reshape(8, hidden // 8), group,
    )
    forwards = [(i, i + group) for i in range(ctx - group)]
    backwards = [(i + group, i) for i in range(ctx - group)]
    swapped = [(i, (i + 1) % sides) for i in range(sides)]
    before = lax.ppermute(kv, "ctx", forwards)
    after = lax.ppermute(kv, "ctx", backwards)
    down_b = lax.ppermute(w_down, "wt", swapped)
    teams = [[g * group + l for l in range(group)] for g in range(groups)]
    late_tokens, kv = lax.optimization_barrier((tokens, kv))
    group_tokens = lax.all_gather(late_tokens, "ctx", axis_index_groups=teams, tiled=True)

    state, mstate = forward_own(doc_starts, q, kv, mq, mkv, docs, memory_rows)
    o, wide = forward_halo(doc_starts, q, before, after, state, docs)
    mixed_t, mem_t, mwide = mix(o, mstate, group, sides, groups, half)
    final, mfinal, back, first_back, gown, gpeer = feed(
        tokens, mem_pad, cotangent, mem_cotangent, mixed_t, mem_t,
        (w_output, out_b, w_up, up_b, w_down, down_b),
        [b_output, first_gain, first_bias, b_down, second_gain, second_bias],
        row(b_up), bias_b.reshape(1, hidden), half, grad_rows,
    )
    pieces = lambda g: g.reshape(ctx // 2, 2, grad_rows // ctx, model)
    do, total = unmix(back, pieces(gown), pieces(gpeer), group, sides, half)
    from_side = lax.ppermute(total[1], "wt", swapped)

    part, dbefore, dafter = backward_halo(doc_starts, q, do, wide, before, after, docs)
    from_side, dbefore, dafter, final_late = lax.optimization_barrier(
        (from_side, dbefore, dafter, final)
    )
    size = grad_rows // ctx
    total = (total[0].astype(F32) + from_side.astype(F32)).reshape(groups, 2, size, model)
    row_half = lax.rem(lax.axis_index("ctx"), group) // 2
    leaving = lax.dynamic_index_in_dim(total, 1 - row_half, 1, False).astype(BF16)
    staying = lax.dynamic_index_in_dim(total, row_half, 1, False).astype(BF16)
    crossed = [(i, i ^ 2) for i in range(ctx)]
    from_row = lax.ppermute(leaving, "ctx", crossed)
    from_after = lax.ppermute(dbefore, "ctx", backwards)
    from_before = lax.ppermute(dafter, "ctx", forwards)
    dq, dkv, dmq, dmkv, kt, delta, wide_dq = backward_first(
        doc_starts, q, do, wide, kv, part, mq, back, mwide, mkv, docs, memory_rows
    )
    from_row, from_after, from_before, dq, dkv = lax.optimization_barrier(
        (from_row, from_after, from_before, dq, dkv)
    )
    total = (staying.astype(F32) + from_row.astype(F32)).astype(BF16)
    columns = [[g * group + l for g in range(groups)] for l in range(group)]
    total = lax.all_to_all(total, "ctx", 0, 0, axis_index_groups=columns, tiled=True)
    far = lax.ppermute(lax.optimization_barrier((final_late, dq))[0], "wt", swapped)
    dq, dkv = backward_second(
        doc_starts, q, do, wide, kv, kt, delta, wide_dq, dq, dkv, docs
    )
    total, far, dq, dkv = lax.optimization_barrier((total, far, dq, dkv))
    piece = jnp.sum(total.astype(F32), axis=0).astype(BF16)
    total = lax.all_gather(piece, "ctx", tiled=True)
    dkv, pack = weight_grads(
        dq, dkv, from_after, from_before, group_tokens, dmq, dmkv, mem_pad, wq_t, w_pair
    )
    part, other, packs = tail(
        dq, dkv, pack, first_back, wq_t, w_pair, group, groups, sides, block
    )
    (
        token_out, token_grad, memory_grad, query_grad, query_bias, key_grad, value_grad, value_bias,
        out_grad, up_grad, down_grad, up_bias, small,
    ) = results(
        part, other, packs, first_back, total, final, far, group, memory_rows, hidden
    )
    chunks = hidden // model
    return (
        token_out, mfinal[:memory_rows], token_grad, memory_grad,
        query_grad, query_bias.reshape(width), key_grad, value_grad, value_bias.reshape(width),
        out_grad, small[chunks], small[chunks + 1], small[chunks + 2],
        up_grad, up_bias.reshape(hidden), down_grad,
        small[chunks + 3], small[chunks + 4], small[chunks + 5],
    )


def solution(mesh):
    placed = (
        P("ctx", None), P(), P(), P(None, "wt"), P("wt"), P(None, "wt"), P(None, "wt"), P("wt"),
        P("wt", None), P(), P(), P(), P(None, "wt"), P("wt"), P("wt", None), P(), P(), P(),
        P("ctx", None), P(),
    )
    return jax.shard_map(
        local,
        mesh=mesh,
        in_specs=placed,
        out_specs=(
            P("ctx", None), P(), P("ctx", None), P(), P(None, "wt"), P("wt"), P(None, "wt"),
            P(None, "wt"), P("wt"), P("wt", None), P(), P(), P(), P(None, "wt"), P("wt"),
            P("wt", None), P(), P(), P(),
        ),
        check_vma=False,
    )
```

```python
import functools

import jax
import jax.numpy as jnp
from jax import lax
from jax.experimental import pallas as pl
from jax.experimental.pallas import tpu as pltpu
from jax.sharding import PartitionSpec as P

HEAD = 64
EPSILON = 1e-05
MASKED = -1e30
MESH = pl.DeviceIdType.MESH
TQ = 512
TK = 512
MEMK = 32
MEMQ = 128
ONES = 16
VROWS = HEAD + ONES
SROWS = VROWS + 8
PACK = 256
BIAS = 128
CHUNKS = 4
AHEAD = 2
GROUP = 4
F32 = jnp.float32
BF16 = jnp.bfloat16
VMEM_LIMIT = 56 * 1024 * 1024


def vmem():
    return pl.BlockSpec(memory_space=pltpu.VMEM)


def smem():
    return pl.BlockSpec(memory_space=pltpu.SMEM)


def anyspace():
    return pl.BlockSpec(memory_space=pl.ANY)


def dot(a, b):
    return jnp.dot(a, b, preferred_element_type=F32)


def dot_nt(a, b):
    return lax.dot_general(a, b, (((1,), (1,)), ((), ())), preferred_element_type=F32)


def greet(partners):
    barrier = pltpu.get_barrier_semaphore()
    for partner in partners:
        pl.semaphore_signal(barrier, inc=1, device_id=partner, device_id_type=MESH)
    pl.semaphore_wait(barrier, len(partners))


def remote(src, dst, send, recv, device):
    return pltpu.make_async_remote_copy(
        src_ref=src, dst_ref=dst, send_sem=send, recv_sem=recv, device_id=device, device_id_type=MESH
    )


def group_place(group):
    here = lax.axis_index("ctx")
    return here // group * group, lax.rem(here, group), lax.axis_index("wt")


def core_partner(me):
    return me + 1 - 2 * lax.rem(me, 2)


def scatter_kernel(
    group, block, tokens_ref, memory_ref, wq_ref, bq_ref, wk_ref, wv_ref, bv_ref,
    wo_ref, wu_ref, bu_ref,
    qo_ref, kvo_ref, wo_other, wu_other, bu_other, mq_ref, mkv_ref, mem_ref, wp_ref, wqt_ref,
    qs, kvs, bpair, bcol, own, send, recv, wsend, wrecv, fsend, frecv,
):
    base, me, side = group_place(group)
    width = 2 * HEAD
    partners = [(base + lax.rem(me + t, group), side) for t in range(1, group)]
    across = (base + me, lax.rem(side + 1, lax.axis_size("wt")))
    beside = (base + core_partner(me), side)
    greet(partners + [across])
    core = lax.rem(me, 2)
    rows_o, rows_u = wo_ref.shape[0] // 2, wu_ref.shape[0] // 2

    def part(ref, rows, which):
        return ref.at[pl.ds(pl.multiple_of(which * rows, rows), rows), :]

    firsts = [
        remote(part(wo_ref, rows_o, core), part(wo_other, rows_o, core), wsend.at[0], wrecv.at[0], across),
        remote(part(wu_ref, rows_u, core), part(wu_other, rows_u, core), wsend.at[1], wrecv.at[1], across),
        remote(bu_ref, bu_other, wsend.at[2], wrecv.at[2], across),
    ]
    for copy in firsts:
        copy.start()

    bq = bq_ref[...].astype(F32).reshape(1, bq_ref.shape[0])
    bv = bv_ref[...].astype(F32).reshape(1, bv_ref.shape[0])
    none = jnp.zeros((1, HEAD), F32)
    for h in range(group):
        at = slice(h * HEAD, (h + 1) * HEAD)
        wp_ref[:, h * width : (h + 1) * width] = jnp.concatenate([wk_ref[:, at], wv_ref[:, at]], axis=1)
        bpair[:, h * width : (h + 1) * width] = jnp.concatenate([none, bv[:, at]], axis=1)
    wqt_ref[...] = wq_ref[...].T
    bcol[...] = jnp.broadcast_to(bq, (BIAS, bq.shape[1])).T
    mem_ref[...] = jnp.zeros_like(mem_ref)
    mem_ref[0 : memory_ref.shape[0], :] = memory_ref[...]
    scale = HEAD ** (-0.5)

    def project(rows_value, head):
        lanes_at = pl.ds(pl.multiple_of(head * width, width), width)
        rows_at = pl.ds(pl.multiple_of(head * HEAD, HEAD), HEAD)
        pair = (dot(rows_value, wp_ref[:, lanes_at]) + bpair[:, lanes_at]).astype(BF16)
        query = (dot_nt(wqt_ref[rows_at, :], rows_value) + bcol[rows_at, 0:1]).astype(BF16)
        return pair, query * jnp.asarray(scale, BF16)

    copies = []
    mine_rows = pl.ds(pl.multiple_of(me * block, block), block)
    for k, t in enumerate((2, 1, 3) if group == 4 else range(1, group)):
        peer = lax.rem(me + t, group)
        pair, query = project(tokens_ref[...], peer)
        kvs[t] = pair
        qs[t] = query
        device = (base + peer, side)
        copies.append(remote(kvs.at[t], kvo_ref.at[mine_rows, :], send.at[2 * k], recv.at[2 * t - 2], device))
        copies.append(remote(qs.at[t], qo_ref.at[:, mine_rows], send.at[2 * k + 1], recv.at[2 * t - 1], device))
        copies[-2].start()
        copies[-1].start()
    pair, query = project(tokens_ref[...], me)
    kvs[0] = pair
    qs[0] = query
    mine = [
        pltpu.make_async_copy(kvs.at[0], kvo_ref.at[mine_rows, :], own.at[0]),
        pltpu.make_async_copy(qs.at[0], qo_ref.at[:, mine_rows], own.at[1]),
    ]
    for copy in mine:
        copy.start()
    pair, query = project(mem_ref[...], me)
    mkv_ref[...] = pair
    mq_ref[...] = query
    for copy in firsts:
        copy.wait()
    forwards = [
        remote(part(wo_other, rows_o, core), part(wo_other, rows_o, core), fsend.at[0], frecv.at[0], beside),
        remote(part(wu_other, rows_u, core), part(wu_other, rows_u, core), fsend.at[1], frecv.at[1], beside),
    ]
    for copy in forwards:
        copy.start()
    for copy in mine + copies + forwards:
        copy.wait()


def scatter_heads(tokens, memory, wq, bq, wk, wv, bv, wo, wu, bu, group):
    block, model = tokens.shape
    width = wq.shape[1]
    like = lambda a: jax.ShapeDtypeStruct(a.shape, a.dtype)
    return pl.pallas_call(
        functools.partial(scatter_kernel, group, block),
        out_shape=(
            jax.ShapeDtypeStruct((HEAD, group * block), BF16),
            jax.ShapeDtypeStruct((group * block, 2 * HEAD), BF16),
            like(wo), like(wu), like(bu),
            jax.ShapeDtypeStruct((HEAD, MEMQ), BF16),
            jax.ShapeDtypeStruct((MEMQ, 2 * HEAD), BF16),
            jax.ShapeDtypeStruct((MEMQ, model), BF16),
            jax.ShapeDtypeStruct((model, 2 * width), BF16),
            jax.ShapeDtypeStruct((width, model), BF16),
        ),
        in_specs=[vmem()] * 7 + [anyspace()] * 3,
        out_specs=(anyspace(),) * 5 + (vmem(),) * 5,
        scratch_shapes=[
            pltpu.VMEM((group, HEAD, block), BF16),
            pltpu.VMEM((group, block, 2 * HEAD), BF16),
            pltpu.VMEM((1, 2 * width), F32),
            pltpu.VMEM((width, BIAS), F32),
            pltpu.SemaphoreType.DMA((2,)),
            pltpu.SemaphoreType.DMA((2 * group - 2,)),
            pltpu.SemaphoreType.DMA((2 * group - 2,)),
            pltpu.SemaphoreType.DMA((3,)),
            pltpu.SemaphoreType.DMA((3,)),
            pltpu.SemaphoreType.DMA((2,)),
            pltpu.SemaphoreType.DMA((2,)),
        ],
        compiler_params=pltpu.CompilerParams(
            collective_id=0, has_side_effects=True, vmem_limit_bytes=VMEM_LIMIT
        ),
        name="scatter_heads",
    )(tokens, memory, wq, bq, wk, wv, bv, wo, wu, bu)


def tail_kernel(
    group, groups, sides, block, dq_ref, wide_ref, one_ref, two_ref, tokens_ref, dmq_ref, dmkv_ref,
    mem_ref, first_ref, wqt_ref, wp_ref,
    part_ref, other_ref, packs_ref,
    dkv_ref, left_ref, pack_ref, parts, sums, mems, qrows, kvrows, low, own, send, recv, rsend, rrecv, gsend, grecv,
    xsend, xrecv, psend, precv, msend, mrecv,
):
    base, me, side = group_place(group)
    number = base // group
    width = 2 * HEAD
    across = (base + me, lax.rem(side + 1, sides))
    partners = [(base + lax.rem(me + t, group), side) for t in range(1, group)]
    far = [(lax.rem(number + t, groups) * group + me, side) for t in range(1, groups)]
    greet(partners + far + [across])
    rows = PACK // groups
    reduces = []
    for t in range(1, groups):
        peer = lax.rem(number + t, groups)
        at = pl.ds(pl.multiple_of(peer * rows, rows), rows)
        reduces.append(
            remote(pack_ref.at[at, :], parts.at[t - 1], rsend.at[t - 1], rrecv.at[t - 1], far[t - 1])
        )
    chunk = block // CHUNKS
    head_rows = pl.ds(pl.multiple_of(me * HEAD, HEAD), HEAD)
    head_lanes = pl.ds(pl.multiple_of(me * width, width), width)
    moves = []
    for r in range(CHUNKS):
        step = []
        for t in range(1, group):
            peer = lax.rem(me + t, group)
            at = pl.ds(pl.multiple_of(peer * block + r * chunk, chunk), chunk)
            here = pl.ds(r * chunk, chunk)
            slot = (r * (group - 1) + t - 1) * 2
            step.append(
                remote(dkv_ref.at[at, :], kvrows.at[here, head_lanes], send.at[slot], recv.at[slot], partners[t - 1])
            )
            step.append(
                remote(dq_ref.at[:, at], qrows.at[head_rows, here], send.at[slot + 1], recv.at[slot + 1], partners[t - 1])
            )
        moves.append(step)
    span = group * block

    def settle(k, carry):
        at = pl.ds(pl.multiple_of(k * block, block), block)
        dkv_ref[at, :] = (
            wide_ref[at, :] + one_ref[at, :].astype(F32) + two_ref[at, :].astype(F32)
        ).astype(BF16)
        return carry

    lax.fori_loop(0, group, settle, 0)
    for step in moves[:AHEAD]:
        for copy in step:
            copy.start()
    at = pl.ds(pl.multiple_of(me * block, block), block)
    mine = [
        pltpu.make_async_copy(dkv_ref.at[at, :], kvrows.at[:, head_lanes], own.at[0]),
        pltpu.make_async_copy(dq_ref.at[:, at], qrows.at[head_rows, :], own.at[1]),
    ]
    for copy in mine:
        copy.start()
    left_ref[0:HEAD, :] = dq_ref[...]
    for k in range(span // 512):
        at = slice(k * 512, (k + 1) * 512)
        left_ref[HEAD : 3 * HEAD, at] = dkv_ref[at, :].T
    dmkv = dmkv_ref[...].astype(BF16)
    left = jnp.concatenate([dmq_ref[...], dmkv.T], axis=0)
    model = mem_ref.shape[1]
    pack_ref[0 : 3 * HEAD, :] = (
        dot(left_ref[...], tokens_ref[...]) + dot(left, mem_ref[...])
    ).astype(BF16)
    columns = dot(left_ref[...], jnp.ones((span, BIAS), BF16)) + jnp.sum(
        left.astype(F32), axis=1, keepdims=True
    )
    wq = wqt_ref[pl.ds(pl.multiple_of(me * HEAD, HEAD), HEAD), :]
    wp = wp_ref[:, pl.ds(pl.multiple_of(me * width, width), width)]
    memory_part = dot(dmq_ref[...].T, wq) + dot_nt(dmkv, wp)
    pack_ref[3 * HEAD : 3 * HEAD + MEMK, :] = memory_part[0:MEMK, :].astype(BF16)
    rest = PACK - 3 * HEAD - MEMK
    turned = columns.T[0:rest, :]
    pack_ref[3 * HEAD + MEMK : PACK, :] = jnp.concatenate(
        [turned, jnp.zeros((rest, model - 3 * HEAD), F32)], axis=1
    ).astype(BF16)
    for copy in reduces:
        copy.start()
    mine[0].wait()
    mine[1].wait()
    swaps, spread = [], []
    half = block // sides
    memory = pl.ds(3 * HEAD, MEMK)
    here = pl.ds(pl.multiple_of(number * rows, rows), rows)

    def reduced():
        total = pack_ref[here, :].astype(F32)
        for t in range(1, groups):
            reduces[t - 1].wait()
            total = total + parts[t - 1].astype(F32)
        sums[here, :] = total.astype(BF16)
        for t in range(1, groups):
            spread.append(
                remote(sums.at[here, :], sums.at[here, :], gsend.at[t - 1], grecv.at[t - 1], far[t - 1])
            )
            spread[-1].start()

    exchange = remote(sums.at[memory, :], mems, msend, mrecv, across)
    beside = (base + core_partner(me), side)
    opposite = lax.rem(me + 2, group)
    first = [
        remote(sums, packs_ref.at[me], psend.at[0], precv.at[0], (base + opposite, side)),
        remote(sums, packs_ref.at[me], psend.at[1], precv.at[1], beside),
    ]
    last = pltpu.make_async_copy(sums, packs_ref.at[me], own.at[2])
    second = remote(packs_ref.at[opposite], packs_ref.at[opposite], psend.at[2], precv.at[2], beside)
    for r in range(CHUNKS):
        for copy in moves[r]:
            copy.wait()
        if r + AHEAD < CHUNKS:
            for copy in moves[r + AHEAD]:
                copy.start()
        at = pl.ds(r * chunk, chunk)
        value = dot(qrows[:, at].T, wqt_ref[...]) + dot_nt(kvrows[at, :], wp_ref[...])
        inside = (r * chunk) // half
        extra = first_ref[pl.ds(r * chunk - inside * half, chunk), :]
        value = value + extra * (side == inside).astype(F32)
        part_ref[at, :] = value
        low[at, :] = value.astype(BF16)
        swaps.append(remote(low.at[at, :], other_ref.at[at, :], xsend.at[r], xrecv.at[r], across))
        swaps[-1].start()
        if r == 0:
            reduced()
        if r == 1:
            for copy in spread:
                copy.wait()
            exchange.start()
        if r == CHUNKS - 1:
            exchange.wait()
            sums[memory, :] = (sums[memory, :].astype(F32) + mems[...].astype(F32)).astype(BF16)
            for copy in first:
                copy.start()
            last.start()
    first[0].wait()
    second.start()
    last.wait()
    first[1].wait()
    second.wait()
    for copy in swaps:
        copy.wait()


def tail(dq, dkv, one, two, tokens, dmq, dmkv, mem, first, wqt, wp, group, groups, sides, block):
    model = first.shape[1]
    width = wqt.shape[0]
    moves = CHUNKS * (group - 1) * 2
    return pl.pallas_call(
        functools.partial(tail_kernel, group, groups, sides, block),
        out_shape=(
            jax.ShapeDtypeStruct((block, model), F32),
            jax.ShapeDtypeStruct((block, model), BF16),
            jax.ShapeDtypeStruct((group, PACK, model), BF16),
        ),
        in_specs=[vmem()] * 11,
        out_specs=(vmem(),) + (anyspace(),) * 2,
        scratch_shapes=[
            pltpu.VMEM((group * block, 2 * HEAD), BF16),
            pltpu.VMEM((3 * HEAD, group * block), BF16),
            pltpu.VMEM((PACK, model), BF16),
            pltpu.VMEM((groups - 1, PACK // groups, model), BF16),
            pltpu.VMEM((PACK, model), BF16),
            pltpu.VMEM((MEMK, model), BF16),
            pltpu.VMEM((width, block), BF16),
            pltpu.VMEM((block, 2 * width), BF16),
            pltpu.VMEM((block, model), BF16),
            pltpu.SemaphoreType.DMA((3,)),
            pltpu.SemaphoreType.DMA((moves,)),
            pltpu.SemaphoreType.DMA((moves,)),
            pltpu.SemaphoreType.DMA((groups - 1,)),
            pltpu.SemaphoreType.DMA((groups - 1,)),
            pltpu.SemaphoreType.DMA((groups - 1,)),
            pltpu.SemaphoreType.DMA((groups - 1,)),
            pltpu.SemaphoreType.DMA((CHUNKS,)),
            pltpu.SemaphoreType.DMA((CHUNKS,)),
            pltpu.SemaphoreType.DMA((3,)),
            pltpu.SemaphoreType.DMA((3,)),
            pltpu.SemaphoreType.DMA,
            pltpu.SemaphoreType.DMA,
        ],
        compiler_params=pltpu.CompilerParams(
            collective_id=1, has_side_effects=True, vmem_limit_bytes=VMEM_LIMIT
        ),
        name="tail",
    )(dq, dkv, one, two, tokens, dmq, dmkv, mem, first, wqt, wp)


def near_partners(group, sides):
    base, me, side = group_place(group)
    found = []
    for u in range(sides):
        for t in range(group):
            if t or u:
                found.append((lax.rem(me + t, group), lax.rem(side + u, sides), u))
    return base, me, side, found


def span_place(span):
    block = span // GROUP
    return lax.axis_size("ctx") * block, lax.axis_index("ctx") // GROUP * span


def doc_bounds(starts_ref, docs, first, last, total):
    low = starts_ref[0]
    low_end = total
    top = starts_ref[0]
    high = total
    for d in range(docs):
        start = starts_ref[d]
        low = jnp.where(start <= first, start, low)
        top = jnp.where(start <= last, start, top)
    for d in range(docs - 1, -1, -1):
        start = starts_ref[d]
        low_end = jnp.where(start > first, start, low_end)
        high = jnp.where(start > last, start, high)
    return low, low_end, top, high


def doc_rows(starts_ref, docs, first, total):
    place = first + lax.broadcasted_iota(jnp.int32, (1, TQ), 1)
    low = jnp.zeros((1, TQ), jnp.int32)
    high = jnp.full((1, TQ), total, jnp.int32)
    for d in range(docs):
        start = starts_ref[d]
        low = jnp.where(place >= start, start, low)
    for d in range(docs - 1, -1, -1):
        start = starts_ref[d]
        high = jnp.where(place < start, start, high)
    return low, high


def allowed_block(key_first, low, high):
    place = lax.broadcasted_iota(jnp.int32, (TK, TQ), 0) - (low - key_first)
    return place.astype(jnp.uint32) < (high - low).astype(jnp.uint32)


def tile(ref, number, size):
    return ref[pl.ds(pl.multiple_of(number * size, size), size), :]


def lanes(ref, number, size):
    return ref[:, pl.ds(pl.multiple_of(number * size, size), size)]


def pad_query(q, size):
    return jnp.concatenate([q, jnp.zeros((HEAD, size), BF16)], axis=0)


def fill_values(kv_ref, va, column, begin, end):
    def step(k, carry):
        turned = tile(kv_ref, k, TK).T
        at = pl.ds(pl.multiple_of(column + k * TK, TK), TK)
        va[0:HEAD, at] = turned[HEAD : 2 * HEAD, :]
        va[HEAD:VROWS, at] = jnp.ones((ONES, TK), BF16)
        return carry

    lax.fori_loop(begin, end, step, 0)


def key_range(bounds, kv_first, count):
    begin = jnp.clip(bounds[0] - kv_first, 0, count) // TK
    end = (jnp.clip(bounds[3] - kv_first, 0, count) + TK - 1) // TK
    return begin, end


def pair_loop(bounds, begin, end, kv_first, low, high, score, use):
    doc_first, doc_first_end, doc_last, doc_end = bounds
    single = doc_first == doc_last

    @pl.when(begin < end)
    def _():
        score(0, begin)

        def step(i, carry):
            k = begin + 2 * i
            at = kv_first + k * TK
            both = k + 1 < end
            whole = single & both & (at >= doc_first) & (at + 2 * TK <= doc_end)

            @pl.when(whole)
            def _():
                score(1, k + 1)
                use(0, k, None)
                score(0, k + 2)
                use(1, k + 1, None)

            @pl.when(jnp.logical_not(whole) & both)
            def _():
                score(1, k + 1)
                use(0, k, allowed_block(at, low, high))
                score(0, k + 2)
                use(1, k + 1, allowed_block(at + TK, low, high))

            @pl.when(jnp.logical_not(both))
            def _():
                use(0, k, allowed_block(at, low, high))

            return carry

        lax.fori_loop(0, (end - begin + 1) // 2, step, 0)


def online(score, value, acc, top):
    old = top[0:1, :]
    new = jnp.maximum(old, jnp.max(score, axis=0, keepdims=True))
    share = jnp.exp(score - new).astype(BF16)
    acc[...] = acc[...] * jnp.exp(old - new) + dot(value, share)
    top[...] = jnp.broadcast_to(new, top.shape)


def forward_tiles(bounds, low, high, kv_ref, kv_first, va, va_column, qz, acc, top, held):
    begin, end = key_range(bounds, kv_first, kv_ref.shape[0])

    def score(slot, k):
        held[slot][...] = dot(tile(kv_ref, jnp.minimum(k, end - 1), TK), qz)

    def use(slot, k, allowed):
        at = pl.ds(pl.multiple_of(va_column + k * TK, TK), TK)
        score = held[slot][...]
        if allowed is not None:
            score = jnp.where(allowed, score, MASKED)
        online(score, va[:, at], acc, top)

    pair_loop(bounds, begin, end, kv_first, low, high, score, use)


def forward_own_kernel(
    docs, span, memory_rows, meta_ref, q_ref, kv_ref, mq_ref, mkv_ref,
    state_ref, mstate_ref, va, acc, top, held0, held1,
):
    total, base = span_place(span)
    fill_values(kv_ref, va, 0, 0, span // TK)
    turned = mkv_ref[...].T
    mem_value = jnp.concatenate(
        [turned[HEAD : 2 * HEAD, 0:MEMK], jnp.ones((ONES, MEMK), BF16)], axis=0
    )
    score = dot(mkv_ref[0:MEMK, 0:HEAD], q_ref[...])
    inside = lax.broadcasted_iota(jnp.int32, score.shape, 0) < memory_rows
    score = jnp.where(inside, score, MASKED)
    new = jnp.max(score, axis=0, keepdims=True)
    state_ref[0:VROWS, :] = dot(mem_value, jnp.exp(score - new).astype(BF16))
    state_ref[VROWS:SROWS, :] = jnp.broadcast_to(new, (8, span))

    def query_step(qi, carry):
        first = base + qi * TQ
        bounds = doc_bounds(meta_ref, docs, first, first + TQ - 1, total)
        low, high = doc_rows(meta_ref, docs, first, total)
        at = pl.ds(pl.multiple_of(qi * TQ, TQ), TQ)
        qz = pad_query(q_ref[:, at], TQ)
        acc[...] = state_ref[0:VROWS, at]
        top[...] = state_ref[VROWS:SROWS, at]
        forward_tiles(bounds, low, high, kv_ref, base, va, 0, qz, acc, top, (held0, held1))
        state_ref[0:VROWS, at] = acc[...]
        state_ref[VROWS:SROWS, at] = top[...]
        return carry

    lax.fori_loop(0, span // TQ, query_step, 0)

    score = dot(kv_ref[...], pad_query(mq_ref[...], MEMQ))
    new = jnp.max(score, axis=0, keepdims=True)
    mstate_ref[0:VROWS, :] = dot(va[...], jnp.exp(score - new).astype(BF16))
    mstate_ref[VROWS:SROWS, :] = jnp.broadcast_to(new, (8, MEMQ))


def forward_own(meta, q, kv, mq, mkv, docs, memory_rows):
    count = kv.shape[0]
    return pl.pallas_call(
        functools.partial(forward_own_kernel, docs, count, memory_rows),
        out_shape=(
            jax.ShapeDtypeStruct((SROWS, count), F32),
            jax.ShapeDtypeStruct((SROWS, MEMQ), F32),
        ),
        in_specs=[smem()] + [vmem()] * 4,
        out_specs=(vmem(), vmem()),
        scratch_shapes=[
            pltpu.VMEM((VROWS, count), BF16),
            pltpu.VMEM((VROWS, TQ), F32),
            pltpu.VMEM((8, TQ), F32),
            pltpu.VMEM((TK, TQ), F32),
            pltpu.VMEM((TK, TQ), F32),
        ],
        compiler_params=pltpu.CompilerParams(vmem_limit_bytes=VMEM_LIMIT),
        cost_estimate=pl.CostEstimate(
            flops=8 * count * count * HEAD, bytes_accessed=4 << 20, transcendentals=count * count
        ),
        name="forward_own",
    )(meta, q, kv, mq, mkv)


def halo_ranges(meta_ref, docs, base, span, total):
    first = doc_bounds(meta_ref, docs, base, base + span - 1, total)
    before = jnp.clip(first[0] - (base - span), 0, span) // TK
    after = (jnp.clip(first[3] - (base + span), 0, span) + TK - 1) // TK
    return before, after


def forward_halo_kernel(
    docs, span, meta_ref, q_ref, before_ref, after_ref, state_ref, o_ref, wide_ref,
    va, acc, top, held0, held1,
):
    total, base = span_place(span)
    count = before_ref.shape[0]
    from_before, to_after = halo_ranges(meta_ref, docs, base, span, total)
    fill_values(before_ref, va, 0, from_before, span // TK)
    fill_values(after_ref, va, count, 0, to_after)
    held = (held0, held1)

    def query_step(qi, carry):
        first = base + qi * TQ
        bounds = doc_bounds(meta_ref, docs, first, first + TQ - 1, total)
        low, high = doc_rows(meta_ref, docs, first, total)
        at = pl.ds(pl.multiple_of(qi * TQ, TQ), TQ)
        qz = pad_query(q_ref[:, at], TQ)
        acc[...] = state_ref[0:VROWS, at]
        top[...] = state_ref[VROWS:SROWS, at]
        forward_tiles(bounds, low, high, before_ref, base - count, va, 0, qz, acc, top, held)
        forward_tiles(bounds, low, high, after_ref, base + count, va, count, qz, acc, top, held)
        mass = acc[HEAD : HEAD + 1, :]
        wide = acc[0:HEAD, :] / mass
        o_ref[:, at] = wide.astype(BF16)
        wide_ref[0:HEAD, at] = wide
        wide_ref[HEAD : HEAD + 8, at] = top[...] + jnp.log(jnp.broadcast_to(mass, top.shape))
        return carry

    lax.fori_loop(0, span // TQ, query_step, 0)


def forward_halo(meta, q, before, after, state, docs):
    count = before.shape[0]
    return pl.pallas_call(
        functools.partial(forward_halo_kernel, docs, count),
        out_shape=(
            jax.ShapeDtypeStruct((HEAD, count), BF16),
            jax.ShapeDtypeStruct((HEAD + 8, count), F32),
        ),
        in_specs=[smem()] + [vmem()] * 4,
        out_specs=(vmem(), vmem()),
        scratch_shapes=[
            pltpu.VMEM((VROWS, 2 * count), BF16),
            pltpu.VMEM((VROWS, TQ), F32),
            pltpu.VMEM((8, TQ), F32),
            pltpu.VMEM((TK, TQ), F32),
            pltpu.VMEM((TK, TQ), F32),
        ],
        compiler_params=pltpu.CompilerParams(vmem_limit_bytes=VMEM_LIMIT),
        cost_estimate=pl.CostEstimate(
            flops=4 * count * count * HEAD, bytes_accessed=6 << 20, transcendentals=count * count
        ),
        name="forward_halo",
    )(meta, q, before, after, state)


def backward_tiles(
    bounds, low, high, kv_ref, kv_first, kt, kt_column, grad, sides, stats, acc, held
):
    qz, doz, qr, dor = sides
    log_total, delta = stats
    begin, end = key_range(bounds, kv_first, kv_ref.shape[0])

    def score(slot, k):
        pair = tile(kv_ref, jnp.minimum(k, end - 1), TK)
        held[slot][...] = dot(pair, qz)
        held[slot + 2][...] = dot(pair, doz)

    def use(slot, k, allowed):
        at = pl.ds(pl.multiple_of(kt_column + k * TK, TK), TK)
        share = jnp.exp(held[slot][...] - log_total)
        if allowed is not None:
            share = jnp.where(allowed, share, 0.0)
        back = (share * (held[slot + 2][...] - delta)).astype(BF16)
        grad[at, :] += dot(back, qr) + dot(share.astype(BF16), dor)
        acc[...] += dot(kt[:, at], back)

    pair_loop(bounds, begin, end, kv_first, low, high, score, use)


def fill_keys(kv_ref, kt, column, begin, end):
    def step(k, carry):
        turned = tile(kv_ref, k, TK).T
        kt[:, pl.ds(pl.multiple_of(column + k * TK, TK), TK)] = turned[0:HEAD, :]
        return carry

    lax.fori_loop(begin, end, step, 0)


def query_sides(q, do, size):
    zero = jnp.zeros((HEAD, size), BF16)
    qz = jnp.concatenate([q, zero], axis=0)
    doz = jnp.concatenate([zero, do], axis=0)
    return qz, doz, qz.T, doz.T


def row_stats(wide, do):
    return wide[HEAD : HEAD + 1, :], jnp.sum(
        wide[0:HEAD, :] * do.astype(F32), axis=0, keepdims=True
    )


def backward_halo_kernel(
    docs, span, meta_ref, q_ref, do_ref, wide_ref, before_ref, after_ref,
    dq_ref, dbefore_ref, dafter_ref, kt, grad, acc, *held,
):
    total, base = span_place(span)
    count = before_ref.shape[0]
    from_before, to_after = halo_ranges(meta_ref, docs, base, span, total)
    fill_keys(before_ref, kt, 0, from_before, span // TK)
    fill_keys(after_ref, kt, count, 0, to_after)

    def clear(k, carry):
        grad[pl.ds(pl.multiple_of(k * TK, TK), TK), :] = jnp.zeros((TK, 2 * HEAD), F32)
        return carry

    lax.fori_loop(from_before, span // TK + to_after, clear, 0)

    def query_step(qi, carry):
        first = base + qi * TQ
        bounds = doc_bounds(meta_ref, docs, first, first + TQ - 1, total)
        low, high = doc_rows(meta_ref, docs, first, total)
        at = pl.ds(pl.multiple_of(qi * TQ, TQ), TQ)
        acc[...] = jnp.zeros_like(acc)

        @pl.when((bounds[0] < base) | (bounds[3] > base + count))
        def _():
            do = do_ref[:, at]
            sides = query_sides(q_ref[:, at], do, TQ)
            stats = row_stats(wide_ref[:, at], do)
            for ref, begin, column in (
                (before_ref, base - count, 0),
                (after_ref, base + count, count),
            ):
                backward_tiles(
                    bounds, low, high, ref, begin, kt, column, grad, sides, stats, acc, held
                )

        dq_ref[:, at] = acc[...]
        return carry

    lax.fori_loop(0, span // TQ, query_step, 0)
    dbefore_ref[...] = jnp.zeros_like(dbefore_ref)
    dafter_ref[...] = jnp.zeros_like(dafter_ref)

    def keep_before(k, carry):
        at = pl.ds(pl.multiple_of(k * TK, TK), TK)
        dbefore_ref[at, :] = grad[at, :].astype(BF16)
        return carry

    def keep_after(k, carry):
        at = pl.ds(pl.multiple_of(k * TK, TK), TK)
        dafter_ref[at, :] = grad[pl.ds(pl.multiple_of(count + k * TK, TK), TK), :].astype(BF16)
        return carry

    lax.fori_loop(from_before, span // TK, keep_before, 0)
    lax.fori_loop(0, to_after, keep_after, 0)


def backward_halo(meta, q, do, wide, before, after, docs):
    count = before.shape[0]
    return pl.pallas_call(
        functools.partial(backward_halo_kernel, docs, count),
        out_shape=(
            jax.ShapeDtypeStruct((HEAD, count), F32),
            jax.ShapeDtypeStruct((count, 2 * HEAD), BF16),
            jax.ShapeDtypeStruct((count, 2 * HEAD), BF16),
        ),
        in_specs=[smem()] + [vmem()] * 5,
        out_specs=(vmem(),) * 3,
        scratch_shapes=[
            pltpu.VMEM((HEAD, 2 * count), BF16),
            pltpu.VMEM((2 * count, 2 * HEAD), F32),
            pltpu.VMEM((HEAD, TQ), F32),
        ]
        + [pltpu.VMEM((TK, TQ), F32)] * 4,
        compiler_params=pltpu.CompilerParams(vmem_limit_bytes=VMEM_LIMIT),
        cost_estimate=pl.CostEstimate(
            flops=8 * count * count * HEAD, bytes_accessed=8 << 20, transcendentals=count * count
        ),
        name="backward_halo",
    )(meta, q, do, wide, before, after)


def backward_queries(
    docs, span, first_tile, last_tile, meta_ref, q_ref, do_ref, wide_ref, kv_ref,
    dq_ref, grad, kt, acc, delta_ref, wide_dq, held,
):
    total, base = span_place(span)
    scale = HEAD ** (-0.5)

    def query_step(qi, carry):
        first = base + qi * TQ
        bounds = doc_bounds(meta_ref, docs, first, first + TQ - 1, total)
        low, high = doc_rows(meta_ref, docs, first, total)
        at = pl.ds(pl.multiple_of(qi * TQ, TQ), TQ)
        sides = query_sides(q_ref[:, at], do_ref[:, at], TQ)
        stats = wide_ref[HEAD : HEAD + 1, at], delta_ref[0:1, at]
        acc[...] = wide_dq[:, at]
        backward_tiles(bounds, low, high, kv_ref, base, kt, 0, grad, sides, stats, acc, held)
        dq_ref[:, at] = (acc[...] * scale).astype(BF16)
        return carry

    lax.fori_loop(first_tile, last_tile, query_step, 0)


def backward_first_kernel(
    docs, span, memory_rows, meta_ref, q_ref, do_ref, wide_ref, kv_ref, part_ref,
    mq_ref, mdo_ref, mwide_ref, mkv_ref,
    dq_ref, grad, dmq_ref, mgrad, kt, delta_ref, wide_dq, acc, *held,
):
    fill_keys(kv_ref, kt, 0, 0, span // TK)
    scale = HEAD ** (-0.5)

    delta_ref[...] = jnp.broadcast_to(
        jnp.sum(wide_ref[0:HEAD, :] * do_ref[...].astype(F32), axis=0, keepdims=True), (8, span)
    )
    score = dot(mkv_ref[0:MEMK, 0:HEAD], q_ref[...])
    inside = lax.broadcasted_iota(jnp.int32, score.shape, 0) < memory_rows
    share = jnp.exp(jnp.where(inside, score, MASKED) - wide_ref[HEAD : HEAD + 1, :])
    slope = dot(mkv_ref[0:MEMK, HEAD : 2 * HEAD], do_ref[...])
    back = (share * (slope - delta_ref[0:1, :])).astype(BF16)
    mgrad[...] = jnp.zeros_like(mgrad)
    mgrad[0:MEMK, :] = jnp.concatenate(
        [dot_nt(back, q_ref[...]), dot_nt(share.astype(BF16), do_ref[...])], axis=1
    )
    mem_key = mkv_ref[...].T[0:HEAD, 0:MEMK]
    wide_dq[...] = part_ref[...] + dot(mem_key, back)

    mdo = mdo_ref[...]
    qz, doz, qr, dor = query_sides(mq_ref[...], mdo, MEMQ)
    log_total, delta = row_stats(mwide_ref[...], mdo)
    share = jnp.exp(dot(kv_ref[...], qz) - log_total)
    back = (share * (dot(kv_ref[...], doz) - delta)).astype(BF16)
    grad[...] = dot(back, qr) + dot(share.astype(BF16), dor)
    dmq_ref[...] = (dot(kt[...], back) * scale).astype(BF16)
    dq_ref[:, span // 2 :] = jnp.zeros((HEAD, span // 2), BF16)
    backward_queries(
        docs, span, 0, span // TQ // 2, meta_ref, q_ref, do_ref, wide_ref, kv_ref,
        dq_ref, grad, kt, acc, delta_ref, wide_dq, held,
    )


def backward_second_kernel(
    docs, span, meta_ref, q_ref, do_ref, wide_ref, kv_ref, kt, delta_ref, wide_dq, dq_in, grad_in,
    dq_ref, grad, acc, *held,
):
    dq_ref[...] = dq_in[...]
    grad[...] = grad_in[...]
    backward_queries(
        docs, span, span // TQ // 2, span // TQ, meta_ref, q_ref, do_ref, wide_ref, kv_ref,
        dq_ref, grad, kt, acc, delta_ref, wide_dq, held,
    )


def backward_first(meta, q, do, wide, kv, part, mq, mdo, mwide, mkv, docs, memory_rows):
    count = kv.shape[0]
    return pl.pallas_call(
        functools.partial(backward_first_kernel, docs, count, memory_rows),
        out_shape=(
            jax.ShapeDtypeStruct((HEAD, count), BF16),
            jax.ShapeDtypeStruct((count, 2 * HEAD), F32),
            jax.ShapeDtypeStruct((HEAD, MEMQ), BF16),
            jax.ShapeDtypeStruct((MEMQ, 2 * HEAD), F32),
            jax.ShapeDtypeStruct((HEAD, count), BF16),
            jax.ShapeDtypeStruct((8, count), F32),
            jax.ShapeDtypeStruct((HEAD, count), F32),
        ),
        in_specs=[smem()] + [vmem()] * 9,
        out_specs=(vmem(),) * 7,
        scratch_shapes=[pltpu.VMEM((HEAD, TQ), F32)] + [pltpu.VMEM((TK, TQ), F32)] * 4,
        compiler_params=pltpu.CompilerParams(vmem_limit_bytes=VMEM_LIMIT),
        cost_estimate=pl.CostEstimate(
            flops=8 * count * count * HEAD, bytes_accessed=8 << 20, transcendentals=count * count
        ),
        name="backward_first",
    )(meta, q, do, wide, kv, part, mq, mdo, mwide, mkv)


def backward_second(meta, q, do, wide, kv, kt, delta, wide_dq, dq, grad, docs):
    count = kv.shape[0]
    return pl.pallas_call(
        functools.partial(backward_second_kernel, docs, count),
        out_shape=(
            jax.ShapeDtypeStruct((HEAD, count), BF16),
            jax.ShapeDtypeStruct((count, 2 * HEAD), F32),
        ),
        in_specs=[smem()] + [vmem()] * 9,
        out_specs=(vmem(),) * 2,
        scratch_shapes=[pltpu.VMEM((HEAD, TQ), F32)] + [pltpu.VMEM((TK, TQ), F32)] * 4,
        compiler_params=pltpu.CompilerParams(vmem_limit_bytes=VMEM_LIMIT),
        cost_estimate=pl.CostEstimate(
            flops=8 * count * count * HEAD, bytes_accessed=8 << 20, transcendentals=count * count
        ),
        name="backward_second",
    )(meta, q, do, wide, kv, kt, delta, wide_dq, dq, grad)


def mean(value):
    return jnp.mean(value, axis=-1, keepdims=True)


def norm_parts(value):
    centered = value - mean(value)
    scale = lax.rsqrt(mean(centered * centered) + EPSILON)
    return centered * scale, scale


def norm_back(back, hat, scale):
    return scale * (back - mean(back) - hat * mean(back * hat))


def middle_kernel(
    group, sides, groups, half,
    o_ref, mstate_ref, tokens_ref, mem_ref, cot_ref, mcot_ref,
    wo_a, wo_b, wu_a, wu_b, wd_a, wd_b, bo_ref, fg_ref, fb_ref, bd_ref, sg_ref, sb_ref, bu_a, bu_b,
    final_ref, mfinal_ref, first_ref, do_ref, mdo_ref, hown_ref, hpeer_ref, sum_ref,
    mixed_ref, memt_ref, parts, memt, back_ref, gown_ref, gpeer_ref, buffers,
    acted_ref, slope_ref, backs_ref, hidden_ref, low_ref, lowt_ref, fed_ref, mup_ref,
    inner_0, inner_1,
    own, psend, precv, send, recv, msend, mrecv, dsend, drecv, csend, crecv,
):
    inner_refs = (inner_0, inner_1)
    base, me, side, found = near_partners(group, sides)
    number = base // group
    far = [(lax.rem(number + t, groups) * group + me, side) for t in range(1, groups)]
    greet([(base + l, u) for l, u, apart in found] + far)
    exchanges = [
        remote(mstate_ref, parts.at[t], psend.at[t - 1], precv.at[t - 1], far[t - 1])
        for t in range(1, groups)
    ]
    for copy in exchanges:
        copy.start()

    def rows_of(apart):
        slot = (sides - apart) % sides * group
        return pl.ds(pl.multiple_of((slot + me) * HEAD, HEAD), HEAD)

    copies = []
    for k, (l, u, apart) in enumerate(found):
        start = pl.multiple_of((l * sides + u) * half, half)
        copies.append(
            remote(
                o_ref.at[:, pl.ds(start, half)],
                mixed_ref.at[rows_of(apart), :],
                send.at[k],
                recv.at[k],
                (base + l, u),
            )
        )
    for copy in copies:
        copy.start()
    columns = pl.ds(pl.multiple_of((me * sides + side) * half, half), half)
    mixed_ref[rows_of(0), :] = o_ref[:, columns]
    parts[0] = mstate_ref[...]
    for copy in exchanges:
        copy.wait()
    top = parts[0, VROWS : VROWS + 1, :]
    for t in range(1, groups):
        top = jnp.maximum(top, parts[t, VROWS : VROWS + 1, :])
    total = jnp.zeros((VROWS, MEMQ), F32)
    for t in range(groups):
        total = total + parts[t, 0:VROWS, :] * jnp.exp(parts[t, VROWS : VROWS + 1, :] - top)
    mass = total[HEAD : HEAD + 1, :]
    wide = total[0:HEAD, :] / mass
    sum_ref[0:HEAD, :] = wide
    sum_ref[HEAD : HEAD + 8, :] = jnp.broadcast_to(top + jnp.log(mass), (8, MEMQ))
    memt[...] = wide.astype(BF16)
    memt_ref[rows_of(0), :] = memt[...]
    more = []
    for k, (l, u, apart) in enumerate(found):
        more.append(
            remote(memt, memt_ref.at[rows_of(apart), :], msend.at[k], mrecv.at[k], (base + l, u))
        )
    for copy in more:
        copy.start()
    leader = ((lax.axis_index("ctx") == 0) & (side == 0)).astype(jnp.int32)
    mup_ref[...] = jnp.zeros_like(mup_ref)
    mup_ref[0 : mcot_ref.shape[0], :] = mcot_ref[...]
    model = tokens_ref.shape[1]
    rows = half + MEMQ
    mine = pl.ds(pl.multiple_of(side * half, half), half)
    hidden = wu_a.shape[1]
    chunk = 512
    place = lax.broadcasted_iota(jnp.int32, (rows, 1), 0)
    weight = jnp.where((place < half) | (leader == 1), 1.0, 0.0).astype(F32)
    b_output, first_gain, first_bias, b_down, second_gain, second_bias = (
        ref[...].astype(F32).reshape(1, model)
        for ref in (bo_ref, fg_ref, fb_ref, bd_ref, sg_ref, sb_ref)
    )
    for copy in copies + more:
        copy.wait()

    mixed_t = jnp.concatenate([mixed_ref[...], memt_ref[...]], axis=1)
    mixed = mixed_t.T
    heads = wo_a.shape[0]
    attended = dot(mixed[:, 0:heads], wo_a[...]) + dot(mixed[:, heads : 2 * heads], wo_b[...])
    own_rows = jnp.concatenate([tokens_ref[mine, :], mem_ref[...]], axis=0).astype(F32)
    first_hat, first_scale = norm_parts(own_rows + attended + b_output)
    normed = first_hat * first_gain + first_bias
    low = normed.astype(BF16)
    low_ref[...] = low
    lowt_ref[...] = (low.astype(F32) * weight).astype(BF16).T
    hidden_ref[...] = normed + b_down
    root = 0.7978845608028654
    count = hidden // chunk
    parts_of = [
        (
            slice(k * chunk, (k + 1) * chunk),
            slice((part * count + k) * chunk, (part * count + k + 1) * chunk),
            part,
        )
        for part in range(2)
        for k in range(count)
    ]
    ups, downs, up_biases, grads = (wu_a, wu_b), (wd_a, wd_b), (bu_a, bu_b), (gown_ref, gpeer_ref)

    def widen(k):
        at, to, part = parts_of[k]
        inner_refs[k % 2][...] = dot(low_ref[...], ups[part][:, at])

    widen(0)
    for k, (at, to, part) in enumerate(parts_of):
        if k + 1 < len(parts_of):
            widen(k + 1)
        inner = inner_refs[k % 2][...] + up_biases[part][at].astype(F32).reshape(1, chunk)
        square = inner * inner
        bent = jnp.tanh(inner * (root + (root * 0.044715) * square))
        grown = 0.5 + 0.5 * bent
        acted_ref[:, to] = (inner * grown).astype(BF16)
        slope_ref[:, to] = grown + inner * (1.0 - bent * bent) * (
            0.5 * root + (0.5 * root * 0.134145) * square
        )
        hidden_ref[...] += dot(acted_ref[:, to], downs[part][at, :])
    second_hat, second_scale = norm_parts(hidden_ref[...])
    final = second_hat * second_gain + second_bias
    final_ref[...] = final[0:half].astype(BF16)
    mfinal_ref[...] = final[half:rows].astype(BF16)
    upstream = jnp.concatenate([cot_ref[mine, :], mup_ref[...]], axis=0).astype(F32)
    weighted = upstream * weight
    second_gain_grad = jnp.sum(second_hat * weighted, axis=0, keepdims=True)
    second_bias_grad = jnp.sum(weighted, axis=0, keepdims=True)
    second_back = norm_back(upstream * second_gain, second_hat, second_scale)
    fed = second_back.astype(BF16)
    fed_wide = fed.astype(F32) * weight
    down_bias_grad = jnp.sum(fed_wide, axis=0, keepdims=True)
    fed_ref[...] = fed
    hidden_ref[...] = second_back

    def narrow(k):
        at, to, part = parts_of[k]
        inner_refs[k % 2][...] = dot_nt(fed_ref[...], downs[part][at, :])

    narrow(0)
    for k, (at, to, part) in enumerate(parts_of):
        if k + 1 < len(parts_of):
            narrow(k + 1)
        back = (inner_refs[k % 2][...] * slope_ref[:, to]).astype(BF16)
        backs_ref[:, to] = back
        row = 2 * hidden + heads + k % count
        grads[part][row : row + 1, :] = jnp.sum(
            back.astype(F32) * weight, axis=0, keepdims=True
        ).astype(BF16)
        hidden_ref[...] += dot_nt(backs_ref[:, to], ups[part][:, at])
    normed_back = hidden_ref[...]
    weighted_back = normed_back * weight
    first_gain_grad = jnp.sum(first_hat * weighted_back, axis=0, keepdims=True)
    first_bias_grad = jnp.sum(weighted_back, axis=0, keepdims=True)
    first_back = norm_back(normed_back * first_gain, first_hat, first_scale)
    first_ref[...] = first_back
    attended_back = first_back.astype(BF16)
    attended_wide = attended_back.astype(F32) * weight
    output_bias_grad = jnp.sum(attended_wide, axis=0, keepdims=True)
    back_ref[0:heads, :] = dot_nt(wo_a[...], attended_back).astype(BF16)
    back_ref[heads : 2 * heads, :] = dot_nt(wo_b[...], attended_back).astype(BF16)

    leaving = []
    for k, (l, u, apart) in enumerate(found):
        head = pl.multiple_of((apart * group + l) * HEAD, HEAD)
        leaving.append(
            remote(
                back_ref.at[pl.ds(head, HEAD), pl.ds(0, half)],
                do_ref.at[:, columns],
                dsend.at[k],
                drecv.at[k],
                (base + l, u),
            )
        )
    for copy in leaving:
        copy.start()
    head = pl.multiple_of(me * HEAD, HEAD)
    stays = pltpu.make_async_copy(
        back_ref.at[pl.ds(head, HEAD), pl.ds(0, half)], do_ref.at[:, columns], own
    )
    stays.start()
    mdo_ref[...] = back_ref[pl.ds(head, HEAD), half:rows]

    begin = 2 * hidden + heads + count
    small = jnp.concatenate(
        [
            output_bias_grad, first_gain_grad, first_bias_grad, down_bias_grad,
            second_gain_grad, second_bias_grad,
            jnp.zeros((gown_ref.shape[0] - begin - 6, model), F32),
        ],
        axis=0,
    ).astype(BF16)
    attended_low = attended_wide.astype(BF16)
    fed_low = fed_wide.astype(BF16)
    core = lax.rem(me, 2)
    beside = (base + core_partner(me), side)
    chips, size = hown_ref.shape[0], hown_ref.shape[1]
    sums = {}
    for part, grad_ref in ((1, gpeer_ref), (0, gown_ref)):
        for at, to, owner in parts_of:
            if owner != part:
                continue
            grad_ref[at, :] = dot(lowt_ref[...], backs_ref[:, to]).astype(BF16)
            grad_ref[hidden + at.start : hidden + at.stop, :] = dot(
                acted_ref[:, to].T, fed_low
            ).astype(BF16)
        grad_ref[2 * hidden : 2 * hidden + heads, :] = dot(
            mixed_t[part * heads : (part + 1) * heads, :], attended_low
        ).astype(BF16)
        grad_ref[begin:, :] = small
        sums[part] = []
        for p in range(chips):
            at = pl.ds(pl.multiple_of((2 * p + 1 - core) * size, size), size)
            slot = part * chips + p
            sums[part].append(
                remote(grad_ref.at[at, :], buffers.at[slot], csend.at[slot], crecv.at[slot], beside)
            )
            sums[part][-1].start()
    for part, grad_ref, total_ref in ((1, gpeer_ref, hpeer_ref), (0, gown_ref, hown_ref)):
        for p in range(chips):
            sums[part][p].wait()
            at = pl.ds(pl.multiple_of((2 * p + core) * size, size), size)
            total_ref[p] = (
                grad_ref[at, :].astype(F32) + buffers[part * chips + p].astype(F32)
            ).astype(BF16)
    stays.wait()
    for copy in leaving:
        copy.wait()


def middle(o, mstate, tokens, mem, cot, mcot, weights, vectors, bu_a, bu_b, group, sides, groups, half, grad_rows):
    model = tokens.shape[1]
    rows = half + MEMQ
    heads, hidden = weights[0].shape[0], weights[2].shape[1]
    near = group * sides - 1
    chips = groups * group // 2
    size = grad_rows // (2 * chips)
    dma = pltpu.SemaphoreType.DMA
    return pl.pallas_call(
        functools.partial(middle_kernel, group, sides, groups, half),
        out_shape=(
            jax.ShapeDtypeStruct((half, model), BF16),
            jax.ShapeDtypeStruct((MEMQ, model), BF16),
            jax.ShapeDtypeStruct((rows, model), F32),
            jax.ShapeDtypeStruct((HEAD, group * sides * half), BF16),
            jax.ShapeDtypeStruct((HEAD, MEMQ), BF16),
            jax.ShapeDtypeStruct((chips, size, model), BF16),
            jax.ShapeDtypeStruct((chips, size, model), BF16),
            jax.ShapeDtypeStruct((HEAD + 8, MEMQ), F32),
        ),
        in_specs=[vmem()] * 20,
        out_specs=(vmem(),) * 3 + (anyspace(),) + (vmem(),) * 4,
        scratch_shapes=[
            pltpu.VMEM((2 * heads, half), BF16),
            pltpu.VMEM((2 * heads, MEMQ), BF16),
            pltpu.VMEM((groups, SROWS, MEMQ), F32),
            pltpu.VMEM((HEAD, MEMQ), BF16),
            pltpu.VMEM((2 * heads, rows), BF16),
            pltpu.VMEM((grad_rows, model), BF16),
            pltpu.VMEM((grad_rows, model), BF16),
            pltpu.VMEM((2 * chips, size, model), BF16),
            pltpu.VMEM((rows, 2 * hidden), BF16),
            pltpu.VMEM((rows, 2 * hidden), F32),
            pltpu.VMEM((rows, 2 * hidden), BF16),
            pltpu.VMEM((rows, model), F32),
            pltpu.VMEM((rows, model), BF16),
            pltpu.VMEM((model, rows), BF16),
            pltpu.VMEM((rows, model), BF16),
            pltpu.VMEM((MEMQ, model), BF16),
            pltpu.VMEM((rows, model), F32),
            pltpu.VMEM((rows, model), F32),
            dma,
            dma((groups - 1,)), dma((groups - 1,)),
            dma((near,)), dma((near,)), dma((near,)), dma((near,)), dma((near,)), dma((near,)),
            dma((2 * chips,)), dma((2 * chips,)),
        ],
        compiler_params=pltpu.CompilerParams(
            collective_id=2, has_side_effects=True, vmem_limit_bytes=VMEM_LIMIT
        ),
        cost_estimate=pl.CostEstimate(
            flops=12 * rows * model * 2 * hidden, bytes_accessed=16 << 20, transcendentals=rows * hidden
        ),
        name="middle",
    )(o, mstate, tokens, mem, cot, mcot, *weights, *vectors, bu_a, bu_b)


def result_kernel(
    group, memory_rows, part_ref, other_ref, packs_ref, first_ref, sum_ref, final_ref, far_ref,
    out_token_ref, token_ref, memory_ref, query_ref, qbias_ref, key_ref, value_ref, vbias_ref,
    out_ref, up_ref, down_ref, upb_ref, small_ref,
):
    model = part_ref.shape[1]
    hidden, width = down_ref.shape[0], out_ref.shape[0]
    token_ref[...] = part_ref[...] + other_ref[...].astype(F32)
    side = lax.axis_index("wt")
    half = final_ref.shape[0]
    out_token_ref[pl.ds(pl.multiple_of(side * half, half), half), :] = final_ref[...]
    out_token_ref[pl.ds(pl.multiple_of((1 - side) * half, half), half), :] = far_ref[...]
    rows = slice(3 * HEAD, 3 * HEAD + MEMK)
    total = first_ref[first_ref.shape[0] - MEMQ : first_ref.shape[0] - MEMQ + MEMK, :]
    for h in range(group):
        total = total + packs_ref[h, rows, :].astype(F32)
    memory_ref[...] = total[0:memory_rows, :]
    for at, ref in ((0, query_ref), (HEAD, key_ref), (2 * HEAD, value_ref)):
        for h in range(0, group, 2):
            both = jnp.concatenate(
                [packs_ref[h, at : at + HEAD, :], packs_ref[h + 1, at : at + HEAD, :]], axis=0
            )
            ref[:, h * HEAD : (h + 2) * HEAD] = both.T.astype(F32)
    row = 3 * HEAD + MEMK
    for at, ref in ((0, qbias_ref), (2 * HEAD, vbias_ref)):
        ref[...] = jnp.concatenate(
            [packs_ref[h, row : row + 1, at : at + HEAD].astype(F32) for h in range(group)], axis=1
        )
    for k in range(hidden // model):
        up_ref[:, k * model : (k + 1) * model] = sum_ref[k * model : (k + 1) * model, :].astype(F32)
    down_ref[...] = sum_ref[hidden : 2 * hidden, :].astype(F32)
    begin = 2 * hidden + width
    out_ref[...] = sum_ref[2 * hidden : begin, :].astype(F32)
    chunks = hidden // model
    upb_ref[...] = jnp.concatenate(
        [sum_ref[begin + k : begin + k + 1, :].astype(F32) for k in range(chunks)], axis=1
    )
    small_ref[...] = sum_ref[begin : begin + 16, :].astype(F32)


def results(part, other, packs, first, total, final, far, group, memory_rows, hidden):
    block, model = part.shape
    width = group * HEAD
    shape = lambda *dims: jax.ShapeDtypeStruct(dims, F32)
    return pl.pallas_call(
        functools.partial(result_kernel, group, memory_rows),
        out_shape=(
            jax.ShapeDtypeStruct((block, model), BF16),
            shape(block, model), shape(memory_rows, model),
            shape(model, width), shape(1, width), shape(model, width), shape(model, width),
            shape(1, width), shape(width, model), shape(model, hidden), shape(hidden, model),
            shape(1, hidden), shape(16, model),
        ),
        in_specs=[vmem()] * 7,
        out_specs=(vmem(),) * 13,
        compiler_params=pltpu.CompilerParams(vmem_limit_bytes=VMEM_LIMIT),
        name="results",
    )(part, other, packs, first, total, final, far)


def local(
    tokens, memory, doc_starts, w_query, b_query, w_key, w_value, b_value, w_output, b_output,
    first_gain, first_bias, w_up, b_up, w_down, b_down, second_gain, second_bias,
    cotangent, mem_cotangent,
):
    block, model = tokens.shape
    memory_rows = memory.shape[0]
    docs = doc_starts.shape[0]
    width = w_query.shape[1]
    hidden = w_up.shape[1]
    group = width // HEAD
    ctx, sides = lax.axis_size("ctx"), lax.axis_size("wt")
    groups = ctx // group
    half = block // sides
    step = 16 * ctx
    grad_rows = (2 * hidden + width + hidden // model + 6 + step - 1) // step * step
    row = lambda a: a.reshape(1, a.shape[0])

    q, kv, out_b, up_b, bias_b, mq, mkv, mem_pad, w_pair, wq_t = scatter_heads(
        tokens, memory, w_query, b_query, w_key, w_value, b_value,
        w_output, w_up, b_up.reshape(8, hidden // 8), group,
    )
    forwards = [(i, i + group) for i in range(ctx - group)]
    backwards = [(i + group, i) for i in range(ctx - group)]
    swapped = [(i, (i + 1) % sides) for i in range(sides)]
    before = lax.ppermute(kv, "ctx", forwards)
    after = lax.ppermute(kv, "ctx", backwards)
    down_b = lax.ppermute(w_down, "wt", swapped)
    teams = [[g * group + l for l in range(group)] for g in range(groups)]
    late_tokens, kv = lax.optimization_barrier((tokens, kv))
    group_tokens = lax.all_gather(late_tokens, "ctx", axis_index_groups=teams, tiled=True)

    state, mstate = forward_own(doc_starts, q, kv, mq, mkv, docs, memory_rows)
    o, wide = forward_halo(doc_starts, q, before, after, state, docs)
    final, mfinal, first_back, do, mdo, total_own, total_peer, mwide = middle(
        o, mstate, tokens, mem_pad, cotangent, mem_cotangent,
        (w_output, out_b, w_up, up_b, w_down, down_b),
        [b_output, first_gain, first_bias, b_down, second_gain, second_bias],
        b_up, bias_b.reshape(hidden), group, sides, groups, half, grad_rows,
    )
    from_side = lax.ppermute(total_peer, "wt", swapped)

    part, dbefore, dafter = backward_halo(doc_starts, q, do, wide, before, after, docs)
    from_side, dbefore, dafter, final_late = lax.optimization_barrier(
        (from_side, dbefore, dafter, final)
    )
    size = grad_rows // ctx
    total = (total_own.astype(F32) + from_side.astype(F32)).reshape(groups, 2, size, model)
    row_half = lax.rem(lax.axis_index("ctx"), group) // 2
    leaving = lax.dynamic_index_in_dim(total, 1 - row_half, 1, False).astype(BF16)
    staying = lax.dynamic_index_in_dim(total, row_half, 1, False).astype(BF16)
    crossed = [(i, i ^ 2) for i in range(ctx)]
    from_row = lax.ppermute(leaving, "ctx", crossed)
    from_after = lax.ppermute(dbefore, "ctx", backwards)
    from_before = lax.ppermute(dafter, "ctx", forwards)
    dq, dkv, dmq, dmkv, kt, delta, wide_dq = backward_first(
        doc_starts, q, do, wide, kv, part, mq, mdo, mwide, mkv, docs, memory_rows
    )
    from_row, from_after, from_before, dq, dkv = lax.optimization_barrier(
        (from_row, from_after, from_before, dq, dkv)
    )
    total = (staying.astype(F32) + from_row.astype(F32)).astype(BF16)
    columns = [[g * group + l for g in range(groups)] for l in range(group)]
    total = lax.all_to_all(total, "ctx", 0, 0, axis_index_groups=columns, tiled=True)
    far = lax.ppermute(lax.optimization_barrier((final_late, dq))[0], "wt", swapped)
    dq, dkv = backward_second(
        doc_starts, q, do, wide, kv, kt, delta, wide_dq, dq, dkv, docs
    )
    total, far, dq, dkv = lax.optimization_barrier((total, far, dq, dkv))
    piece = jnp.sum(total.astype(F32), axis=0).astype(BF16)
    total = lax.all_gather(piece, "ctx", tiled=True)
    part, other, packs = tail(
        dq, dkv, from_after, from_before, group_tokens, dmq, dmkv, mem_pad, first_back, wq_t, w_pair,
        group, groups, sides, block,
    )
    (
        token_out, token_grad, memory_grad, query_grad, query_bias, key_grad, value_grad, value_bias,
        out_grad, up_grad, down_grad, up_bias, small,
    ) = results(
        part, other, packs, first_back, total, final, far, group, memory_rows, hidden
    )
    chunks = hidden // model
    return (
        token_out, mfinal[:memory_rows], token_grad, memory_grad,
        query_grad, query_bias.reshape(width), key_grad, value_grad, value_bias.reshape(width),
        out_grad, small[chunks], small[chunks + 1], small[chunks + 2],
        up_grad, up_bias.reshape(hidden), down_grad,
        small[chunks + 3], small[chunks + 4], small[chunks + 5],
    )


def solution(mesh):
    placed = (
        P("ctx", None), P(), P(), P(None, "wt"), P("wt"), P(None, "wt"), P(None, "wt"), P("wt"),
        P("wt", None), P(), P(), P(), P(None, "wt"), P("wt"), P("wt", None), P(), P(), P(),
        P("ctx", None), P(),
    )
    return jax.shard_map(
        local,
        mesh=mesh,
        in_specs=placed,
        out_specs=(
            P("ctx", None), P(), P("ctx", None), P(), P(None, "wt"), P("wt"), P(None, "wt"),
            P(None, "wt"), P("wt"), P("wt", None), P(), P(), P(), P(None, "wt"), P("wt"),
            P("wt", None), P(), P(), P(),
        ),
        check_vma=False,
    )
```

```python
import functools

import jax
import jax.numpy as jnp
from jax import lax
from jax.experimental import pallas as pl
from jax.experimental.pallas import tpu as pltpu
from jax.sharding import PartitionSpec as P

HEAD = 64
EPSILON = 1e-05
MASKED = -1e30
MESH = pl.DeviceIdType.MESH
TQ = 512
TK = 512
MEMK = 32
MEMQ = 128
ONES = 16
VROWS = HEAD + ONES
SROWS = VROWS + 8
PACK = 256
BIAS = 128
CHUNKS = 4
AHEAD = 2
BIASES = 16
SHARED = MEMK + BIASES
GROUP = 4
F32 = jnp.float32
BF16 = jnp.bfloat16
VMEM_LIMIT = 56 * 1024 * 1024


def vmem():
    return pl.BlockSpec(memory_space=pltpu.VMEM)


def smem():
    return pl.BlockSpec(memory_space=pltpu.SMEM)


def anyspace():
    return pl.BlockSpec(memory_space=pl.ANY)


def dot(a, b):
    return jnp.dot(a, b, preferred_element_type=F32)


def dot_nt(a, b):
    return lax.dot_general(a, b, (((1,), (1,)), ((), ())), preferred_element_type=F32)


def greet(partners):
    barrier = pltpu.get_barrier_semaphore()
    for partner in partners:
        pl.semaphore_signal(barrier, inc=1, device_id=partner, device_id_type=MESH)
    pl.semaphore_wait(barrier, len(partners))


def remote(src, dst, send, recv, device):
    return pltpu.make_async_remote_copy(
        src_ref=src, dst_ref=dst, send_sem=send, recv_sem=recv, device_id=device, device_id_type=MESH
    )


def group_place(group):
    here = lax.axis_index("ctx")
    return here // group * group, lax.rem(here, group), lax.axis_index("wt")


def core_partner(me):
    return me + 1 - 2 * lax.rem(me, 2)


def scatter_kernel(
    group, block, tokens_ref, memory_ref, wq_ref, bq_ref, wk_ref, wv_ref, bv_ref,
    wo_ref, wu_ref, bu_ref,
    qo_ref, kvo_ref, wo_other, wu_other, bu_other, mq_ref, mkv_ref, mem_ref, wp_ref, wqt_ref,
    qs, kvs, bpair, bcol, own, send, recv, wsend, wrecv, fsend, frecv,
):
    base, me, side = group_place(group)
    width = 2 * HEAD
    partners = [(base + lax.rem(me + t, group), side) for t in range(1, group)]
    across = (base + me, lax.rem(side + 1, lax.axis_size("wt")))
    beside = (base + core_partner(me), side)
    greet(partners + [across])
    core = lax.rem(me, 2)
    rows_o, rows_u = wo_ref.shape[0] // 2, wu_ref.shape[0] // 2

    def part(ref, rows, which):
        return ref.at[pl.ds(pl.multiple_of(which * rows, rows), rows), :]

    firsts = [
        remote(part(wo_ref, rows_o, core), part(wo_other, rows_o, core), wsend.at[0], wrecv.at[0], across),
        remote(part(wu_ref, rows_u, core), part(wu_other, rows_u, core), wsend.at[1], wrecv.at[1], across),
        remote(bu_ref, bu_other, wsend.at[2], wrecv.at[2], across),
    ]
    for copy in firsts:
        copy.start()

    bq = bq_ref[...].astype(F32).reshape(1, bq_ref.shape[0])
    bv = bv_ref[...].astype(F32).reshape(1, bv_ref.shape[0])
    none = jnp.zeros((1, HEAD), F32)
    for h in range(group):
        at = slice(h * HEAD, (h + 1) * HEAD)
        wp_ref[:, h * width : (h + 1) * width] = jnp.concatenate([wk_ref[:, at], wv_ref[:, at]], axis=1)
        bpair[:, h * width : (h + 1) * width] = jnp.concatenate([none, bv[:, at]], axis=1)
    wqt_ref[...] = wq_ref[...].T
    bcol[...] = jnp.broadcast_to(bq, (BIAS, bq.shape[1])).T
    mem_ref[...] = jnp.zeros_like(mem_ref)
    mem_ref[0 : memory_ref.shape[0], :] = memory_ref[...]
    scale = HEAD ** (-0.5)

    def project(rows_value, head):
        lanes_at = pl.ds(pl.multiple_of(head * width, width), width)
        rows_at = pl.ds(pl.multiple_of(head * HEAD, HEAD), HEAD)
        pair = (dot(rows_value, wp_ref[:, lanes_at]) + bpair[:, lanes_at]).astype(BF16)
        query = (dot_nt(wqt_ref[rows_at, :], rows_value) + bcol[rows_at, 0:1]).astype(BF16)
        return pair, query * jnp.asarray(scale, BF16)

    copies = []
    mine_rows = pl.ds(pl.multiple_of(me * block, block), block)
    for k, t in enumerate((2, 1, 3) if group == 4 else range(1, group)):
        peer = lax.rem(me + t, group)
        pair, query = project(tokens_ref[...], peer)
        kvs[t] = pair
        qs[t] = query
        device = (base + peer, side)
        copies.append(remote(kvs.at[t], kvo_ref.at[mine_rows, :], send.at[2 * k], recv.at[2 * t - 2], device))
        copies.append(remote(qs.at[t], qo_ref.at[:, mine_rows], send.at[2 * k + 1], recv.at[2 * t - 1], device))
        copies[-2].start()
        copies[-1].start()
    pair, query = project(tokens_ref[...], me)
    kvs[0] = pair
    qs[0] = query
    mine = [
        pltpu.make_async_copy(kvs.at[0], kvo_ref.at[mine_rows, :], own.at[0]),
        pltpu.make_async_copy(qs.at[0], qo_ref.at[:, mine_rows], own.at[1]),
    ]
    for copy in mine:
        copy.start()
    pair, query = project(mem_ref[...], me)
    mkv_ref[...] = pair
    mq_ref[...] = query
    for copy in firsts:
        copy.wait()
    forwards = [
        remote(part(wo_other, rows_o, core), part(wo_other, rows_o, core), fsend.at[0], frecv.at[0], beside),
        remote(part(wu_other, rows_u, core), part(wu_other, rows_u, core), fsend.at[1], frecv.at[1], beside),
    ]
    for copy in forwards:
        copy.start()
    for copy in mine + copies + forwards:
        copy.wait()


def scatter_heads(tokens, memory, wq, bq, wk, wv, bv, wo, wu, bu, group):
    block, model = tokens.shape
    width = wq.shape[1]
    like = lambda a: jax.ShapeDtypeStruct(a.shape, a.dtype)
    return pl.pallas_call(
        functools.partial(scatter_kernel, group, block),
        out_shape=(
            jax.ShapeDtypeStruct((HEAD, group * block), BF16),
            jax.ShapeDtypeStruct((group * block, 2 * HEAD), BF16),
            like(wo), like(wu), like(bu),
            jax.ShapeDtypeStruct((HEAD, MEMQ), BF16),
            jax.ShapeDtypeStruct((MEMQ, 2 * HEAD), BF16),
            jax.ShapeDtypeStruct((MEMQ, model), BF16),
            jax.ShapeDtypeStruct((model, 2 * width), BF16),
            jax.ShapeDtypeStruct((width, model), BF16),
        ),
        in_specs=[vmem()] * 7 + [anyspace()] * 3,
        out_specs=(anyspace(),) * 5 + (vmem(),) * 5,
        scratch_shapes=[
            pltpu.VMEM((group, HEAD, block), BF16),
            pltpu.VMEM((group, block, 2 * HEAD), BF16),
            pltpu.VMEM((1, 2 * width), F32),
            pltpu.VMEM((width, BIAS), F32),
            pltpu.SemaphoreType.DMA((2,)),
            pltpu.SemaphoreType.DMA((2 * group - 2,)),
            pltpu.SemaphoreType.DMA((2 * group - 2,)),
            pltpu.SemaphoreType.DMA((3,)),
            pltpu.SemaphoreType.DMA((3,)),
            pltpu.SemaphoreType.DMA((2,)),
            pltpu.SemaphoreType.DMA((2,)),
        ],
        compiler_params=pltpu.CompilerParams(
            collective_id=0, has_side_effects=True, vmem_limit_bytes=VMEM_LIMIT
        ),
        name="scatter_heads",
    )(tokens, memory, wq, bq, wk, wv, bv, wo, wu, bu)


def tail_kernel(
    group, groups, sides, block, dq_ref, wide_ref, one_ref, two_ref, own_tokens, beside_tokens, facing_tokens, corner_tokens,
    dmq_ref, dmkv_ref,
    mem_ref, first_ref, wqt_ref, wp_ref, bias_ref, piece_ref,
    part_ref, other_ref, packs_ref, mems_ref, grads_ref,
    dkv_ref, left_ref, pack_ref, parts, sums, qrows, kvrows, low, own, send, recv, rsend, rrecv, gsend, grecv,
    xsend, xrecv, psend, precv, msend, mrecv, zsend, zrecv, ysend, yrecv,
):
    base, me, side = group_place(group)
    number = base // group
    width = 2 * HEAD
    across = (base + me, lax.rem(side + 1, sides))
    partners = [(base + lax.rem(me + t, group), side) for t in range(1, group)]
    far = [(lax.rem(number + t, groups) * group + me, side) for t in range(1, groups)]
    greet(partners + far + [across])
    rows = PACK // groups
    reduces = []
    for t in range(1, groups):
        peer = lax.rem(number + t, groups)
        at = pl.ds(pl.multiple_of(peer * rows, rows), rows)
        reduces.append(
            remote(pack_ref.at[at, :], parts.at[t - 1], rsend.at[t - 1], rrecv.at[t - 1], far[t - 1])
        )
    chunk = block // CHUNKS
    head_rows = pl.ds(pl.multiple_of(me * HEAD, HEAD), HEAD)
    head_lanes = pl.ds(pl.multiple_of(me * width, width), width)
    moves = []
    for r in range(CHUNKS):
        step = []
        for t in range(1, group):
            peer = lax.rem(me + t, group)
            at = pl.ds(pl.multiple_of(peer * block + r * chunk, chunk), chunk)
            here = pl.ds(r * chunk, chunk)
            slot = (r * (group - 1) + t - 1) * 2
            step.append(
                remote(dkv_ref.at[at, :], kvrows.at[here, head_lanes], send.at[slot], recv.at[slot], partners[t - 1])
            )
            step.append(
                remote(dq_ref.at[:, at], qrows.at[head_rows, here], send.at[slot + 1], recv.at[slot + 1], partners[t - 1])
            )
        moves.append(step)
    span = group * block
    lifts = [
        remote(piece_ref, grads_ref.at[number, me], zsend.at[t - 1], zrecv.at[t - 1], far[t - 1])
        for t in range(1, groups)
    ]
    lifts[0].start()

    def settle(k, carry):
        at = pl.ds(pl.multiple_of(k * block, block), block)
        dkv_ref[at, :] = (
            wide_ref[at, :] + one_ref[at, :].astype(F32) + two_ref[at, :].astype(F32)
        ).astype(BF16)
        return carry

    lax.fori_loop(0, group, settle, 0)
    for step in moves[:AHEAD]:
        for copy in step:
            copy.start()
    at = pl.ds(pl.multiple_of(me * block, block), block)
    mine = [
        pltpu.make_async_copy(dkv_ref.at[at, :], kvrows.at[:, head_lanes], own.at[0]),
        pltpu.make_async_copy(dq_ref.at[:, at], qrows.at[head_rows, :], own.at[1]),
        pltpu.make_async_copy(piece_ref, grads_ref.at[number, me], own.at[3]),
    ]
    for copy in mine:
        copy.start()
    left_ref[0:HEAD, :] = dq_ref[...]
    for k in range(span // 512):
        at = slice(k * 512, (k + 1) * 512)
        left_ref[HEAD : 3 * HEAD, at] = dkv_ref[at, :].T
    dmkv = dmkv_ref[...].astype(BF16)
    left = jnp.concatenate([dmq_ref[...], dmkv.T], axis=0)
    model = mem_ref.shape[1]
    product = dot(left, mem_ref[...])
    beside_at = core_partner(me)
    for owner, block_ref in (
        (me, own_tokens),
        (beside_at, beside_tokens),
        (lax.rem(me + 2, group), facing_tokens),
        (lax.rem(beside_at + 2, group), corner_tokens),
    ):
        at = pl.ds(pl.multiple_of(owner * block, block), block)
        product = product + dot(left_ref[:, at], block_ref[...])
    pack_ref[0 : 3 * HEAD, :] = product.astype(BF16)
    columns = dot(left_ref[...], jnp.ones((span, BIAS), BF16)) + jnp.sum(
        left.astype(F32), axis=1, keepdims=True
    )
    wq = wqt_ref[pl.ds(pl.multiple_of(me * HEAD, HEAD), HEAD), :]
    wp = wp_ref[:, pl.ds(pl.multiple_of(me * width, width), width)]
    memory_part = dot(dmq_ref[...].T, wq) + dot_nt(dmkv, wp)
    pack_ref[3 * HEAD : 3 * HEAD + MEMK, :] = memory_part[0:MEMK, :].astype(BF16)
    pack_ref[3 * HEAD + MEMK : 3 * HEAD + SHARED, :] = bias_ref[...].astype(BF16)
    rest = PACK - 3 * HEAD - SHARED
    turned = columns.T[0:rest, :]
    pack_ref[3 * HEAD + SHARED : PACK, :] = jnp.concatenate(
        [turned, jnp.zeros((rest, model - 3 * HEAD), F32)], axis=1
    ).astype(BF16)
    for copy in reduces:
        copy.start()
    mine[0].wait()
    mine[1].wait()
    swaps, spread = [], []
    half = block // sides
    memory = pl.ds(3 * HEAD, SHARED)
    here = pl.ds(pl.multiple_of(number * rows, rows), rows)

    def reduced():
        total = pack_ref[here, :].astype(F32)
        for t in range(1, groups):
            reduces[t - 1].wait()
            total = total + parts[t - 1].astype(F32)
        sums[here, :] = total.astype(BF16)
        for t in range(1, groups):
            spread.append(
                remote(sums.at[here, :], sums.at[here, :], gsend.at[t - 1], grecv.at[t - 1], far[t - 1])
            )
            spread[-1].start()

    beside = (base + core_partner(me), side)
    opposite = lax.rem(me + 2, group)
    facing = (base + opposite, side)
    exchange = remote(sums.at[memory, :], mems_ref.at[me], msend.at[0], mrecv.at[0], across)
    first = [
        remote(sums, packs_ref.at[me], psend.at[0], precv.at[0], facing),
        remote(sums, packs_ref.at[me], psend.at[1], precv.at[1], beside),
    ]
    last = pltpu.make_async_copy(sums, packs_ref.at[me], own.at[2])

    def handed(which, slot, k, device):
        return remote(which.at[slot], which.at[slot], msend.at[k], mrecv.at[k], device)

    second = remote(
        packs_ref.at[opposite], packs_ref.at[opposite], psend.at[2], precv.at[2], beside
    )

    def shifted(slot, k, which, device):
        return remote(
            grads_ref.at[slot, which], grads_ref.at[slot, which], ysend.at[k], yrecv.at[k], device
        )

    def came(t):
        return lax.rem(number - t + groups, groups)

    sideways, passed = [], []
    for r in range(CHUNKS):
        for copy in moves[r]:
            copy.wait()
        if r + AHEAD < CHUNKS:
            for copy in moves[r + AHEAD]:
                copy.start()
        at = pl.ds(r * chunk, chunk)
        value = dot(qrows[:, at].T, wqt_ref[...]) + dot_nt(kvrows[at, :], wp_ref[...])
        inside = (r * chunk) // half
        extra = first_ref[pl.ds(r * chunk - inside * half, chunk), :]
        value = value + extra * (side == inside).astype(F32)
        part_ref[at, :] = value
        low[at, :] = value.astype(BF16)
        swaps.append(remote(low.at[at, :], other_ref.at[at, :], xsend.at[r], xrecv.at[r], across))
        swaps[-1].start()
        if r == 0:
            reduced()
            for copy in lifts[1:]:
                copy.start()
        if r == 1:
            for copy in spread:
                copy.wait()
            exchange.start()
            for copy in first:
                copy.start()
            last.start()
            mine[2].wait()
            sideways.append((shifted(number, 0, me, facing), shifted(number, groups, me, beside)))
            for copy in sideways[0]:
                copy.start()
    for t in range(1, groups):
        lifts[t - 1].wait()
        slot = came(t)
        sideways.append((shifted(slot, t, me, facing), shifted(slot, groups + t, me, beside)))
        for copy in sideways[t]:
            copy.start()
    exchange.wait()
    onward = [handed(mems_ref, me, 1, facing), handed(mems_ref, me, 2, beside)]
    for copy in onward:
        copy.start()
    first[0].wait()
    second.start()
    onward[0].wait()
    relay = handed(mems_ref, opposite, 3, beside)
    relay.start()
    for t in range(groups):
        sideways[t][0].wait()
        passed.append(shifted(came(t), 2 * groups + t, opposite, beside))
        passed[t].start()
    last.wait()
    first[1].wait()
    second.wait()
    onward[1].wait()
    relay.wait()
    for t in range(groups):
        sideways[t][1].wait()
        passed[t].wait()
    for copy in swaps:
        copy.wait()


def tail(dq, dkv, one, two, blocks, dmq, dmkv, mem, first, wqt, wp, biases, piece, group, groups, sides, block):
    model = first.shape[1]
    width = wqt.shape[0]
    moves = CHUNKS * (group - 1) * 2
    return pl.pallas_call(
        functools.partial(tail_kernel, group, groups, sides, block),
        out_shape=(
            jax.ShapeDtypeStruct((block, model), F32),
            jax.ShapeDtypeStruct((block, model), BF16),
            jax.ShapeDtypeStruct((group, PACK, model), BF16),
            jax.ShapeDtypeStruct((group, SHARED, model), BF16),
            jax.ShapeDtypeStruct((groups, group) + piece.shape, BF16),
        ),
        in_specs=[vmem()] * 15 + [anyspace()],
        out_specs=(vmem(),) + (anyspace(),) * 4,
        scratch_shapes=[
            pltpu.VMEM((group * block, 2 * HEAD), BF16),
            pltpu.VMEM((3 * HEAD, group * block), BF16),
            pltpu.VMEM((PACK, model), BF16),
            pltpu.VMEM((groups - 1, PACK // groups, model), BF16),
            pltpu.VMEM((PACK, model), BF16),
            pltpu.VMEM((width, block), BF16),
            pltpu.VMEM((block, 2 * width), BF16),
            pltpu.VMEM((block, model), BF16),
            pltpu.SemaphoreType.DMA((4,)),
            pltpu.SemaphoreType.DMA((moves,)),
            pltpu.SemaphoreType.DMA((moves,)),
            pltpu.SemaphoreType.DMA((groups - 1,)),
            pltpu.SemaphoreType.DMA((groups - 1,)),
            pltpu.SemaphoreType.DMA((groups - 1,)),
            pltpu.SemaphoreType.DMA((groups - 1,)),
            pltpu.SemaphoreType.DMA((CHUNKS,)),
            pltpu.SemaphoreType.DMA((CHUNKS,)),
            pltpu.SemaphoreType.DMA((3,)),
            pltpu.SemaphoreType.DMA((3,)),
            pltpu.SemaphoreType.DMA((4,)),
            pltpu.SemaphoreType.DMA((4,)),
            pltpu.SemaphoreType.DMA((groups - 1,)),
            pltpu.SemaphoreType.DMA((groups - 1,)),
            pltpu.SemaphoreType.DMA((3 * groups,)),
            pltpu.SemaphoreType.DMA((3 * groups,)),
        ],
        compiler_params=pltpu.CompilerParams(
            collective_id=1, has_side_effects=True, vmem_limit_bytes=VMEM_LIMIT
        ),
        name="tail",
    )(dq, dkv, one, two, *blocks, dmq, dmkv, mem, first, wqt, wp, biases, piece)


def near_partners(group, sides):
    base, me, side = group_place(group)
    found = []
    for u in range(sides):
        for t in range(group):
            if t or u:
                found.append((lax.rem(me + t, group), lax.rem(side + u, sides), u))
    return base, me, side, found


def span_place(span):
    block = span // GROUP
    return lax.axis_size("ctx") * block, lax.axis_index("ctx") // GROUP * span


def doc_bounds(starts_ref, docs, first, last, total):
    low = starts_ref[0]
    low_end = total
    top = starts_ref[0]
    high = total
    for d in range(docs):
        start = starts_ref[d]
        low = jnp.where(start <= first, start, low)
        top = jnp.where(start <= last, start, top)
    for d in range(docs - 1, -1, -1):
        start = starts_ref[d]
        low_end = jnp.where(start > first, start, low_end)
        high = jnp.where(start > last, start, high)
    return low, low_end, top, high


def doc_rows(starts_ref, docs, first, total):
    place = first + lax.broadcasted_iota(jnp.int32, (1, TQ), 1)
    low = jnp.zeros((1, TQ), jnp.int32)
    high = jnp.full((1, TQ), total, jnp.int32)
    for d in range(docs):
        start = starts_ref[d]
        low = jnp.where(place >= start, start, low)
    for d in range(docs - 1, -1, -1):
        start = starts_ref[d]
        high = jnp.where(place < start, start, high)
    return low, high


def allowed_block(key_first, low, high):
    place = lax.broadcasted_iota(jnp.int32, (TK, TQ), 0) - (low - key_first)
    return place.astype(jnp.uint32) < (high - low).astype(jnp.uint32)


def tile(ref, number, size):
    return ref[pl.ds(pl.multiple_of(number * size, size), size), :]


def lanes(ref, number, size):
    return ref[:, pl.ds(pl.multiple_of(number * size, size), size)]


def pad_query(q, size):
    return jnp.concatenate([q, jnp.zeros((HEAD, size), BF16)], axis=0)


def fill_values(kv_ref, va, column, begin, end):
    def step(k, carry):
        turned = tile(kv_ref, k, TK).T
        at = pl.ds(pl.multiple_of(column + k * TK, TK), TK)
        va[0:HEAD, at] = turned[HEAD : 2 * HEAD, :]
        va[HEAD:VROWS, at] = jnp.ones((ONES, TK), BF16)
        return carry

    lax.fori_loop(begin, end, step, 0)


def key_range(bounds, kv_first, count):
    begin = jnp.clip(bounds[0] - kv_first, 0, count) // TK
    end = (jnp.clip(bounds[3] - kv_first, 0, count) + TK - 1) // TK
    return begin, end


def pair_loop(bounds, begin, end, kv_first, low, high, score, use):
    doc_first, doc_first_end, doc_last, doc_end = bounds
    single = doc_first == doc_last

    @pl.when(begin < end)
    def _():
        score(0, begin)

        def step(i, carry):
            k = begin + 2 * i
            at = kv_first + k * TK
            both = k + 1 < end
            whole = single & both & (at >= doc_first) & (at + 2 * TK <= doc_end)

            @pl.when(whole)
            def _():
                score(1, k + 1)
                use(0, k, None)
                score(0, k + 2)
                use(1, k + 1, None)

            @pl.when(jnp.logical_not(whole) & both)
            def _():
                score(1, k + 1)
                use(0, k, allowed_block(at, low, high))
                score(0, k + 2)
                use(1, k + 1, allowed_block(at + TK, low, high))

            @pl.when(jnp.logical_not(both))
            def _():
                use(0, k, allowed_block(at, low, high))

            return carry

        lax.fori_loop(0, (end - begin + 1) // 2, step, 0)


def online(score, value, acc, top):
    old = top[0:1, :]
    new = jnp.maximum(old, jnp.max(score, axis=0, keepdims=True))
    share = jnp.exp(score - new).astype(BF16)
    acc[...] = acc[...] * jnp.exp(old - new) + dot(value, share)
    top[...] = jnp.broadcast_to(new, top.shape)


def forward_tiles(bounds, low, high, kv_ref, kv_first, va, va_column, qz, acc, top, held):
    begin, end = key_range(bounds, kv_first, kv_ref.shape[0])

    def score(slot, k):
        held[slot][...] = dot(tile(kv_ref, jnp.minimum(k, end - 1), TK), qz)

    def use(slot, k, allowed):
        at = pl.ds(pl.multiple_of(va_column + k * TK, TK), TK)
        score = held[slot][...]
        if allowed is not None:
            score = jnp.where(allowed, score, MASKED)
        online(score, va[:, at], acc, top)

    pair_loop(bounds, begin, end, kv_first, low, high, score, use)


def forward_own_kernel(
    docs, span, memory_rows, meta_ref, q_ref, kv_ref, mq_ref, mkv_ref,
    state_ref, mstate_ref, va, acc, top, held0, held1,
):
    total, base = span_place(span)
    fill_values(kv_ref, va, 0, 0, span // TK)
    turned = mkv_ref[...].T
    mem_value = jnp.concatenate(
        [turned[HEAD : 2 * HEAD, 0:MEMK], jnp.ones((ONES, MEMK), BF16)], axis=0
    )
    score = dot(mkv_ref[0:MEMK, 0:HEAD], q_ref[...])
    inside = lax.broadcasted_iota(jnp.int32, score.shape, 0) < memory_rows
    score = jnp.where(inside, score, MASKED)
    new = jnp.max(score, axis=0, keepdims=True)
    state_ref[0:VROWS, :] = dot(mem_value, jnp.exp(score - new).astype(BF16))
    state_ref[VROWS:SROWS, :] = jnp.broadcast_to(new, (8, span))

    def query_step(qi, carry):
        first = base + qi * TQ
        bounds = doc_bounds(meta_ref, docs, first, first + TQ - 1, total)
        low, high = doc_rows(meta_ref, docs, first, total)
        at = pl.ds(pl.multiple_of(qi * TQ, TQ), TQ)
        qz = pad_query(q_ref[:, at], TQ)
        acc[...] = state_ref[0:VROWS, at]
        top[...] = state_ref[VROWS:SROWS, at]
        forward_tiles(bounds, low, high, kv_ref, base, va, 0, qz, acc, top, (held0, held1))
        state_ref[0:VROWS, at] = acc[...]
        state_ref[VROWS:SROWS, at] = top[...]
        return carry

    lax.fori_loop(0, span // TQ, query_step, 0)

    score = dot(kv_ref[...], pad_query(mq_ref[...], MEMQ))
    new = jnp.max(score, axis=0, keepdims=True)
    mstate_ref[0:VROWS, :] = dot(va[...], jnp.exp(score - new).astype(BF16))
    mstate_ref[VROWS:SROWS, :] = jnp.broadcast_to(new, (8, MEMQ))


def forward_own(meta, q, kv, mq, mkv, docs, memory_rows):
    count = kv.shape[0]
    return pl.pallas_call(
        functools.partial(forward_own_kernel, docs, count, memory_rows),
        out_shape=(
            jax.ShapeDtypeStruct((SROWS, count), F32),
            jax.ShapeDtypeStruct((SROWS, MEMQ), F32),
        ),
        in_specs=[smem()] + [vmem()] * 4,
        out_specs=(vmem(), vmem()),
        scratch_shapes=[
            pltpu.VMEM((VROWS, count), BF16),
            pltpu.VMEM((VROWS, TQ), F32),
            pltpu.VMEM((8, TQ), F32),
            pltpu.VMEM((TK, TQ), F32),
            pltpu.VMEM((TK, TQ), F32),
        ],
        compiler_params=pltpu.CompilerParams(vmem_limit_bytes=VMEM_LIMIT),
        cost_estimate=pl.CostEstimate(
            flops=8 * count * count * HEAD, bytes_accessed=4 << 20, transcendentals=count * count
        ),
        name="forward_own",
    )(meta, q, kv, mq, mkv)


def halo_ranges(meta_ref, docs, base, span, total):
    first = doc_bounds(meta_ref, docs, base, base + span - 1, total)
    before = jnp.clip(first[0] - (base - span), 0, span) // TK
    after = (jnp.clip(first[3] - (base + span), 0, span) + TK - 1) // TK
    return before, after


def forward_halo_kernel(
    docs, span, meta_ref, q_ref, before_ref, after_ref, state_ref, o_ref, wide_ref,
    va, acc, top, held0, held1,
):
    total, base = span_place(span)
    count = before_ref.shape[0]
    from_before, to_after = halo_ranges(meta_ref, docs, base, span, total)
    fill_values(before_ref, va, 0, from_before, span // TK)
    fill_values(after_ref, va, count, 0, to_after)
    held = (held0, held1)

    def query_step(qi, carry):
        first = base + qi * TQ
        bounds = doc_bounds(meta_ref, docs, first, first + TQ - 1, total)
        low, high = doc_rows(meta_ref, docs, first, total)
        at = pl.ds(pl.multiple_of(qi * TQ, TQ), TQ)
        qz = pad_query(q_ref[:, at], TQ)
        acc[...] = state_ref[0:VROWS, at]
        top[...] = state_ref[VROWS:SROWS, at]
        forward_tiles(bounds, low, high, before_ref, base - count, va, 0, qz, acc, top, held)
        forward_tiles(bounds, low, high, after_ref, base + count, va, count, qz, acc, top, held)
        mass = acc[HEAD : HEAD + 1, :]
        wide = acc[0:HEAD, :] / mass
        o_ref[:, at] = wide.astype(BF16)
        wide_ref[0:HEAD, at] = wide
        wide_ref[HEAD : HEAD + 8, at] = top[...] + jnp.log(jnp.broadcast_to(mass, top.shape))
        return carry

    lax.fori_loop(0, span // TQ, query_step, 0)


def forward_halo(meta, q, before, after, state, docs):
    count = before.shape[0]
    return pl.pallas_call(
        functools.partial(forward_halo_kernel, docs, count),
        out_shape=(
            jax.ShapeDtypeStruct((HEAD, count), BF16),
            jax.ShapeDtypeStruct((HEAD + 8, count), F32),
        ),
        in_specs=[smem()] + [vmem()] * 4,
        out_specs=(vmem(), vmem()),
        scratch_shapes=[
            pltpu.VMEM((VROWS, 2 * count), BF16),
            pltpu.VMEM((VROWS, TQ), F32),
            pltpu.VMEM((8, TQ), F32),
            pltpu.VMEM((TK, TQ), F32),
            pltpu.VMEM((TK, TQ), F32),
        ],
        compiler_params=pltpu.CompilerParams(vmem_limit_bytes=VMEM_LIMIT),
        cost_estimate=pl.CostEstimate(
            flops=4 * count * count * HEAD, bytes_accessed=6 << 20, transcendentals=count * count
        ),
        name="forward_halo",
    )(meta, q, before, after, state)


def backward_tiles(
    bounds, low, high, kv_ref, kv_first, kt, kt_column, grad, sides, stats, acc, held
):
    qz, doz, qr, dor = sides
    log_total, delta = stats
    begin, end = key_range(bounds, kv_first, kv_ref.shape[0])

    def score(slot, k):
        pair = tile(kv_ref, jnp.minimum(k, end - 1), TK)
        held[slot][...] = dot(pair, qz)
        held[slot + 2][...] = dot(pair, doz)

    def use(slot, k, allowed):
        at = pl.ds(pl.multiple_of(kt_column + k * TK, TK), TK)
        share = jnp.exp(held[slot][...] - log_total)
        if allowed is not None:
            share = jnp.where(allowed, share, 0.0)
        back = (share * (held[slot + 2][...] - delta)).astype(BF16)
        grad[at, :] += dot(back, qr) + dot(share.astype(BF16), dor)
        acc[...] += dot(kt[:, at], back)

    pair_loop(bounds, begin, end, kv_first, low, high, score, use)


def fill_keys(kv_ref, kt, column, begin, end):
    def step(k, carry):
        turned = tile(kv_ref, k, TK).T
        kt[:, pl.ds(pl.multiple_of(column + k * TK, TK), TK)] = turned[0:HEAD, :]
        return carry

    lax.fori_loop(begin, end, step, 0)


def query_sides(q, do, size):
    zero = jnp.zeros((HEAD, size), BF16)
    qz = jnp.concatenate([q, zero], axis=0)
    doz = jnp.concatenate([zero, do], axis=0)
    return qz, doz, qz.T, doz.T


def row_stats(wide, do):
    return wide[HEAD : HEAD + 1, :], jnp.sum(
        wide[0:HEAD, :] * do.astype(F32), axis=0, keepdims=True
    )


def backward_halo_kernel(
    docs, span, meta_ref, q_ref, do_ref, wide_ref, before_ref, after_ref,
    dq_ref, dbefore_ref, dafter_ref, kt, grad, acc, *held,
):
    total, base = span_place(span)
    count = before_ref.shape[0]
    from_before, to_after = halo_ranges(meta_ref, docs, base, span, total)
    fill_keys(before_ref, kt, 0, from_before, span // TK)
    fill_keys(after_ref, kt, count, 0, to_after)

    def clear(k, carry):
        grad[pl.ds(pl.multiple_of(k * TK, TK), TK), :] = jnp.zeros((TK, 2 * HEAD), F32)
        return carry

    lax.fori_loop(from_before, span // TK + to_after, clear, 0)

    def query_step(qi, carry):
        first = base + qi * TQ
        bounds = doc_bounds(meta_ref, docs, first, first + TQ - 1, total)
        low, high = doc_rows(meta_ref, docs, first, total)
        at = pl.ds(pl.multiple_of(qi * TQ, TQ), TQ)
        acc[...] = jnp.zeros_like(acc)

        @pl.when((bounds[0] < base) | (bounds[3] > base + count))
        def _():
            do = do_ref[:, at]
            sides = query_sides(q_ref[:, at], do, TQ)
            stats = row_stats(wide_ref[:, at], do)
            for ref, begin, column in (
                (before_ref, base - count, 0),
                (after_ref, base + count, count),
            ):
                backward_tiles(
                    bounds, low, high, ref, begin, kt, column, grad, sides, stats, acc, held
                )

        dq_ref[:, at] = acc[...]
        return carry

    lax.fori_loop(0, span // TQ, query_step, 0)
    dbefore_ref[...] = jnp.zeros_like(dbefore_ref)
    dafter_ref[...] = jnp.zeros_like(dafter_ref)

    def keep_before(k, carry):
        at = pl.ds(pl.multiple_of(k * TK, TK), TK)
        dbefore_ref[at, :] = grad[at, :].astype(BF16)
        return carry

    def keep_after(k, carry):
        at = pl.ds(pl.multiple_of(k * TK, TK), TK)
        dafter_ref[at, :] = grad[pl.ds(pl.multiple_of(count + k * TK, TK), TK), :].astype(BF16)
        return carry

    lax.fori_loop(from_before, span // TK, keep_before, 0)
    lax.fori_loop(0, to_after, keep_after, 0)


def backward_halo(meta, q, do, wide, before, after, docs):
    count = before.shape[0]
    return pl.pallas_call(
        functools.partial(backward_halo_kernel, docs, count),
        out_shape=(
            jax.ShapeDtypeStruct((HEAD, count), F32),
            jax.ShapeDtypeStruct((count, 2 * HEAD), BF16),
            jax.ShapeDtypeStruct((count, 2 * HEAD), BF16),
        ),
        in_specs=[smem()] + [vmem()] * 5,
        out_specs=(vmem(),) * 3,
        scratch_shapes=[
            pltpu.VMEM((HEAD, 2 * count), BF16),
            pltpu.VMEM((2 * count, 2 * HEAD), F32),
            pltpu.VMEM((HEAD, TQ), F32),
        ]
        + [pltpu.VMEM((TK, TQ), F32)] * 4,
        compiler_params=pltpu.CompilerParams(vmem_limit_bytes=VMEM_LIMIT),
        cost_estimate=pl.CostEstimate(
            flops=8 * count * count * HEAD, bytes_accessed=8 << 20, transcendentals=count * count
        ),
        name="backward_halo",
    )(meta, q, do, wide, before, after)


def backward_queries(
    docs, span, first_tile, last_tile, meta_ref, q_ref, do_ref, wide_ref, kv_ref,
    dq_ref, grad, kt, acc, delta_ref, wide_dq, held,
):
    total, base = span_place(span)
    scale = HEAD ** (-0.5)

    def query_step(qi, carry):
        first = base + qi * TQ
        bounds = doc_bounds(meta_ref, docs, first, first + TQ - 1, total)
        low, high = doc_rows(meta_ref, docs, first, total)
        at = pl.ds(pl.multiple_of(qi * TQ, TQ), TQ)
        sides = query_sides(q_ref[:, at], do_ref[:, at], TQ)
        stats = wide_ref[HEAD : HEAD + 1, at], delta_ref[0:1, at]
        acc[...] = wide_dq[:, at]
        backward_tiles(bounds, low, high, kv_ref, base, kt, 0, grad, sides, stats, acc, held)
        dq_ref[:, at] = (acc[...] * scale).astype(BF16)
        return carry

    lax.fori_loop(first_tile, last_tile, query_step, 0)


def backward_first_kernel(
    docs, span, memory_rows, meta_ref, q_ref, do_ref, wide_ref, kv_ref, part_ref,
    mq_ref, mdo_ref, mwide_ref, mkv_ref,
    dq_ref, grad, dmq_ref, mgrad, kt, delta_ref, wide_dq, acc, *held,
):
    fill_keys(kv_ref, kt, 0, 0, span // TK)
    scale = HEAD ** (-0.5)

    delta_ref[...] = jnp.broadcast_to(
        jnp.sum(wide_ref[0:HEAD, :] * do_ref[...].astype(F32), axis=0, keepdims=True), (8, span)
    )
    score = dot(mkv_ref[0:MEMK, 0:HEAD], q_ref[...])
    inside = lax.broadcasted_iota(jnp.int32, score.shape, 0) < memory_rows
    share = jnp.exp(jnp.where(inside, score, MASKED) - wide_ref[HEAD : HEAD + 1, :])
    slope = dot(mkv_ref[0:MEMK, HEAD : 2 * HEAD], do_ref[...])
    back = (share * (slope - delta_ref[0:1, :])).astype(BF16)
    mgrad[...] = jnp.zeros_like(mgrad)
    mgrad[0:MEMK, :] = jnp.concatenate(
        [dot_nt(back, q_ref[...]), dot_nt(share.astype(BF16), do_ref[...])], axis=1
    )
    mem_key = mkv_ref[...].T[0:HEAD, 0:MEMK]
    wide_dq[...] = part_ref[...] + dot(mem_key, back)

    mdo = mdo_ref[...]
    qz, doz, qr, dor = query_sides(mq_ref[...], mdo, MEMQ)
    log_total, delta = row_stats(mwide_ref[...], mdo)
    share = jnp.exp(dot(kv_ref[...], qz) - log_total)
    back = (share * (dot(kv_ref[...], doz) - delta)).astype(BF16)
    grad[...] = dot(back, qr) + dot(share.astype(BF16), dor)
    dmq_ref[...] = (dot(kt[...], back) * scale).astype(BF16)
    dq_ref[:, span // 2 :] = jnp.zeros((HEAD, span // 2), BF16)
    backward_queries(
        docs, span, 0, span // TQ // 2, meta_ref, q_ref, do_ref, wide_ref, kv_ref,
        dq_ref, grad, kt, acc, delta_ref, wide_dq, held,
    )


def backward_second_kernel(
    docs, span, meta_ref, q_ref, do_ref, wide_ref, kv_ref, kt, delta_ref, wide_dq, dq_in, grad_in,
    dq_ref, grad, acc, *held,
):
    dq_ref[...] = dq_in[...]
    grad[...] = grad_in[...]
    backward_queries(
        docs, span, span // TQ // 2, span // TQ, meta_ref, q_ref, do_ref, wide_ref, kv_ref,
        dq_ref, grad, kt, acc, delta_ref, wide_dq, held,
    )


def backward_first(meta, q, do, wide, kv, part, mq, mdo, mwide, mkv, docs, memory_rows):
    count = kv.shape[0]
    return pl.pallas_call(
        functools.partial(backward_first_kernel, docs, count, memory_rows),
        out_shape=(
            jax.ShapeDtypeStruct((HEAD, count), BF16),
            jax.ShapeDtypeStruct((count, 2 * HEAD), F32),
            jax.ShapeDtypeStruct((HEAD, MEMQ), BF16),
            jax.ShapeDtypeStruct((MEMQ, 2 * HEAD), F32),
            jax.ShapeDtypeStruct((HEAD, count), BF16),
            jax.ShapeDtypeStruct((8, count), F32),
            jax.ShapeDtypeStruct((HEAD, count), F32),
        ),
        in_specs=[smem()] + [vmem()] * 9,
        out_specs=(vmem(),) * 7,
        scratch_shapes=[pltpu.VMEM((HEAD, TQ), F32)] + [pltpu.VMEM((TK, TQ), F32)] * 4,
        compiler_params=pltpu.CompilerParams(vmem_limit_bytes=VMEM_LIMIT),
        cost_estimate=pl.CostEstimate(
            flops=8 * count * count * HEAD, bytes_accessed=8 << 20, transcendentals=count * count
        ),
        name="backward_first",
    )(meta, q, do, wide, kv, part, mq, mdo, mwide, mkv)


def backward_second(meta, q, do, wide, kv, kt, delta, wide_dq, dq, grad, docs):
    count = kv.shape[0]
    return pl.pallas_call(
        functools.partial(backward_second_kernel, docs, count),
        out_shape=(
            jax.ShapeDtypeStruct((HEAD, count), BF16),
            jax.ShapeDtypeStruct((count, 2 * HEAD), F32),
        ),
        in_specs=[smem()] + [vmem()] * 9,
        out_specs=(vmem(),) * 2,
        scratch_shapes=[pltpu.VMEM((HEAD, TQ), F32)] + [pltpu.VMEM((TK, TQ), F32)] * 4,
        compiler_params=pltpu.CompilerParams(vmem_limit_bytes=VMEM_LIMIT),
        cost_estimate=pl.CostEstimate(
            flops=8 * count * count * HEAD, bytes_accessed=8 << 20, transcendentals=count * count
        ),
        name="backward_second",
    )(meta, q, do, wide, kv, kt, delta, wide_dq, dq, grad)


def mean(value):
    return jnp.mean(value, axis=-1, keepdims=True)


def norm_parts(value):
    centered = value - mean(value)
    scale = lax.rsqrt(mean(centered * centered) + EPSILON)
    return centered * scale, scale


def norm_back(back, hat, scale):
    return scale * (back - mean(back) - hat * mean(back * hat))


def middle_kernel(
    group, sides, groups, half,
    o_ref, mstate_ref, tokens_ref, mem_ref, cot_ref, mcot_ref,
    wo_a, wo_b, wu_a, wu_b, wd_a, wd_b, bo_ref, fg_ref, fb_ref, bd_ref, sg_ref, sb_ref, bu_a, bu_b,
    final_ref, mfinal_ref, first_ref, do_ref, mdo_ref, hown_ref, hpeer_ref, sum_ref, bias_ref,
    mixed_ref, memt_ref, parts, memt, back_ref, gown_ref, gpeer_ref, buffers,
    acted_ref, slope_ref, backs_ref, hidden_ref, low_ref, lowt_ref, fed_ref, mup_ref,
    inner_0, inner_1,
    own, psend, precv, send, recv, msend, mrecv, dsend, drecv, csend, crecv,
):
    inner_refs = (inner_0, inner_1)
    base, me, side, found = near_partners(group, sides)
    number = base // group
    far = [(lax.rem(number + t, groups) * group + me, side) for t in range(1, groups)]
    greet([(base + l, u) for l, u, apart in found] + far)
    exchanges = [
        remote(mstate_ref, parts.at[t], psend.at[t - 1], precv.at[t - 1], far[t - 1])
        for t in range(1, groups)
    ]
    for copy in exchanges:
        copy.start()

    def rows_of(apart):
        slot = (sides - apart) % sides * group
        return pl.ds(pl.multiple_of((slot + me) * HEAD, HEAD), HEAD)

    copies = []
    for k, (l, u, apart) in enumerate(found):
        start = pl.multiple_of((l * sides + u) * half, half)
        copies.append(
            remote(
                o_ref.at[:, pl.ds(start, half)],
                mixed_ref.at[rows_of(apart), :],
                send.at[k],
                recv.at[k],
                (base + l, u),
            )
        )
    for copy in copies:
        copy.start()
    columns = pl.ds(pl.multiple_of((me * sides + side) * half, half), half)
    mixed_ref[rows_of(0), :] = o_ref[:, columns]
    parts[0] = mstate_ref[...]
    for copy in exchanges:
        copy.wait()
    top = parts[0, VROWS : VROWS + 1, :]
    for t in range(1, groups):
        top = jnp.maximum(top, parts[t, VROWS : VROWS + 1, :])
    total = jnp.zeros((VROWS, MEMQ), F32)
    for t in range(groups):
        total = total + parts[t, 0:VROWS, :] * jnp.exp(parts[t, VROWS : VROWS + 1, :] - top)
    mass = total[HEAD : HEAD + 1, :]
    wide = total[0:HEAD, :] / mass
    sum_ref[0:HEAD, :] = wide
    sum_ref[HEAD : HEAD + 8, :] = jnp.broadcast_to(top + jnp.log(mass), (8, MEMQ))
    memt[...] = wide.astype(BF16)
    memt_ref[rows_of(0), :] = memt[...]
    more = []
    for k, (l, u, apart) in enumerate(found):
        more.append(
            remote(memt, memt_ref.at[rows_of(apart), :], msend.at[k], mrecv.at[k], (base + l, u))
        )
    for copy in more:
        copy.start()
    leader = ((lax.axis_index("ctx") == 0) & (side == 0)).astype(jnp.int32)
    mup_ref[...] = jnp.zeros_like(mup_ref)
    mup_ref[0 : mcot_ref.shape[0], :] = mcot_ref[...]
    model = tokens_ref.shape[1]
    rows = half + MEMQ
    mine = pl.ds(pl.multiple_of(side * half, half), half)
    hidden = wu_a.shape[1]
    chunk = 512
    place = lax.broadcasted_iota(jnp.int32, (rows, 1), 0)
    weight = jnp.where((place < half) | (leader == 1), 1.0, 0.0).astype(F32)
    b_output, first_gain, first_bias, b_down, second_gain, second_bias = (
        ref[...].astype(F32).reshape(1, model)
        for ref in (bo_ref, fg_ref, fb_ref, bd_ref, sg_ref, sb_ref)
    )
    for copy in copies + more:
        copy.wait()

    mixed_t = jnp.concatenate([mixed_ref[...], memt_ref[...]], axis=1)
    mixed = mixed_t.T
    heads = wo_a.shape[0]
    attended = dot(mixed[:, 0:heads], wo_a[...]) + dot(mixed[:, heads : 2 * heads], wo_b[...])
    own_rows = jnp.concatenate([tokens_ref[mine, :], mem_ref[...]], axis=0).astype(F32)
    first_hat, first_scale = norm_parts(own_rows + attended + b_output)
    normed = first_hat * first_gain + first_bias
    low = normed.astype(BF16)
    low_ref[...] = low
    lowt_ref[...] = (low.astype(F32) * weight).astype(BF16).T
    hidden_ref[...] = normed + b_down
    root = 0.7978845608028654
    count = hidden // chunk
    parts_of = [
        (
            slice(k * chunk, (k + 1) * chunk),
            slice((part * count + k) * chunk, (part * count + k + 1) * chunk),
            part,
        )
        for part in range(2)
        for k in range(count)
    ]
    ups, downs, up_biases, grads = (wu_a, wu_b), (wd_a, wd_b), (bu_a, bu_b), (gown_ref, gpeer_ref)

    def widen(k):
        at, to, part = parts_of[k]
        inner_refs[k % 2][...] = dot(low_ref[...], ups[part][:, at])

    widen(0)
    for k, (at, to, part) in enumerate(parts_of):
        if k + 1 < len(parts_of):
            widen(k + 1)
        inner = inner_refs[k % 2][...] + up_biases[part][at].astype(F32).reshape(1, chunk)
        square = inner * inner
        bent = jnp.tanh(inner * (root + (root * 0.044715) * square))
        grown = 0.5 + 0.5 * bent
        acted_ref[:, to] = (inner * grown).astype(BF16)
        slope_ref[:, to] = grown + inner * (1.0 - bent * bent) * (
            0.5 * root + (0.5 * root * 0.134145) * square
        )
        hidden_ref[...] += dot(acted_ref[:, to], downs[part][at, :])
    second_hat, second_scale = norm_parts(hidden_ref[...])
    final = second_hat * second_gain + second_bias
    final_ref[...] = final[0:half].astype(BF16)
    mfinal_ref[...] = final[half:rows].astype(BF16)
    upstream = jnp.concatenate([cot_ref[mine, :], mup_ref[...]], axis=0).astype(F32)
    weighted = upstream * weight
    second_gain_grad = jnp.sum(second_hat * weighted, axis=0, keepdims=True)
    second_bias_grad = jnp.sum(weighted, axis=0, keepdims=True)
    second_back = norm_back(upstream * second_gain, second_hat, second_scale)
    fed = second_back.astype(BF16)
    fed_wide = fed.astype(F32) * weight
    down_bias_grad = jnp.sum(fed_wide, axis=0, keepdims=True)
    fed_ref[...] = fed
    hidden_ref[...] = second_back

    def narrow(k):
        at, to, part = parts_of[k]
        inner_refs[k % 2][...] = dot_nt(fed_ref[...], downs[part][at, :])

    bias_ref[...] = jnp.zeros_like(bias_ref)
    narrow(0)
    for k, (at, to, part) in enumerate(parts_of):
        if k + 1 < len(parts_of):
            narrow(k + 1)
        back = (inner_refs[k % 2][...] * slope_ref[:, to]).astype(BF16)
        backs_ref[:, to] = back
        owner = lax.rem(side + part, sides)
        bias_ref[pl.ds(owner * count + k % count, 1), :] = jnp.sum(
            back.astype(F32) * weight, axis=0, keepdims=True
        )
        hidden_ref[...] += dot_nt(backs_ref[:, to], ups[part][:, at])
    normed_back = hidden_ref[...]
    weighted_back = normed_back * weight
    first_gain_grad = jnp.sum(first_hat * weighted_back, axis=0, keepdims=True)
    first_bias_grad = jnp.sum(weighted_back, axis=0, keepdims=True)
    first_back = norm_back(normed_back * first_gain, first_hat, first_scale)
    first_ref[...] = first_back
    attended_back = first_back.astype(BF16)
    attended_wide = attended_back.astype(F32) * weight
    output_bias_grad = jnp.sum(attended_wide, axis=0, keepdims=True)
    back_ref[0:heads, :] = dot_nt(wo_a[...], attended_back).astype(BF16)
    back_ref[heads : 2 * heads, :] = dot_nt(wo_b[...], attended_back).astype(BF16)

    leaving = []
    for k, (l, u, apart) in enumerate(found):
        head = pl.multiple_of((apart * group + l) * HEAD, HEAD)
        leaving.append(
            remote(
                back_ref.at[pl.ds(head, HEAD), pl.ds(0, half)],
                do_ref.at[:, columns],
                dsend.at[k],
                drecv.at[k],
                (base + l, u),
            )
        )
    for copy in leaving:
        copy.start()
    head = pl.multiple_of(me * HEAD, HEAD)
    stays = pltpu.make_async_copy(
        back_ref.at[pl.ds(head, HEAD), pl.ds(0, half)], do_ref.at[:, columns], own
    )
    stays.start()
    mdo_ref[...] = back_ref[pl.ds(head, HEAD), half:rows]

    for k, value in enumerate(
        (
            output_bias_grad, first_gain_grad, first_bias_grad, down_bias_grad,
            second_gain_grad, second_bias_grad,
        )
    ):
        bias_ref[sides * count + k : sides * count + k + 1, :] = value
    filled = 2 * hidden + heads
    if filled < gown_ref.shape[0]:
        gown_ref[filled:, :] = jnp.zeros((gown_ref.shape[0] - filled, model), BF16)
        gpeer_ref[filled:, :] = jnp.zeros((gown_ref.shape[0] - filled, model), BF16)
    attended_low = attended_wide.astype(BF16)
    fed_low = fed_wide.astype(BF16)
    core = lax.rem(me, 2)
    beside = (base + core_partner(me), side)
    chips, size = hown_ref.shape[0], hown_ref.shape[1]
    sums = {}
    for part, grad_ref in ((1, gpeer_ref), (0, gown_ref)):
        for at, to, owner in parts_of:
            if owner != part:
                continue
            grad_ref[at, :] = dot(lowt_ref[...], backs_ref[:, to]).astype(BF16)
            grad_ref[hidden + at.start : hidden + at.stop, :] = dot(
                acted_ref[:, to].T, fed_low
            ).astype(BF16)
        grad_ref[2 * hidden : 2 * hidden + heads, :] = dot(
            mixed_t[part * heads : (part + 1) * heads, :], attended_low
        ).astype(BF16)
        sums[part] = []
        for p in range(chips):
            at = pl.ds(pl.multiple_of((2 * p + 1 - core) * size, size), size)
            slot = part * chips + p
            sums[part].append(
                remote(grad_ref.at[at, :], buffers.at[slot], csend.at[slot], crecv.at[slot], beside)
            )
            sums[part][-1].start()
    for part, grad_ref, total_ref in ((1, gpeer_ref, hpeer_ref), (0, gown_ref, hown_ref)):
        for p in range(chips):
            sums[part][p].wait()
            at = pl.ds(pl.multiple_of((2 * p + core) * size, size), size)
            total_ref[p] = (
                grad_ref[at, :].astype(F32) + buffers[part * chips + p].astype(F32)
            ).astype(BF16)
    stays.wait()
    for copy in leaving:
        copy.wait()


def middle(o, mstate, tokens, mem, cot, mcot, weights, vectors, bu_a, bu_b, group, sides, groups, half, grad_rows):
    model = tokens.shape[1]
    rows = half + MEMQ
    heads, hidden = weights[0].shape[0], weights[2].shape[1]
    near = group * sides - 1
    chips = groups * group // 2
    size = grad_rows // (2 * chips)
    dma = pltpu.SemaphoreType.DMA
    return pl.pallas_call(
        functools.partial(middle_kernel, group, sides, groups, half),
        out_shape=(
            jax.ShapeDtypeStruct((half, model), BF16),
            jax.ShapeDtypeStruct((MEMQ, model), BF16),
            jax.ShapeDtypeStruct((rows, model), F32),
            jax.ShapeDtypeStruct((HEAD, group * sides * half), BF16),
            jax.ShapeDtypeStruct((HEAD, MEMQ), BF16),
            jax.ShapeDtypeStruct((chips, size, model), BF16),
            jax.ShapeDtypeStruct((chips, size, model), BF16),
            jax.ShapeDtypeStruct((HEAD + 8, MEMQ), F32),
            jax.ShapeDtypeStruct((16, model), F32),
        ),
        in_specs=[vmem()] * 20,
        out_specs=(vmem(),) * 3 + (anyspace(),) + (vmem(),) * 5,
        scratch_shapes=[
            pltpu.VMEM((2 * heads, half), BF16),
            pltpu.VMEM((2 * heads, MEMQ), BF16),
            pltpu.VMEM((groups, SROWS, MEMQ), F32),
            pltpu.VMEM((HEAD, MEMQ), BF16),
            pltpu.VMEM((2 * heads, rows), BF16),
            pltpu.VMEM((grad_rows, model), BF16),
            pltpu.VMEM((grad_rows, model), BF16),
            pltpu.VMEM((2 * chips, size, model), BF16),
            pltpu.VMEM((rows, 2 * hidden), BF16),
            pltpu.VMEM((rows, 2 * hidden), F32),
            pltpu.VMEM((rows, 2 * hidden), BF16),
            pltpu.VMEM((rows, model), F32),
            pltpu.VMEM((rows, model), BF16),
            pltpu.VMEM((model, rows), BF16),
            pltpu.VMEM((rows, model), BF16),
            pltpu.VMEM((MEMQ, model), BF16),
            pltpu.VMEM((rows, model), F32),
            pltpu.VMEM((rows, model), F32),
            dma,
            dma((groups - 1,)), dma((groups - 1,)),
            dma((near,)), dma((near,)), dma((near,)), dma((near,)), dma((near,)), dma((near,)),
            dma((2 * chips,)), dma((2 * chips,)),
        ],
        compiler_params=pltpu.CompilerParams(
            collective_id=2, has_side_effects=True, vmem_limit_bytes=VMEM_LIMIT
        ),
        cost_estimate=pl.CostEstimate(
            flops=12 * rows * model * 2 * hidden, bytes_accessed=16 << 20, transcendentals=rows * hidden
        ),
        name="middle",
    )(o, mstate, tokens, mem, cot, mcot, *weights, *vectors, bu_a, bu_b)


def result_kernel(
    group, memory_rows, part_ref, other_ref, packs_ref, mems_ref, first_ref, sum_ref, final_ref,
    far_ref, mfinal_ref,
    out_token_ref, out_memory_ref, token_ref, memory_ref, query_ref, qbias_ref, key_ref, value_ref,
    vbias_ref, out_ref, up_ref, down_ref, upb_ref, *rest,
):
    small_refs, shared = rest[:-1], rest[-1]
    model = part_ref.shape[1]
    hidden, width = down_ref.shape[0], out_ref.shape[0]
    token_ref[...] = part_ref[...] + other_ref[...].astype(F32)
    side = lax.axis_index("wt")
    half = final_ref.shape[0]
    out_token_ref[pl.ds(pl.multiple_of(side * half, half), half), :] = final_ref[...]
    out_token_ref[pl.ds(pl.multiple_of((1 - side) * half, half), half), :] = far_ref[...]
    out_memory_ref[...] = mfinal_ref[0:memory_rows, :]
    rows = slice(3 * HEAD, 3 * HEAD + SHARED)
    total = packs_ref[0, rows, :].astype(F32) + mems_ref[0].astype(F32)
    for h in range(1, group):
        total = total + packs_ref[h, rows, :].astype(F32) + mems_ref[h].astype(F32)
    shared[...] = total
    begin = first_ref.shape[0] - MEMQ
    memory = shared[0:MEMK, :] + first_ref[begin : begin + MEMK, :]
    memory_ref[...] = memory[0:memory_rows, :]
    for at, ref in ((0, query_ref), (HEAD, key_ref), (2 * HEAD, value_ref)):
        for h in range(0, group, 2):
            both = jnp.concatenate(
                [packs_ref[h, at : at + HEAD, :], packs_ref[h + 1, at : at + HEAD, :]], axis=0
            )
            ref[:, h * HEAD : (h + 2) * HEAD] = both.T.astype(F32)
    row = 3 * HEAD + SHARED
    for at, ref in ((0, qbias_ref), (2 * HEAD, vbias_ref)):
        ref[...] = jnp.concatenate(
            [packs_ref[h, row : row + 1, at : at + HEAD].astype(F32) for h in range(group)], axis=1
        )
    chunks = hidden // model
    for k in range(chunks):
        up_ref[:, k * model : (k + 1) * model] = sum_ref[k * model : (k + 1) * model, :].astype(F32)
        upb_ref[:, k * model : (k + 1) * model] = shared[pl.ds(MEMK + side * chunks + k, 1), :]
    down_ref[...] = sum_ref[hidden : 2 * hidden, :].astype(F32)
    out_ref[...] = sum_ref[2 * hidden : 2 * hidden + width, :].astype(F32)
    for k, ref in enumerate(small_refs):
        at = MEMK + 2 * chunks + k
        ref[...] = shared[at : at + 1, :].reshape(model)


def results(part, other, packs, mems, first, total, final, far, mfinal, group, memory_rows, hidden):
    block, model = part.shape
    width = group * HEAD
    shape = lambda *dims: jax.ShapeDtypeStruct(dims, F32)
    return pl.pallas_call(
        functools.partial(result_kernel, group, memory_rows),
        out_shape=(
            jax.ShapeDtypeStruct((block, model), BF16),
            jax.ShapeDtypeStruct((memory_rows, model), BF16),
            shape(block, model), shape(memory_rows, model),
            shape(model, width), shape(1, width), shape(model, width), shape(model, width),
            shape(1, width), shape(width, model), shape(model, hidden), shape(hidden, model),
            shape(1, hidden),
        )
        + (shape(model),) * 6,
        in_specs=[vmem()] * 9,
        out_specs=(vmem(),) * 19,
        scratch_shapes=[pltpu.VMEM((SHARED, model), F32)],
        compiler_params=pltpu.CompilerParams(vmem_limit_bytes=VMEM_LIMIT),
        name="results",
    )(part, other, packs, mems, first, total, final, far, mfinal)


def local(
    tokens, memory, doc_starts, w_query, b_query, w_key, w_value, b_value, w_output, b_output,
    first_gain, first_bias, w_up, b_up, w_down, b_down, second_gain, second_bias,
    cotangent, mem_cotangent,
):
    block, model = tokens.shape
    memory_rows = memory.shape[0]
    docs = doc_starts.shape[0]
    width = w_query.shape[1]
    hidden = w_up.shape[1]
    group = width // HEAD
    ctx, sides = lax.axis_size("ctx"), lax.axis_size("wt")
    groups = ctx // group
    half = block // sides
    step = 16 * ctx
    grad_rows = (2 * hidden + width + step - 1) // step * step
    row = lambda a: a.reshape(1, a.shape[0])

    q, kv, out_b, up_b, bias_b, mq, mkv, mem_pad, w_pair, wq_t = scatter_heads(
        tokens, memory, w_query, b_query, w_key, w_value, b_value,
        w_output, w_up, b_up.reshape(8, hidden // 8), group,
    )
    forwards = [(i, i + group) for i in range(ctx - group)]
    backwards = [(i + group, i) for i in range(ctx - group)]
    swapped = [(i, (i + 1) % sides) for i in range(sides)]
    before = lax.ppermute(kv, "ctx", forwards)
    after = lax.ppermute(kv, "ctx", backwards)
    down_b = lax.ppermute(w_down, "wt", swapped)
    crossed = [(i, i ^ 2) for i in range(ctx)]
    neighbours = [(i, i ^ 1) for i in range(ctx)]
    late_tokens, kv = lax.optimization_barrier((tokens, kv))
    facing_tokens = lax.ppermute(late_tokens, "ctx", crossed)
    beside_tokens = lax.ppermute(late_tokens, "ctx", neighbours)

    state, mstate = forward_own(doc_starts, q, kv, mq, mkv, docs, memory_rows)
    state, facing_tokens, beside_tokens, down_b, before, after = lax.optimization_barrier(
        (state, facing_tokens, beside_tokens, down_b, before, after)
    )
    corner_tokens = lax.ppermute(facing_tokens, "ctx", neighbours)
    o, wide = forward_halo(doc_starts, q, before, after, state, docs)
    o, corner_tokens = lax.optimization_barrier((o, corner_tokens))
    final, mfinal, first_back, do, mdo, total_own, total_peer, mwide, biases = middle(
        o, mstate, tokens, mem_pad, cotangent, mem_cotangent,
        (w_output, out_b, w_up, up_b, w_down, down_b),
        [b_output, first_gain, first_bias, b_down, second_gain, second_bias],
        b_up, bias_b.reshape(hidden), group, sides, groups, half, grad_rows,
    )
    from_side = lax.ppermute(total_peer, "wt", swapped)

    part, dbefore, dafter = backward_halo(doc_starts, q, do, wide, before, after, docs)
    from_side, dbefore, dafter, final_late = lax.optimization_barrier(
        (from_side, dbefore, dafter, final)
    )
    size = grad_rows // ctx
    total = (total_own.astype(F32) + from_side.astype(F32)).reshape(groups, 2, size, model)
    row_half = lax.rem(lax.axis_index("ctx"), group) // 2
    leaving = lax.dynamic_index_in_dim(total, 1 - row_half, 1, False).astype(BF16)
    staying = lax.dynamic_index_in_dim(total, row_half, 1, False).astype(BF16)
    from_row = lax.ppermute(leaving, "ctx", crossed)
    from_after = lax.ppermute(dbefore, "ctx", backwards)
    from_before = lax.ppermute(dafter, "ctx", forwards)
    dq, dkv, dmq, dmkv, kt, delta, wide_dq = backward_first(
        doc_starts, q, do, wide, kv, part, mq, mdo, mwide, mkv, docs, memory_rows
    )
    from_row, from_after, from_before, dq, dkv = lax.optimization_barrier(
        (from_row, from_after, from_before, dq, dkv)
    )
    total = (staying.astype(F32) + from_row.astype(F32)).astype(BF16)
    columns = [[g * group + l for g in range(groups)] for l in range(group)]
    total = lax.all_to_all(total, "ctx", 0, 0, axis_index_groups=columns, tiled=True)
    far = lax.ppermute(lax.optimization_barrier((final_late, dq))[0], "wt", swapped)
    dq, dkv = backward_second(
        doc_starts, q, do, wide, kv, kt, delta, wide_dq, dq, dkv, docs
    )
    total, far, dq, dkv = lax.optimization_barrier((total, far, dq, dkv))
    piece = jnp.sum(total.astype(F32), axis=0).astype(BF16)
    part, other, packs, mems, total = tail(
        dq, dkv, from_after, from_before,
        (tokens, beside_tokens, facing_tokens, corner_tokens), dmq, dmkv, mem_pad, first_back, wq_t, w_pair,
        biases, piece, group, groups, sides, block,
    )
    total = total.reshape(grad_rows, model)
    (
        token_out, memory_out, token_grad, memory_grad, query_grad, query_bias, key_grad, value_grad,
        value_bias, out_grad, up_grad, down_grad, up_bias, *small,
    ) = results(
        part, other, packs, mems, first_back, total, final, far, mfinal, group, memory_rows, hidden
    )
    return (
        token_out, memory_out, token_grad, memory_grad,
        query_grad, query_bias.reshape(width), key_grad, value_grad, value_bias.reshape(width),
        out_grad, small[0], small[1], small[2],
        up_grad, up_bias.reshape(hidden), down_grad, small[3], small[4], small[5],
    )


def solution(mesh):
    placed = (
        P("ctx", None), P(), P(), P(None, "wt"), P("wt"), P(None, "wt"), P(None, "wt"), P("wt"),
        P("wt", None), P(), P(), P(), P(None, "wt"), P("wt"), P("wt", None), P(), P(), P(),
        P("ctx", None), P(),
    )
    return jax.shard_map(
        local,
        mesh=mesh,
        in_specs=placed,
        out_specs=(
            P("ctx", None), P(), P("ctx", None), P(), P(None, "wt"), P("wt"), P(None, "wt"),
            P(None, "wt"), P("wt"), P("wt", None), P(), P(), P(), P(None, "wt"), P("wt"),
            P("wt", None), P(), P(), P(),
        ),
        check_vma=False,
    )
```

```python
import functools

import jax
import jax.numpy as jnp
from jax import lax
from jax.experimental import pallas as pl
from jax.experimental.pallas import tpu as pltpu
from jax.sharding import PartitionSpec as P

HEAD = 64
EPSILON = 1e-05
MASKED = -1e30
MESH = pl.DeviceIdType.MESH
TQ = 512
TK = 512
MEMK = 32
MEMQ = 128
ONES = 16
VROWS = HEAD + ONES
SROWS = VROWS + 8
PACK = 256
BIAS = 128
CHUNKS = 4
AHEAD = 2
BIASES = 16
SHARED = MEMK + BIASES
GROUP = 4
F32 = jnp.float32
BF16 = jnp.bfloat16
VMEM_LIMIT = 56 * 1024 * 1024


def vmem():
    return pl.BlockSpec(memory_space=pltpu.VMEM)


def smem():
    return pl.BlockSpec(memory_space=pltpu.SMEM)


def anyspace():
    return pl.BlockSpec(memory_space=pl.ANY)


def dot(a, b):
    return jnp.dot(a, b, preferred_element_type=F32)


def dot_nt(a, b):
    return lax.dot_general(a, b, (((1,), (1,)), ((), ())), preferred_element_type=F32)


def greet(partners):
    barrier = pltpu.get_barrier_semaphore()
    for partner in partners:
        pl.semaphore_signal(barrier, inc=1, device_id=partner, device_id_type=MESH)
    pl.semaphore_wait(barrier, len(partners))


def remote(src, dst, send, recv, device):
    return pltpu.make_async_remote_copy(
        src_ref=src, dst_ref=dst, send_sem=send, recv_sem=recv, device_id=device, device_id_type=MESH
    )


def group_place(group):
    here = lax.axis_index("ctx")
    return here // group * group, lax.rem(here, group), lax.axis_index("wt")


def core_partner(me):
    return me + 1 - 2 * lax.rem(me, 2)


def scatter_kernel(
    group, block, tokens_ref, memory_ref, wq_ref, bq_ref, wk_ref, wv_ref, bv_ref,
    wo_ref, wu_ref, bu_ref,
    qo_ref, kvo_ref, wo_other, wu_other, bu_other, mq_ref, mkv_ref, mem_ref, wp_ref, wqt_ref,
    qs, kvs, bpair, bcol, own, send, recv, wsend, wrecv, fsend, frecv,
):
    base, me, side = group_place(group)
    width = 2 * HEAD
    partners = [(base + lax.rem(me + t, group), side) for t in range(1, group)]
    across = (base + me, lax.rem(side + 1, lax.axis_size("wt")))
    beside = (base + core_partner(me), side)
    greet(partners + [across])
    core = lax.rem(me, 2)
    rows_o, rows_u = wo_ref.shape[0] // 2, wu_ref.shape[0] // 2

    def part(ref, rows, which):
        return ref.at[pl.ds(pl.multiple_of(which * rows, rows), rows), :]

    firsts = [
        remote(part(wo_ref, rows_o, core), part(wo_other, rows_o, core), wsend.at[0], wrecv.at[0], across),
        remote(part(wu_ref, rows_u, core), part(wu_other, rows_u, core), wsend.at[1], wrecv.at[1], across),
        remote(bu_ref, bu_other, wsend.at[2], wrecv.at[2], across),
    ]
    for copy in firsts:
        copy.start()

    bq = bq_ref[...].astype(F32).reshape(1, bq_ref.shape[0])
    bv = bv_ref[...].astype(F32).reshape(1, bv_ref.shape[0])
    none = jnp.zeros((1, HEAD), F32)
    for h in range(group):
        at = slice(h * HEAD, (h + 1) * HEAD)
        wp_ref[:, h * width : (h + 1) * width] = jnp.concatenate([wk_ref[:, at], wv_ref[:, at]], axis=1)
        bpair[:, h * width : (h + 1) * width] = jnp.concatenate([none, bv[:, at]], axis=1)
    wqt_ref[...] = wq_ref[...].T
    bcol[...] = jnp.broadcast_to(bq, (BIAS, bq.shape[1])).T
    mem_ref[...] = jnp.zeros_like(mem_ref)
    mem_ref[0 : memory_ref.shape[0], :] = memory_ref[...]
    scale = HEAD ** (-0.5)

    def project(rows_value, head):
        lanes_at = pl.ds(pl.multiple_of(head * width, width), width)
        rows_at = pl.ds(pl.multiple_of(head * HEAD, HEAD), HEAD)
        pair = (dot(rows_value, wp_ref[:, lanes_at]) + bpair[:, lanes_at]).astype(BF16)
        query = (dot_nt(wqt_ref[rows_at, :], rows_value) + bcol[rows_at, 0:1]).astype(BF16)
        return pair, query * jnp.asarray(scale, BF16)

    copies = []
    mine_rows = pl.ds(pl.multiple_of(me * block, block), block)
    for k, t in enumerate((2, 1, 3) if group == 4 else range(1, group)):
        peer = lax.rem(me + t, group)
        pair, query = project(tokens_ref[...], peer)
        kvs[t] = pair
        qs[t] = query
        device = (base + peer, side)
        copies.append(remote(kvs.at[t], kvo_ref.at[mine_rows, :], send.at[2 * k], recv.at[2 * t - 2], device))
        copies.append(remote(qs.at[t], qo_ref.at[:, mine_rows], send.at[2 * k + 1], recv.at[2 * t - 1], device))
        copies[-2].start()
        copies[-1].start()
    pair, query = project(tokens_ref[...], me)
    kvs[0] = pair
    qs[0] = query
    mine = [
        pltpu.make_async_copy(kvs.at[0], kvo_ref.at[mine_rows, :], own.at[0]),
        pltpu.make_async_copy(qs.at[0], qo_ref.at[:, mine_rows], own.at[1]),
    ]
    for copy in mine:
        copy.start()
    pair, query = project(mem_ref[...], me)
    mkv_ref[...] = pair
    mq_ref[...] = query
    for copy in firsts:
        copy.wait()
    forwards = [
        remote(part(wo_other, rows_o, core), part(wo_other, rows_o, core), fsend.at[0], frecv.at[0], beside),
        remote(part(wu_other, rows_u, core), part(wu_other, rows_u, core), fsend.at[1], frecv.at[1], beside),
    ]
    for copy in forwards:
        copy.start()
    for copy in mine + copies + forwards:
        copy.wait()


def scatter_heads(tokens, memory, wq, bq, wk, wv, bv, wo, wu, bu, group):
    block, model = tokens.shape
    width = wq.shape[1]
    like = lambda a: jax.ShapeDtypeStruct(a.shape, a.dtype)
    return pl.pallas_call(
        functools.partial(scatter_kernel, group, block),
        out_shape=(
            jax.ShapeDtypeStruct((HEAD, group * block), BF16),
            jax.ShapeDtypeStruct((group * block, 2 * HEAD), BF16),
            like(wo), like(wu), like(bu),
            jax.ShapeDtypeStruct((HEAD, MEMQ), BF16),
            jax.ShapeDtypeStruct((MEMQ, 2 * HEAD), BF16),
            jax.ShapeDtypeStruct((MEMQ, model), BF16),
            jax.ShapeDtypeStruct((model, 2 * width), BF16),
            jax.ShapeDtypeStruct((width, model), BF16),
        ),
        in_specs=[vmem()] * 7 + [anyspace()] * 3,
        out_specs=(anyspace(),) * 5 + (vmem(),) * 5,
        scratch_shapes=[
            pltpu.VMEM((group, HEAD, block), BF16),
            pltpu.VMEM((group, block, 2 * HEAD), BF16),
            pltpu.VMEM((1, 2 * width), F32),
            pltpu.VMEM((width, BIAS), F32),
            pltpu.SemaphoreType.DMA((2,)),
            pltpu.SemaphoreType.DMA((2 * group - 2,)),
            pltpu.SemaphoreType.DMA((2 * group - 2,)),
            pltpu.SemaphoreType.DMA((3,)),
            pltpu.SemaphoreType.DMA((3,)),
            pltpu.SemaphoreType.DMA((2,)),
            pltpu.SemaphoreType.DMA((2,)),
        ],
        compiler_params=pltpu.CompilerParams(
            collective_id=0, has_side_effects=True, vmem_limit_bytes=VMEM_LIMIT
        ),
        name="scatter_heads",
    )(tokens, memory, wq, bq, wk, wv, bv, wo, wu, bu)


def tail_kernel(
    group, groups, sides, block, dq_ref, wide_ref, one_ref, two_ref, own_tokens, beside_tokens, facing_tokens, corner_tokens,
    dmq_ref, dmkv_ref,
    mem_ref, first_ref, wqt_ref, wp_ref, bias_ref, piece_ref,
    part_ref, other_ref, packs_ref, grads_ref,
    dkv_ref, left_ref, pack_ref, parts, sums, mems, qrows, kvrows, low, own, send, recv, rsend, rrecv, gsend, grecv,
    xsend, xrecv, psend, precv, msend, mrecv, zsend, zrecv, ysend, yrecv,
):
    base, me, side = group_place(group)
    number = base // group
    width = 2 * HEAD
    across = (base + me, lax.rem(side + 1, sides))
    partners = [(base + lax.rem(me + t, group), side) for t in range(1, group)]
    far = [(lax.rem(number + t, groups) * group + me, side) for t in range(1, groups)]
    greet(partners + far + [across])
    rows = PACK // groups
    reduces = []
    for t in range(1, groups):
        peer = lax.rem(number + t, groups)
        at = pl.ds(pl.multiple_of(peer * rows, rows), rows)
        reduces.append(
            remote(pack_ref.at[at, :], parts.at[t - 1], rsend.at[t - 1], rrecv.at[t - 1], far[t - 1])
        )
    chunk = block // CHUNKS
    head_rows = pl.ds(pl.multiple_of(me * HEAD, HEAD), HEAD)
    head_lanes = pl.ds(pl.multiple_of(me * width, width), width)
    moves = []
    for r in range(CHUNKS):
        step = []
        for t in range(1, group):
            peer = lax.rem(me + t, group)
            at = pl.ds(pl.multiple_of(peer * block + r * chunk, chunk), chunk)
            here = pl.ds(r * chunk, chunk)
            slot = (r * (group - 1) + t - 1) * 2
            step.append(
                remote(dkv_ref.at[at, :], kvrows.at[here, head_lanes], send.at[slot], recv.at[slot], partners[t - 1])
            )
            step.append(
                remote(dq_ref.at[:, at], qrows.at[head_rows, here], send.at[slot + 1], recv.at[slot + 1], partners[t - 1])
            )
        moves.append(step)
    span = group * block
    lifts = [
        remote(piece_ref, grads_ref.at[number, me], zsend.at[t - 1], zrecv.at[t - 1], far[t - 1])
        for t in range(1, groups)
    ]
    for copy in lifts:
        copy.start()

    def settle(k, carry):
        at = pl.ds(pl.multiple_of(k * block, block), block)
        dkv_ref[at, :] = (
            wide_ref[at, :] + one_ref[at, :].astype(F32) + two_ref[at, :].astype(F32)
        ).astype(BF16)
        return carry

    lax.fori_loop(0, group, settle, 0)
    for step in moves[:AHEAD]:
        for copy in step:
            copy.start()
    at = pl.ds(pl.multiple_of(me * block, block), block)
    mine = [
        pltpu.make_async_copy(dkv_ref.at[at, :], kvrows.at[:, head_lanes], own.at[0]),
        pltpu.make_async_copy(dq_ref.at[:, at], qrows.at[head_rows, :], own.at[1]),
        pltpu.make_async_copy(piece_ref, grads_ref.at[number, me], own.at[3]),
    ]
    for copy in mine:
        copy.start()
    left_ref[0:HEAD, :] = dq_ref[...]
    for k in range(span // 512):
        at = slice(k * 512, (k + 1) * 512)
        left_ref[HEAD : 3 * HEAD, at] = dkv_ref[at, :].T
    dmkv = dmkv_ref[...].astype(BF16)
    left = jnp.concatenate([dmq_ref[...], dmkv.T], axis=0)
    model = mem_ref.shape[1]
    product = dot(left, mem_ref[...])
    beside_at = core_partner(me)
    for owner, block_ref in (
        (me, own_tokens),
        (beside_at, beside_tokens),
        (lax.rem(me + 2, group), facing_tokens),
        (lax.rem(beside_at + 2, group), corner_tokens),
    ):
        at = pl.ds(pl.multiple_of(owner * block, block), block)
        product = product + dot(left_ref[:, at], block_ref[...])
    pack_ref[0 : 3 * HEAD, :] = product.astype(BF16)
    columns = dot(left_ref[...], jnp.ones((span, BIAS), BF16)) + jnp.sum(
        left.astype(F32), axis=1, keepdims=True
    )
    wq = wqt_ref[pl.ds(pl.multiple_of(me * HEAD, HEAD), HEAD), :]
    wp = wp_ref[:, pl.ds(pl.multiple_of(me * width, width), width)]
    memory_part = dot(dmq_ref[...].T, wq) + dot_nt(dmkv, wp)
    pack_ref[3 * HEAD : 3 * HEAD + MEMK, :] = memory_part[0:MEMK, :].astype(BF16)
    pack_ref[3 * HEAD + MEMK : 3 * HEAD + SHARED, :] = bias_ref[...].astype(BF16)
    rest = PACK - 3 * HEAD - SHARED
    turned = columns.T[0:rest, :]
    pack_ref[3 * HEAD + SHARED : PACK, :] = jnp.concatenate(
        [turned, jnp.zeros((rest, model - 3 * HEAD), F32)], axis=1
    ).astype(BF16)
    memory = pl.ds(3 * HEAD, SHARED)
    exchange = remote(pack_ref.at[memory, :], mems, msend, mrecv, across)
    exchange.start()
    for copy in mine:
        copy.wait()
    swaps, spread = [], []
    half = block // sides
    here = pl.ds(pl.multiple_of(number * rows, rows), rows)

    def reduced():
        total = pack_ref[here, :].astype(F32)
        for t in range(1, groups):
            reduces[t - 1].wait()
            total = total + parts[t - 1].astype(F32)
        sums[here, :] = total.astype(BF16)
        for t in range(1, groups):
            spread.append(
                remote(sums.at[here, :], sums.at[here, :], gsend.at[t - 1], grecv.at[t - 1], far[t - 1])
            )
            spread[-1].start()

    beside = (base + core_partner(me), side)
    opposite = lax.rem(me + 2, group)
    facing = (base + opposite, side)
    first = [
        remote(sums, packs_ref.at[me], psend.at[0], precv.at[0], facing),
        remote(sums, packs_ref.at[me], psend.at[1], precv.at[1], beside),
    ]
    last = pltpu.make_async_copy(sums, packs_ref.at[me], own.at[2])

    second = remote(
        packs_ref.at[opposite], packs_ref.at[opposite], psend.at[2], precv.at[2], beside
    )

    def shifted(slot, k, which, device):
        return remote(
            grads_ref.at[slot, which], grads_ref.at[slot, which], ysend.at[k], yrecv.at[k], device
        )

    def came(t):
        return lax.rem(number - t + groups, groups)

    sideways, passed = [], []
    for r in range(CHUNKS):
        for copy in moves[r]:
            copy.wait()
        if r + AHEAD < CHUNKS:
            for copy in moves[r + AHEAD]:
                copy.start()
        at = pl.ds(r * chunk, chunk)
        value = dot(qrows[:, at].T, wqt_ref[...]) + dot_nt(kvrows[at, :], wp_ref[...])
        inside = (r * chunk) // half
        extra = first_ref[pl.ds(r * chunk - inside * half, chunk), :]
        value = value + extra * (side == inside).astype(F32)
        part_ref[at, :] = value
        low[at, :] = value.astype(BF16)
        swaps.append(remote(low.at[at, :], other_ref.at[at, :], xsend.at[r], xrecv.at[r], across))
        swaps[-1].start()
        if r == 0:
            exchange.wait()
            pack_ref[memory, :] = (
                pack_ref[memory, :].astype(F32) + mems[...].astype(F32)
            ).astype(BF16)
            for copy in reduces:
                copy.start()
        if r == 2:
            reduced()
            for copy in lifts:
                copy.wait()
            for t in range(groups):
                slot = came(t)
                sideways.append((shifted(slot, t, me, facing), shifted(slot, groups + t, me, beside)))
                for copy in sideways[t]:
                    copy.start()
    for copy in spread:
        copy.wait()
    for copy in first:
        copy.start()
    last.start()
    for t in range(groups):
        sideways[t][0].wait()
        passed.append(shifted(came(t), 2 * groups + t, opposite, beside))
        passed[t].start()
    first[0].wait()
    second.start()
    last.wait()
    first[1].wait()
    second.wait()
    for t in range(groups):
        sideways[t][1].wait()
        passed[t].wait()
    for copy in swaps:
        copy.wait()


def tail(dq, dkv, one, two, blocks, dmq, dmkv, mem, first, wqt, wp, biases, piece, group, groups, sides, block):
    model = first.shape[1]
    width = wqt.shape[0]
    moves = CHUNKS * (group - 1) * 2
    return pl.pallas_call(
        functools.partial(tail_kernel, group, groups, sides, block),
        out_shape=(
            jax.ShapeDtypeStruct((block, model), F32),
            jax.ShapeDtypeStruct((block, model), BF16),
            jax.ShapeDtypeStruct((group, PACK, model), BF16),
            jax.ShapeDtypeStruct((groups, group) + piece.shape, BF16),
        ),
        in_specs=[vmem()] * 15 + [anyspace()],
        out_specs=(vmem(),) + (anyspace(),) * 3,
        scratch_shapes=[
            pltpu.VMEM((group * block, 2 * HEAD), BF16),
            pltpu.VMEM((3 * HEAD, group * block), BF16),
            pltpu.VMEM((PACK, model), BF16),
            pltpu.VMEM((groups - 1, PACK // groups, model), BF16),
            pltpu.VMEM((PACK, model), BF16),
            pltpu.VMEM((SHARED, model), BF16),
            pltpu.VMEM((width, block), BF16),
            pltpu.VMEM((block, 2 * width), BF16),
            pltpu.VMEM((block, model), BF16),
            pltpu.SemaphoreType.DMA((4,)),
            pltpu.SemaphoreType.DMA((moves,)),
            pltpu.SemaphoreType.DMA((moves,)),
            pltpu.SemaphoreType.DMA((groups - 1,)),
            pltpu.SemaphoreType.DMA((groups - 1,)),
            pltpu.SemaphoreType.DMA((groups - 1,)),
            pltpu.SemaphoreType.DMA((groups - 1,)),
            pltpu.SemaphoreType.DMA((CHUNKS,)),
            pltpu.SemaphoreType.DMA((CHUNKS,)),
            pltpu.SemaphoreType.DMA((3,)),
            pltpu.SemaphoreType.DMA((3,)),
            pltpu.SemaphoreType.DMA,
            pltpu.SemaphoreType.DMA,
            pltpu.SemaphoreType.DMA((groups - 1,)),
            pltpu.SemaphoreType.DMA((groups - 1,)),
            pltpu.SemaphoreType.DMA((3 * groups,)),
            pltpu.SemaphoreType.DMA((3 * groups,)),
        ],
        compiler_params=pltpu.CompilerParams(
            collective_id=1, has_side_effects=True, vmem_limit_bytes=VMEM_LIMIT
        ),
        name="tail",
    )(dq, dkv, one, two, *blocks, dmq, dmkv, mem, first, wqt, wp, biases, piece)


def near_partners(group, sides):
    base, me, side = group_place(group)
    found = []
    for u in range(sides):
        for t in range(group):
            if t or u:
                found.append((lax.rem(me + t, group), lax.rem(side + u, sides), u))
    return base, me, side, found


def span_place(span):
    block = span // GROUP
    return lax.axis_size("ctx") * block, lax.axis_index("ctx") // GROUP * span


def doc_bounds(starts_ref, docs, first, last, total):
    low = starts_ref[0]
    low_end = total
    top = starts_ref[0]
    high = total
    for d in range(docs):
        start = starts_ref[d]
        low = jnp.where(start <= first, start, low)
        top = jnp.where(start <= last, start, top)
    for d in range(docs - 1, -1, -1):
        start = starts_ref[d]
        low_end = jnp.where(start > first, start, low_end)
        high = jnp.where(start > last, start, high)
    return low, low_end, top, high


def doc_rows(starts_ref, docs, first, total):
    place = first + lax.broadcasted_iota(jnp.int32, (1, TQ), 1)
    low = jnp.zeros((1, TQ), jnp.int32)
    high = jnp.full((1, TQ), total, jnp.int32)
    for d in range(docs):
        start = starts_ref[d]
        low = jnp.where(place >= start, start, low)
    for d in range(docs - 1, -1, -1):
        start = starts_ref[d]
        high = jnp.where(place < start, start, high)
    return low, high


def allowed_block(key_first, low, high):
    place = lax.broadcasted_iota(jnp.int32, (TK, TQ), 0) - (low - key_first)
    return place.astype(jnp.uint32) < (high - low).astype(jnp.uint32)


def tile(ref, number, size):
    return ref[pl.ds(pl.multiple_of(number * size, size), size), :]


def lanes(ref, number, size):
    return ref[:, pl.ds(pl.multiple_of(number * size, size), size)]


def pad_query(q, size):
    return jnp.concatenate([q, jnp.zeros((HEAD, size), BF16)], axis=0)


def fill_values(kv_ref, va, column, begin, end):
    def step(k, carry):
        turned = tile(kv_ref, k, TK).T
        at = pl.ds(pl.multiple_of(column + k * TK, TK), TK)
        va[0:HEAD, at] = turned[HEAD : 2 * HEAD, :]
        va[HEAD:VROWS, at] = jnp.ones((ONES, TK), BF16)
        return carry

    lax.fori_loop(begin, end, step, 0)


def key_range(bounds, kv_first, count):
    begin = jnp.clip(bounds[0] - kv_first, 0, count) // TK
    end = (jnp.clip(bounds[3] - kv_first, 0, count) + TK - 1) // TK
    return begin, end


def pair_loop(bounds, begin, end, kv_first, low, high, score, use):
    doc_first, doc_first_end, doc_last, doc_end = bounds
    single = doc_first == doc_last

    @pl.when(begin < end)
    def _():
        score(0, begin)

        def step(i, carry):
            k = begin + 2 * i
            at = kv_first + k * TK
            both = k + 1 < end
            whole = single & both & (at >= doc_first) & (at + 2 * TK <= doc_end)

            @pl.when(whole)
            def _():
                score(1, k + 1)
                use(0, k, None)
                score(0, k + 2)
                use(1, k + 1, None)

            @pl.when(jnp.logical_not(whole) & both)
            def _():
                score(1, k + 1)
                use(0, k, allowed_block(at, low, high))
                score(0, k + 2)
                use(1, k + 1, allowed_block(at + TK, low, high))

            @pl.when(jnp.logical_not(both))
            def _():
                use(0, k, allowed_block(at, low, high))

            return carry

        lax.fori_loop(0, (end - begin + 1) // 2, step, 0)


def online(score, value, acc, top):
    old = top[0:1, :]
    new = jnp.maximum(old, jnp.max(score, axis=0, keepdims=True))
    share = jnp.exp(score - new).astype(BF16)
    acc[...] = acc[...] * jnp.exp(old - new) + dot(value, share)
    top[...] = jnp.broadcast_to(new, top.shape)


def forward_tiles(bounds, low, high, kv_ref, kv_first, va, va_column, qz, acc, top, held):
    begin, end = key_range(bounds, kv_first, kv_ref.shape[0])

    def score(slot, k):
        held[slot][...] = dot(tile(kv_ref, jnp.minimum(k, end - 1), TK), qz)

    def use(slot, k, allowed):
        at = pl.ds(pl.multiple_of(va_column + k * TK, TK), TK)
        score = held[slot][...]
        if allowed is not None:
            score = jnp.where(allowed, score, MASKED)
        online(score, va[:, at], acc, top)

    pair_loop(bounds, begin, end, kv_first, low, high, score, use)


def forward_own_kernel(
    docs, span, memory_rows, meta_ref, q_ref, kv_ref, mq_ref, mkv_ref,
    state_ref, mstate_ref, va, acc, top, held0, held1,
):
    total, base = span_place(span)
    fill_values(kv_ref, va, 0, 0, span // TK)
    turned = mkv_ref[...].T
    mem_value = jnp.concatenate(
        [turned[HEAD : 2 * HEAD, 0:MEMK], jnp.ones((ONES, MEMK), BF16)], axis=0
    )
    score = dot(mkv_ref[0:MEMK, 0:HEAD], q_ref[...])
    inside = lax.broadcasted_iota(jnp.int32, score.shape, 0) < memory_rows
    score = jnp.where(inside, score, MASKED)
    new = jnp.max(score, axis=0, keepdims=True)
    state_ref[0:VROWS, :] = dot(mem_value, jnp.exp(score - new).astype(BF16))
    state_ref[VROWS:SROWS, :] = jnp.broadcast_to(new, (8, span))

    def query_step(qi, carry):
        first = base + qi * TQ
        bounds = doc_bounds(meta_ref, docs, first, first + TQ - 1, total)
        low, high = doc_rows(meta_ref, docs, first, total)
        at = pl.ds(pl.multiple_of(qi * TQ, TQ), TQ)
        qz = pad_query(q_ref[:, at], TQ)
        acc[...] = state_ref[0:VROWS, at]
        top[...] = state_ref[VROWS:SROWS, at]
        forward_tiles(bounds, low, high, kv_ref, base, va, 0, qz, acc, top, (held0, held1))
        state_ref[0:VROWS, at] = acc[...]
        state_ref[VROWS:SROWS, at] = top[...]
        return carry

    lax.fori_loop(0, span // TQ, query_step, 0)

    score = dot(kv_ref[...], pad_query(mq_ref[...], MEMQ))
    new = jnp.max(score, axis=0, keepdims=True)
    mstate_ref[0:VROWS, :] = dot(va[...], jnp.exp(score - new).astype(BF16))
    mstate_ref[VROWS:SROWS, :] = jnp.broadcast_to(new, (8, MEMQ))


def forward_own(meta, q, kv, mq, mkv, docs, memory_rows):
    count = kv.shape[0]
    return pl.pallas_call(
        functools.partial(forward_own_kernel, docs, count, memory_rows),
        out_shape=(
            jax.ShapeDtypeStruct((SROWS, count), F32),
            jax.ShapeDtypeStruct((SROWS, MEMQ), F32),
        ),
        in_specs=[smem()] + [vmem()] * 4,
        out_specs=(vmem(), vmem()),
        scratch_shapes=[
            pltpu.VMEM((VROWS, count), BF16),
            pltpu.VMEM((VROWS, TQ), F32),
            pltpu.VMEM((8, TQ), F32),
            pltpu.VMEM((TK, TQ), F32),
            pltpu.VMEM((TK, TQ), F32),
        ],
        compiler_params=pltpu.CompilerParams(vmem_limit_bytes=VMEM_LIMIT),
        cost_estimate=pl.CostEstimate(
            flops=8 * count * count * HEAD, bytes_accessed=4 << 20, transcendentals=count * count
        ),
        name="forward_own",
    )(meta, q, kv, mq, mkv)


def halo_ranges(meta_ref, docs, base, span, total):
    first = doc_bounds(meta_ref, docs, base, base + span - 1, total)
    before = jnp.clip(first[0] - (base - span), 0, span) // TK
    after = (jnp.clip(first[3] - (base + span), 0, span) + TK - 1) // TK
    return before, after


def forward_halo_kernel(
    docs, span, meta_ref, q_ref, before_ref, after_ref, state_ref, o_ref, wide_ref,
    va, acc, top, held0, held1,
):
    total, base = span_place(span)
    count = before_ref.shape[0]
    from_before, to_after = halo_ranges(meta_ref, docs, base, span, total)
    fill_values(before_ref, va, 0, from_before, span // TK)
    fill_values(after_ref, va, count, 0, to_after)
    held = (held0, held1)

    def query_step(qi, carry):
        first = base + qi * TQ
        bounds = doc_bounds(meta_ref, docs, first, first + TQ - 1, total)
        low, high = doc_rows(meta_ref, docs, first, total)
        at = pl.ds(pl.multiple_of(qi * TQ, TQ), TQ)
        qz = pad_query(q_ref[:, at], TQ)
        acc[...] = state_ref[0:VROWS, at]
        top[...] = state_ref[VROWS:SROWS, at]
        forward_tiles(bounds, low, high, before_ref, base - count, va, 0, qz, acc, top, held)
        forward_tiles(bounds, low, high, after_ref, base + count, va, count, qz, acc, top, held)
        mass = acc[HEAD : HEAD + 1, :]
        wide = acc[0:HEAD, :] / mass
        o_ref[:, at] = wide.astype(BF16)
        wide_ref[0:HEAD, at] = wide
        wide_ref[HEAD : HEAD + 8, at] = top[...] + jnp.log(jnp.broadcast_to(mass, top.shape))
        return carry

    lax.fori_loop(0, span // TQ, query_step, 0)


def forward_halo(meta, q, before, after, state, docs):
    count = before.shape[0]
    return pl.pallas_call(
        functools.partial(forward_halo_kernel, docs, count),
        out_shape=(
            jax.ShapeDtypeStruct((HEAD, count), BF16),
            jax.ShapeDtypeStruct((HEAD + 8, count), F32),
        ),
        in_specs=[smem()] + [vmem()] * 4,
        out_specs=(vmem(), vmem()),
        scratch_shapes=[
            pltpu.VMEM((VROWS, 2 * count), BF16),
            pltpu.VMEM((VROWS, TQ), F32),
            pltpu.VMEM((8, TQ), F32),
            pltpu.VMEM((TK, TQ), F32),
            pltpu.VMEM((TK, TQ), F32),
        ],
        compiler_params=pltpu.CompilerParams(vmem_limit_bytes=VMEM_LIMIT),
        cost_estimate=pl.CostEstimate(
            flops=4 * count * count * HEAD, bytes_accessed=6 << 20, transcendentals=count * count
        ),
        name="forward_halo",
    )(meta, q, before, after, state)


def backward_tiles(
    bounds, low, high, kv_ref, kv_first, kt, kt_column, grad, sides, stats, acc, held
):
    qz, doz, qr, dor = sides
    log_total, delta = stats
    begin, end = key_range(bounds, kv_first, kv_ref.shape[0])

    def score(slot, k):
        pair = tile(kv_ref, jnp.minimum(k, end - 1), TK)
        held[slot][...] = dot(pair, qz)
        held[slot + 2][...] = dot(pair, doz)

    def use(slot, k, allowed):
        at = pl.ds(pl.multiple_of(kt_column + k * TK, TK), TK)
        share = jnp.exp(held[slot][...] - log_total)
        if allowed is not None:
            share = jnp.where(allowed, share, 0.0)
        back = (share * (held[slot + 2][...] - delta)).astype(BF16)
        grad[at, :] += dot(back, qr) + dot(share.astype(BF16), dor)
        acc[...] += dot(kt[:, at], back)

    pair_loop(bounds, begin, end, kv_first, low, high, score, use)


def fill_keys(kv_ref, kt, column, begin, end):
    def step(k, carry):
        turned = tile(kv_ref, k, TK).T
        kt[:, pl.ds(pl.multiple_of(column + k * TK, TK), TK)] = turned[0:HEAD, :]
        return carry

    lax.fori_loop(begin, end, step, 0)


def query_sides(q, do, size):
    zero = jnp.zeros((HEAD, size), BF16)
    qz = jnp.concatenate([q, zero], axis=0)
    doz = jnp.concatenate([zero, do], axis=0)
    return qz, doz, qz.T, doz.T


def row_stats(wide, do):
    return wide[HEAD : HEAD + 1, :], jnp.sum(
        wide[0:HEAD, :] * do.astype(F32), axis=0, keepdims=True
    )


def backward_halo_kernel(
    docs, span, meta_ref, q_ref, do_ref, wide_ref, before_ref, after_ref,
    dq_ref, dbefore_ref, dafter_ref, kt, grad, acc, *held,
):
    total, base = span_place(span)
    count = before_ref.shape[0]
    from_before, to_after = halo_ranges(meta_ref, docs, base, span, total)
    fill_keys(before_ref, kt, 0, from_before, span // TK)
    fill_keys(after_ref, kt, count, 0, to_after)

    def clear(k, carry):
        grad[pl.ds(pl.multiple_of(k * TK, TK), TK), :] = jnp.zeros((TK, 2 * HEAD), F32)
        return carry

    lax.fori_loop(from_before, span // TK + to_after, clear, 0)

    def query_step(qi, carry):
        first = base + qi * TQ
        bounds = doc_bounds(meta_ref, docs, first, first + TQ - 1, total)
        low, high = doc_rows(meta_ref, docs, first, total)
        at = pl.ds(pl.multiple_of(qi * TQ, TQ), TQ)
        acc[...] = jnp.zeros_like(acc)

        @pl.when((bounds[0] < base) | (bounds[3] > base + count))
        def _():
            do = do_ref[:, at]
            sides = query_sides(q_ref[:, at], do, TQ)
            stats = row_stats(wide_ref[:, at], do)
            for ref, begin, column in (
                (before_ref, base - count, 0),
                (after_ref, base + count, count),
            ):
                backward_tiles(
                    bounds, low, high, ref, begin, kt, column, grad, sides, stats, acc, held
                )

        dq_ref[:, at] = acc[...]
        return carry

    lax.fori_loop(0, span // TQ, query_step, 0)
    dbefore_ref[...] = jnp.zeros_like(dbefore_ref)
    dafter_ref[...] = jnp.zeros_like(dafter_ref)

    def keep_before(k, carry):
        at = pl.ds(pl.multiple_of(k * TK, TK), TK)
        dbefore_ref[at, :] = grad[at, :].astype(BF16)
        return carry

    def keep_after(k, carry):
        at = pl.ds(pl.multiple_of(k * TK, TK), TK)
        dafter_ref[at, :] = grad[pl.ds(pl.multiple_of(count + k * TK, TK), TK), :].astype(BF16)
        return carry

    lax.fori_loop(from_before, span // TK, keep_before, 0)
    lax.fori_loop(0, to_after, keep_after, 0)


def backward_halo(meta, q, do, wide, before, after, docs):
    count = before.shape[0]
    return pl.pallas_call(
        functools.partial(backward_halo_kernel, docs, count),
        out_shape=(
            jax.ShapeDtypeStruct((HEAD, count), F32),
            jax.ShapeDtypeStruct((count, 2 * HEAD), BF16),
            jax.ShapeDtypeStruct((count, 2 * HEAD), BF16),
        ),
        in_specs=[smem()] + [vmem()] * 5,
        out_specs=(vmem(),) * 3,
        scratch_shapes=[
            pltpu.VMEM((HEAD, 2 * count), BF16),
            pltpu.VMEM((2 * count, 2 * HEAD), F32),
            pltpu.VMEM((HEAD, TQ), F32),
        ]
        + [pltpu.VMEM((TK, TQ), F32)] * 4,
        compiler_params=pltpu.CompilerParams(vmem_limit_bytes=VMEM_LIMIT),
        cost_estimate=pl.CostEstimate(
            flops=8 * count * count * HEAD, bytes_accessed=8 << 20, transcendentals=count * count
        ),
        name="backward_halo",
    )(meta, q, do, wide, before, after)


def backward_queries(
    docs, span, first_tile, last_tile, meta_ref, q_ref, do_ref, wide_ref, kv_ref,
    dq_ref, grad, kt, acc, delta_ref, wide_dq, held,
):
    total, base = span_place(span)
    scale = HEAD ** (-0.5)

    def query_step(qi, carry):
        first = base + qi * TQ
        bounds = doc_bounds(meta_ref, docs, first, first + TQ - 1, total)
        low, high = doc_rows(meta_ref, docs, first, total)
        at = pl.ds(pl.multiple_of(qi * TQ, TQ), TQ)
        sides = query_sides(q_ref[:, at], do_ref[:, at], TQ)
        stats = wide_ref[HEAD : HEAD + 1, at], delta_ref[0:1, at]
        acc[...] = wide_dq[:, at]
        backward_tiles(bounds, low, high, kv_ref, base, kt, 0, grad, sides, stats, acc, held)
        dq_ref[:, at] = (acc[...] * scale).astype(BF16)
        return carry

    lax.fori_loop(first_tile, last_tile, query_step, 0)


def backward_first_kernel(
    docs, span, memory_rows, meta_ref, q_ref, do_ref, wide_ref, kv_ref, part_ref,
    mq_ref, mdo_ref, mwide_ref, mkv_ref,
    dq_ref, grad, dmq_ref, mgrad, kt, delta_ref, wide_dq, acc, *held,
):
    fill_keys(kv_ref, kt, 0, 0, span // TK)
    scale = HEAD ** (-0.5)

    delta_ref[...] = jnp.broadcast_to(
        jnp.sum(wide_ref[0:HEAD, :] * do_ref[...].astype(F32), axis=0, keepdims=True), (8, span)
    )
    score = dot(mkv_ref[0:MEMK, 0:HEAD], q_ref[...])
    inside = lax.broadcasted_iota(jnp.int32, score.shape, 0) < memory_rows
    share = jnp.exp(jnp.where(inside, score, MASKED) - wide_ref[HEAD : HEAD + 1, :])
    slope = dot(mkv_ref[0:MEMK, HEAD : 2 * HEAD], do_ref[...])
    back = (share * (slope - delta_ref[0:1, :])).astype(BF16)
    mgrad[...] = jnp.zeros_like(mgrad)
    mgrad[0:MEMK, :] = jnp.concatenate(
        [dot_nt(back, q_ref[...]), dot_nt(share.astype(BF16), do_ref[...])], axis=1
    )
    mem_key = mkv_ref[...].T[0:HEAD, 0:MEMK]
    wide_dq[...] = part_ref[...] + dot(mem_key, back)

    mdo = mdo_ref[...]
    qz, doz, qr, dor = query_sides(mq_ref[...], mdo, MEMQ)
    log_total, delta = row_stats(mwide_ref[...], mdo)
    share = jnp.exp(dot(kv_ref[...], qz) - log_total)
    back = (share * (dot(kv_ref[...], doz) - delta)).astype(BF16)
    grad[...] = dot(back, qr) + dot(share.astype(BF16), dor)
    dmq_ref[...] = (dot(kt[...], back) * scale).astype(BF16)
    dq_ref[:, span // 2 :] = jnp.zeros((HEAD, span // 2), BF16)
    backward_queries(
        docs, span, 0, span // TQ // 2, meta_ref, q_ref, do_ref, wide_ref, kv_ref,
        dq_ref, grad, kt, acc, delta_ref, wide_dq, held,
    )


def backward_second_kernel(
    docs, span, meta_ref, q_ref, do_ref, wide_ref, kv_ref, kt, delta_ref, wide_dq, dq_in, grad_in,
    dq_ref, grad, acc, *held,
):
    dq_ref[...] = dq_in[...]
    grad[...] = grad_in[...]
    backward_queries(
        docs, span, span // TQ // 2, span // TQ, meta_ref, q_ref, do_ref, wide_ref, kv_ref,
        dq_ref, grad, kt, acc, delta_ref, wide_dq, held,
    )


def backward_first(meta, q, do, wide, kv, part, mq, mdo, mwide, mkv, docs, memory_rows):
    count = kv.shape[0]
    return pl.pallas_call(
        functools.partial(backward_first_kernel, docs, count, memory_rows),
        out_shape=(
            jax.ShapeDtypeStruct((HEAD, count), BF16),
            jax.ShapeDtypeStruct((count, 2 * HEAD), F32),
            jax.ShapeDtypeStruct((HEAD, MEMQ), BF16),
            jax.ShapeDtypeStruct((MEMQ, 2 * HEAD), F32),
            jax.ShapeDtypeStruct((HEAD, count), BF16),
            jax.ShapeDtypeStruct((8, count), F32),
            jax.ShapeDtypeStruct((HEAD, count), F32),
        ),
        in_specs=[smem()] + [vmem()] * 9,
        out_specs=(vmem(),) * 7,
        scratch_shapes=[pltpu.VMEM((HEAD, TQ), F32)] + [pltpu.VMEM((TK, TQ), F32)] * 4,
        compiler_params=pltpu.CompilerParams(vmem_limit_bytes=VMEM_LIMIT),
        cost_estimate=pl.CostEstimate(
            flops=8 * count * count * HEAD, bytes_accessed=8 << 20, transcendentals=count * count
        ),
        name="backward_first",
    )(meta, q, do, wide, kv, part, mq, mdo, mwide, mkv)


def backward_second(meta, q, do, wide, kv, kt, delta, wide_dq, dq, grad, docs):
    count = kv.shape[0]
    return pl.pallas_call(
        functools.partial(backward_second_kernel, docs, count),
        out_shape=(
            jax.ShapeDtypeStruct((HEAD, count), BF16),
            jax.ShapeDtypeStruct((count, 2 * HEAD), F32),
        ),
        in_specs=[smem()] + [vmem()] * 9,
        out_specs=(vmem(),) * 2,
        scratch_shapes=[pltpu.VMEM((HEAD, TQ), F32)] + [pltpu.VMEM((TK, TQ), F32)] * 4,
        compiler_params=pltpu.CompilerParams(vmem_limit_bytes=VMEM_LIMIT),
        cost_estimate=pl.CostEstimate(
            flops=8 * count * count * HEAD, bytes_accessed=8 << 20, transcendentals=count * count
        ),
        name="backward_second",
    )(meta, q, do, wide, kv, kt, delta, wide_dq, dq, grad)


def mean(value):
    return jnp.mean(value, axis=-1, keepdims=True)


def norm_parts(value):
    centered = value - mean(value)
    scale = lax.rsqrt(mean(centered * centered) + EPSILON)
    return centered * scale, scale


def norm_back(back, hat, scale):
    return scale * (back - mean(back) - hat * mean(back * hat))


def middle_kernel(
    group, sides, groups, half,
    o_ref, mstate_ref, tokens_ref, mem_ref, cot_ref, mcot_ref,
    wo_a, wo_b, wu_a, wu_b, wd_a, wd_b, bo_ref, fg_ref, fb_ref, bd_ref, sg_ref, sb_ref, bu_a, bu_b,
    final_ref, mfinal_ref, first_ref, do_ref, mdo_ref, hown_ref, hpeer_ref, sum_ref, bias_ref,
    mixed_ref, memt_ref, parts, memt, back_ref, gown_ref, gpeer_ref, buffers,
    acted_ref, slope_ref, backs_ref, hidden_ref, low_ref, lowt_ref, fed_ref, mup_ref,
    inner_0, inner_1,
    own, psend, precv, send, recv, msend, mrecv, dsend, drecv, csend, crecv,
):
    inner_refs = (inner_0, inner_1)
    base, me, side, found = near_partners(group, sides)
    number = base // group
    far = [(lax.rem(number + t, groups) * group + me, side) for t in range(1, groups)]
    greet([(base + l, u) for l, u, apart in found] + far)
    exchanges = [
        remote(mstate_ref, parts.at[t], psend.at[t - 1], precv.at[t - 1], far[t - 1])
        for t in range(1, groups)
    ]
    for copy in exchanges:
        copy.start()

    def rows_of(apart):
        slot = (sides - apart) % sides * group
        return pl.ds(pl.multiple_of((slot + me) * HEAD, HEAD), HEAD)

    copies = []
    for k, (l, u, apart) in enumerate(found):
        start = pl.multiple_of((l * sides + u) * half, half)
        copies.append(
            remote(
                o_ref.at[:, pl.ds(start, half)],
                mixed_ref.at[rows_of(apart), :],
                send.at[k],
                recv.at[k],
                (base + l, u),
            )
        )
    for copy in copies:
        copy.start()
    columns = pl.ds(pl.multiple_of((me * sides + side) * half, half), half)
    mixed_ref[rows_of(0), :] = o_ref[:, columns]
    parts[0] = mstate_ref[...]
    for copy in exchanges:
        copy.wait()
    top = parts[0, VROWS : VROWS + 1, :]
    for t in range(1, groups):
        top = jnp.maximum(top, parts[t, VROWS : VROWS + 1, :])
    total = jnp.zeros((VROWS, MEMQ), F32)
    for t in range(groups):
        total = total + parts[t, 0:VROWS, :] * jnp.exp(parts[t, VROWS : VROWS + 1, :] - top)
    mass = total[HEAD : HEAD + 1, :]
    wide = total[0:HEAD, :] / mass
    sum_ref[0:HEAD, :] = wide
    sum_ref[HEAD : HEAD + 8, :] = jnp.broadcast_to(top + jnp.log(mass), (8, MEMQ))
    memt[...] = wide.astype(BF16)
    memt_ref[rows_of(0), :] = memt[...]
    more = []
    for k, (l, u, apart) in enumerate(found):
        more.append(
            remote(memt, memt_ref.at[rows_of(apart), :], msend.at[k], mrecv.at[k], (base + l, u))
        )
    for copy in more:
        copy.start()
    leader = ((lax.axis_index("ctx") == 0) & (side == 0)).astype(jnp.int32)
    mup_ref[...] = jnp.zeros_like(mup_ref)
    mup_ref[0 : mcot_ref.shape[0], :] = mcot_ref[...]
    model = tokens_ref.shape[1]
    rows = half + MEMQ
    mine = pl.ds(pl.multiple_of(side * half, half), half)
    hidden = wu_a.shape[1]
    chunk = 512
    place = lax.broadcasted_iota(jnp.int32, (rows, 1), 0)
    weight = jnp.where((place < half) | (leader == 1), 1.0, 0.0).astype(F32)
    b_output, first_gain, first_bias, b_down, second_gain, second_bias = (
        ref[...].astype(F32).reshape(1, model)
        for ref in (bo_ref, fg_ref, fb_ref, bd_ref, sg_ref, sb_ref)
    )
    for copy in copies + more:
        copy.wait()

    mixed_t = jnp.concatenate([mixed_ref[...], memt_ref[...]], axis=1)
    mixed = mixed_t.T
    heads = wo_a.shape[0]
    attended = dot(mixed[:, 0:heads], wo_a[...]) + dot(mixed[:, heads : 2 * heads], wo_b[...])
    own_rows = jnp.concatenate([tokens_ref[mine, :], mem_ref[...]], axis=0).astype(F32)
    first_hat, first_scale = norm_parts(own_rows + attended + b_output)
    normed = first_hat * first_gain + first_bias
    low = normed.astype(BF16)
    low_ref[...] = low
    lowt_ref[...] = (low.astype(F32) * weight).astype(BF16).T
    hidden_ref[...] = normed + b_down
    root = 0.7978845608028654
    count = hidden // chunk
    parts_of = [
        (
            slice(k * chunk, (k + 1) * chunk),
            slice((part * count + k) * chunk, (part * count + k + 1) * chunk),
            part,
        )
        for part in range(2)
        for k in range(count)
    ]
    ups, downs, up_biases, grads = (wu_a, wu_b), (wd_a, wd_b), (bu_a, bu_b), (gown_ref, gpeer_ref)

    def widen(k):
        at, to, part = parts_of[k]
        inner_refs[k % 2][...] = dot(low_ref[...], ups[part][:, at])

    widen(0)
    for k, (at, to, part) in enumerate(parts_of):
        if k + 1 < len(parts_of):
            widen(k + 1)
        inner = inner_refs[k % 2][...] + up_biases[part][at].astype(F32).reshape(1, chunk)
        square = inner * inner
        bent = jnp.tanh(inner * (root + (root * 0.044715) * square))
        grown = 0.5 + 0.5 * bent
        acted_ref[:, to] = (inner * grown).astype(BF16)
        slope_ref[:, to] = grown + inner * (1.0 - bent * bent) * (
            0.5 * root + (0.5 * root * 0.134145) * square
        )
        hidden_ref[...] += dot(acted_ref[:, to], downs[part][at, :])
    second_hat, second_scale = norm_parts(hidden_ref[...])
    final = second_hat * second_gain + second_bias
    final_ref[...] = final[0:half].astype(BF16)
    mfinal_ref[...] = final[half:rows].astype(BF16)
    upstream = jnp.concatenate([cot_ref[mine, :], mup_ref[...]], axis=0).astype(F32)
    weighted = upstream * weight
    second_gain_grad = jnp.sum(second_hat * weighted, axis=0, keepdims=True)
    second_bias_grad = jnp.sum(weighted, axis=0, keepdims=True)
    second_back = norm_back(upstream * second_gain, second_hat, second_scale)
    fed = second_back.astype(BF16)
    fed_wide = fed.astype(F32) * weight
    down_bias_grad = jnp.sum(fed_wide, axis=0, keepdims=True)
    fed_ref[...] = fed
    hidden_ref[...] = second_back

    def narrow(k):
        at, to, part = parts_of[k]
        inner_refs[k % 2][...] = dot_nt(fed_ref[...], downs[part][at, :])

    bias_ref[...] = jnp.zeros_like(bias_ref)
    narrow(0)
    for k, (at, to, part) in enumerate(parts_of):
        if k + 1 < len(parts_of):
            narrow(k + 1)
        back = (inner_refs[k % 2][...] * slope_ref[:, to]).astype(BF16)
        backs_ref[:, to] = back
        owner = lax.rem(side + part, sides)
        bias_ref[pl.ds(owner * count + k % count, 1), :] = jnp.sum(
            back.astype(F32) * weight, axis=0, keepdims=True
        )
        hidden_ref[...] += dot_nt(backs_ref[:, to], ups[part][:, at])
    normed_back = hidden_ref[...]
    weighted_back = normed_back * weight
    first_gain_grad = jnp.sum(first_hat * weighted_back, axis=0, keepdims=True)
    first_bias_grad = jnp.sum(weighted_back, axis=0, keepdims=True)
    first_back = norm_back(normed_back * first_gain, first_hat, first_scale)
    first_ref[...] = first_back
    attended_back = first_back.astype(BF16)
    attended_wide = attended_back.astype(F32) * weight
    output_bias_grad = jnp.sum(attended_wide, axis=0, keepdims=True)
    back_ref[0:heads, :] = dot_nt(wo_a[...], attended_back).astype(BF16)
    back_ref[heads : 2 * heads, :] = dot_nt(wo_b[...], attended_back).astype(BF16)

    leaving = []
    for k, (l, u, apart) in enumerate(found):
        head = pl.multiple_of((apart * group + l) * HEAD, HEAD)
        leaving.append(
            remote(
                back_ref.at[pl.ds(head, HEAD), pl.ds(0, half)],
                do_ref.at[:, columns],
                dsend.at[k],
                drecv.at[k],
                (base + l, u),
            )
        )
    for copy in leaving:
        copy.start()
    head = pl.multiple_of(me * HEAD, HEAD)
    stays = pltpu.make_async_copy(
        back_ref.at[pl.ds(head, HEAD), pl.ds(0, half)], do_ref.at[:, columns], own
    )
    stays.start()
    mdo_ref[...] = back_ref[pl.ds(head, HEAD), half:rows]

    for k, value in enumerate(
        (
            output_bias_grad, first_gain_grad, first_bias_grad, down_bias_grad,
            second_gain_grad, second_bias_grad,
        )
    ):
        bias_ref[sides * count + k : sides * count + k + 1, :] = value
    filled = 2 * hidden + heads
    if filled < gown_ref.shape[0]:
        gown_ref[filled:, :] = jnp.zeros((gown_ref.shape[0] - filled, model), BF16)
        gpeer_ref[filled:, :] = jnp.zeros((gown_ref.shape[0] - filled, model), BF16)
    attended_low = attended_wide.astype(BF16)
    fed_low = fed_wide.astype(BF16)
    core = lax.rem(me, 2)
    beside = (base + core_partner(me), side)
    chips, size = hown_ref.shape[0], hown_ref.shape[1]
    sums = {}
    for part, grad_ref in ((1, gpeer_ref), (0, gown_ref)):
        for at, to, owner in parts_of:
            if owner != part:
                continue
            grad_ref[at, :] = dot(lowt_ref[...], backs_ref[:, to]).astype(BF16)
            grad_ref[hidden + at.start : hidden + at.stop, :] = dot(
                acted_ref[:, to].T, fed_low
            ).astype(BF16)
        grad_ref[2 * hidden : 2 * hidden + heads, :] = dot(
            mixed_t[part * heads : (part + 1) * heads, :], attended_low
        ).astype(BF16)
        sums[part] = []
        for p in range(chips):
            at = pl.ds(pl.multiple_of((2 * p + 1 - core) * size, size), size)
            slot = part * chips + p
            sums[part].append(
                remote(grad_ref.at[at, :], buffers.at[slot], csend.at[slot], crecv.at[slot], beside)
            )
            sums[part][-1].start()
    for part, grad_ref, total_ref in ((1, gpeer_ref, hpeer_ref), (0, gown_ref, hown_ref)):
        for p in range(chips):
            sums[part][p].wait()
            at = pl.ds(pl.multiple_of((2 * p + core) * size, size), size)
            total_ref[p] = (
                grad_ref[at, :].astype(F32) + buffers[part * chips + p].astype(F32)
            ).astype(BF16)
    stays.wait()
    for copy in leaving:
        copy.wait()


def middle(o, mstate, tokens, mem, cot, mcot, weights, vectors, bu_a, bu_b, group, sides, groups, half, grad_rows):
    model = tokens.shape[1]
    rows = half + MEMQ
    heads, hidden = weights[0].shape[0], weights[2].shape[1]
    near = group * sides - 1
    chips = groups * group // 2
    size = grad_rows // (2 * chips)
    dma = pltpu.SemaphoreType.DMA
    return pl.pallas_call(
        functools.partial(middle_kernel, group, sides, groups, half),
        out_shape=(
            jax.ShapeDtypeStruct((half, model), BF16),
            jax.ShapeDtypeStruct((MEMQ, model), BF16),
            jax.ShapeDtypeStruct((rows, model), F32),
            jax.ShapeDtypeStruct((HEAD, group * sides * half), BF16),
            jax.ShapeDtypeStruct((HEAD, MEMQ), BF16),
            jax.ShapeDtypeStruct((chips, size, model), BF16),
            jax.ShapeDtypeStruct((chips, size, model), BF16),
            jax.ShapeDtypeStruct((HEAD + 8, MEMQ), F32),
            jax.ShapeDtypeStruct((16, model), F32),
        ),
        in_specs=[vmem()] * 20,
        out_specs=(vmem(),) * 3 + (anyspace(),) + (vmem(),) * 5,
        scratch_shapes=[
            pltpu.VMEM((2 * heads, half), BF16),
            pltpu.VMEM((2 * heads, MEMQ), BF16),
            pltpu.VMEM((groups, SROWS, MEMQ), F32),
            pltpu.VMEM((HEAD, MEMQ), BF16),
            pltpu.VMEM((2 * heads, rows), BF16),
            pltpu.VMEM((grad_rows, model), BF16),
            pltpu.VMEM((grad_rows, model), BF16),
            pltpu.VMEM((2 * chips, size, model), BF16),
            pltpu.VMEM((rows, 2 * hidden), BF16),
            pltpu.VMEM((rows, 2 * hidden), F32),
            pltpu.VMEM((rows, 2 * hidden), BF16),
            pltpu.VMEM((rows, model), F32),
            pltpu.VMEM((rows, model), BF16),
            pltpu.VMEM((model, rows), BF16),
            pltpu.VMEM((rows, model), BF16),
            pltpu.VMEM((MEMQ, model), BF16),
            pltpu.VMEM((rows, model), F32),
            pltpu.VMEM((rows, model), F32),
            dma,
            dma((groups - 1,)), dma((groups - 1,)),
            dma((near,)), dma((near,)), dma((near,)), dma((near,)), dma((near,)), dma((near,)),
            dma((2 * chips,)), dma((2 * chips,)),
        ],
        compiler_params=pltpu.CompilerParams(
            collective_id=2, has_side_effects=True, vmem_limit_bytes=VMEM_LIMIT
        ),
        cost_estimate=pl.CostEstimate(
            flops=12 * rows * model * 2 * hidden, bytes_accessed=16 << 20, transcendentals=rows * hidden
        ),
        name="middle",
    )(o, mstate, tokens, mem, cot, mcot, *weights, *vectors, bu_a, bu_b)


def result_kernel(
    group, memory_rows, part_ref, other_ref, packs_ref, first_ref, sum_ref, final_ref,
    far_ref, mfinal_ref,
    out_token_ref, out_memory_ref, token_ref, memory_ref, query_ref, qbias_ref, key_ref, value_ref,
    vbias_ref, out_ref, up_ref, down_ref, upb_ref, *rest,
):
    small_refs, shared = rest[:-1], rest[-1]
    model = part_ref.shape[1]
    hidden, width = down_ref.shape[0], out_ref.shape[0]
    token_ref[...] = part_ref[...] + other_ref[...].astype(F32)
    side = lax.axis_index("wt")
    half = final_ref.shape[0]
    out_token_ref[pl.ds(pl.multiple_of(side * half, half), half), :] = final_ref[...]
    out_token_ref[pl.ds(pl.multiple_of((1 - side) * half, half), half), :] = far_ref[...]
    out_memory_ref[...] = mfinal_ref[0:memory_rows, :]
    rows = slice(3 * HEAD, 3 * HEAD + SHARED)
    total = packs_ref[0, rows, :].astype(F32)
    for h in range(1, group):
        total = total + packs_ref[h, rows, :].astype(F32)
    shared[...] = total
    begin = first_ref.shape[0] - MEMQ
    memory = shared[0:MEMK, :] + first_ref[begin : begin + MEMK, :]
    memory_ref[...] = memory[0:memory_rows, :]
    for at, ref in ((0, query_ref), (HEAD, key_ref), (2 * HEAD, value_ref)):
        for h in range(0, group, 2):
            both = jnp.concatenate(
                [packs_ref[h, at : at + HEAD, :], packs_ref[h + 1, at : at + HEAD, :]], axis=0
            )
            ref[:, h * HEAD : (h + 2) * HEAD] = both.T.astype(F32)
    row = 3 * HEAD + SHARED
    for at, ref in ((0, qbias_ref), (2 * HEAD, vbias_ref)):
        ref[...] = jnp.concatenate(
            [packs_ref[h, row : row + 1, at : at + HEAD].astype(F32) for h in range(group)], axis=1
        )
    chunks = hidden // model
    for k in range(chunks):
        up_ref[:, k * model : (k + 1) * model] = sum_ref[k * model : (k + 1) * model, :].astype(F32)
        upb_ref[:, k * model : (k + 1) * model] = shared[pl.ds(MEMK + side * chunks + k, 1), :]
    down_ref[...] = sum_ref[hidden : 2 * hidden, :].astype(F32)
    out_ref[...] = sum_ref[2 * hidden : 2 * hidden + width, :].astype(F32)
    for k, ref in enumerate(small_refs):
        at = MEMK + 2 * chunks + k
        ref[...] = shared[at : at + 1, :].reshape(model)


def results(part, other, packs, first, total, final, far, mfinal, group, memory_rows, hidden):
    block, model = part.shape
    width = group * HEAD
    shape = lambda *dims: jax.ShapeDtypeStruct(dims, F32)
    return pl.pallas_call(
        functools.partial(result_kernel, group, memory_rows),
        out_shape=(
            jax.ShapeDtypeStruct((block, model), BF16),
            jax.ShapeDtypeStruct((memory_rows, model), BF16),
            shape(block, model), shape(memory_rows, model),
            shape(model, width), shape(1, width), shape(model, width), shape(model, width),
            shape(1, width), shape(width, model), shape(model, hidden), shape(hidden, model),
            shape(1, hidden),
        )
        + (shape(model),) * 6,
        in_specs=[vmem()] * 8,
        out_specs=(vmem(),) * 19,
        scratch_shapes=[pltpu.VMEM((SHARED, model), F32)],
        compiler_params=pltpu.CompilerParams(vmem_limit_bytes=VMEM_LIMIT),
        name="results",
    )(part, other, packs, first, total, final, far, mfinal)


def local(
    tokens, memory, doc_starts, w_query, b_query, w_key, w_value, b_value, w_output, b_output,
    first_gain, first_bias, w_up, b_up, w_down, b_down, second_gain, second_bias,
    cotangent, mem_cotangent,
):
    block, model = tokens.shape
    memory_rows = memory.shape[0]
    docs = doc_starts.shape[0]
    width = w_query.shape[1]
    hidden = w_up.shape[1]
    group = width // HEAD
    ctx, sides = lax.axis_size("ctx"), lax.axis_size("wt")
    groups = ctx // group
    half = block // sides
    step = 16 * ctx
    grad_rows = (2 * hidden + width + step - 1) // step * step
    row = lambda a: a.reshape(1, a.shape[0])

    q, kv, out_b, up_b, bias_b, mq, mkv, mem_pad, w_pair, wq_t = scatter_heads(
        tokens, memory, w_query, b_query, w_key, w_value, b_value,
        w_output, w_up, b_up.reshape(8, hidden // 8), group,
    )
    forwards = [(i, i + group) for i in range(ctx - group)]
    backwards = [(i + group, i) for i in range(ctx - group)]
    swapped = [(i, (i + 1) % sides) for i in range(sides)]
    before = lax.ppermute(kv, "ctx", forwards)
    after = lax.ppermute(kv, "ctx", backwards)
    down_b = lax.ppermute(w_down, "wt", swapped)
    crossed = [(i, i ^ 2) for i in range(ctx)]
    neighbours = [(i, i ^ 1) for i in range(ctx)]
    late_tokens, kv = lax.optimization_barrier((tokens, kv))
    facing_tokens = lax.ppermute(late_tokens, "ctx", crossed)
    beside_tokens = lax.ppermute(late_tokens, "ctx", neighbours)

    state, mstate = forward_own(doc_starts, q, kv, mq, mkv, docs, memory_rows)
    state, facing_tokens, beside_tokens, down_b, before, after = lax.optimization_barrier(
        (state, facing_tokens, beside_tokens, down_b, before, after)
    )
    corner_tokens = lax.ppermute(facing_tokens, "ctx", neighbours)
    o, wide = forward_halo(doc_starts, q, before, after, state, docs)
    o, corner_tokens = lax.optimization_barrier((o, corner_tokens))
    final, mfinal, first_back, do, mdo, total_own, total_peer, mwide, biases = middle(
        o, mstate, tokens, mem_pad, cotangent, mem_cotangent,
        (w_output, out_b, w_up, up_b, w_down, down_b),
        [b_output, first_gain, first_bias, b_down, second_gain, second_bias],
        b_up, bias_b.reshape(hidden), group, sides, groups, half, grad_rows,
    )
    from_side = lax.ppermute(total_peer, "wt", swapped)

    part, dbefore, dafter = backward_halo(doc_starts, q, do, wide, before, after, docs)
    from_side, dbefore, dafter, final_late = lax.optimization_barrier(
        (from_side, dbefore, dafter, final)
    )
    size = grad_rows // ctx
    total = (total_own.astype(F32) + from_side.astype(F32)).reshape(groups, 2, size, model)
    row_half = lax.rem(lax.axis_index("ctx"), group) // 2
    leaving = lax.dynamic_index_in_dim(total, 1 - row_half, 1, False).astype(BF16)
    staying = lax.dynamic_index_in_dim(total, row_half, 1, False).astype(BF16)
    from_row = lax.ppermute(leaving, "ctx", crossed)
    from_after = lax.ppermute(dbefore, "ctx", backwards)
    from_before = lax.ppermute(dafter, "ctx", forwards)
    dq, dkv, dmq, dmkv, kt, delta, wide_dq = backward_first(
        doc_starts, q, do, wide, kv, part, mq, mdo, mwide, mkv, docs, memory_rows
    )
    from_row, from_after, from_before, dq, dkv = lax.optimization_barrier(
        (from_row, from_after, from_before, dq, dkv)
    )
    total = (staying.astype(F32) + from_row.astype(F32)).astype(BF16)
    columns = [[g * group + l for g in range(groups)] for l in range(group)]
    total = lax.all_to_all(total, "ctx", 0, 0, axis_index_groups=columns, tiled=True)
    far = lax.ppermute(lax.optimization_barrier((final_late, dq))[0], "wt", swapped)
    dq, dkv = backward_second(
        doc_starts, q, do, wide, kv, kt, delta, wide_dq, dq, dkv, docs
    )
    total, far, dq, dkv = lax.optimization_barrier((total, far, dq, dkv))
    piece = jnp.sum(total.astype(F32), axis=0).astype(BF16)
    part, other, packs, total = tail(
        dq, dkv, from_after, from_before,
        (tokens, beside_tokens, facing_tokens, corner_tokens), dmq, dmkv, mem_pad, first_back, wq_t, w_pair,
        biases, piece, group, groups, sides, block,
    )
    total = total.reshape(grad_rows, model)
    (
        token_out, memory_out, token_grad, memory_grad, query_grad, query_bias, key_grad, value_grad,
        value_bias, out_grad, up_grad, down_grad, up_bias, *small,
    ) = results(
        part, other, packs, first_back, total, final, far, mfinal, group, memory_rows, hidden
    )
    return (
        token_out, memory_out, token_grad, memory_grad,
        query_grad, query_bias.reshape(width), key_grad, value_grad, value_bias.reshape(width),
        out_grad, small[0], small[1], small[2],
        up_grad, up_bias.reshape(hidden), down_grad, small[3], small[4], small[5],
    )


def solution(mesh):
    placed = (
        P("ctx", None), P(), P(), P(None, "wt"), P("wt"), P(None, "wt"), P(None, "wt"), P("wt"),
        P("wt", None), P(), P(), P(), P(None, "wt"), P("wt"), P("wt", None), P(), P(), P(),
        P("ctx", None), P(),
    )
    return jax.shard_map(
        local,
        mesh=mesh,
        in_specs=placed,
        out_specs=(
            P("ctx", None), P(), P("ctx", None), P(), P(None, "wt"), P("wt"), P(None, "wt"),
            P(None, "wt"), P("wt"), P("wt", None), P(), P(), P(), P(None, "wt"), P("wt"),
            P("wt", None), P(), P(), P(),
        ),
        check_vma=False,
    )
```
